32 devices in a mesh: sweep: 4 (over x, core), bulk: 8 (over z, y).
Axes of the slice: x: 2, y: 2, z: 4, core: 2. Of those that a mesh axis runs over, the one named last changes fastest.
Arguments:
- source: float32 [128, 5, 128, 128], P('sweep', None, 'bulk'), may hold values from -6 to 6
- psi_old: float32 [128, 5, 128, 128], P('sweep', None, 'bulk'), may hold values from -6 to 6
- lateral: float32 [128, 2, 128, 128], P('sweep', None, 'bulk'), may hold values from 0.1 to 0.6
- lower_jac: float32 [128, 5, 5, 128, 128], P('sweep', None, None, 'bulk')
- upper_jac: float32 [128, 5, 5, 128, 128], P('sweep', None, None, 'bulk')
- diag_inv: float32 [128, 5, 5, 128, 128], P('sweep', None, None, 'bulk')
- face_weight: float32 [5, 65536], P(None, ('sweep', 'bulk')), may hold values from -6 to 6
- face_cell: int32 [65536], P(('sweep', 'bulk')), may hold values from 0 to 65535
- face_owner: int32 [65536, 1], P(('sweep', 'bulk')), may hold values from 0 to 7; in each aligned block of 2048 rows (0 to 2047, 2048 to 4095, ...) at most 512 rows name the same one
- face_node: int32 [65536], P(('sweep', 'bulk')), may hold values from 0 to 16383
- face_count: int32 [32], P(('sweep', 'bulk')), may hold values from 1 to 2048, as said below
Outputs:
- adjoint: float32 [128, 5, 128, 128], P('sweep', None, 'bulk')
- node_sens: float32 [131072], P('bulk')
The draws below stay inside these ranges and needn't reach their ends.
Inputs may be any that keep to these rules, and one draw needn't show every extreme that they name: `face_owner`: among the 2048 faces of one device no owner appears more than 512 times; some device reaches 512. `face_count`: some device has all 2048 slots live.
All inputs are finite; a program needn't handle non-finite values.
Results may differ from the reference program's by a relative error of at most 0.00011.
Values sent between devices are 32-bit elements; how exact they have to be, the bound alone decides.
No kernel may reach another device: no remote copies, remote signals or barrier semaphores. Data moves between devices by JAX's collectives and lax.ppermute only.
A program may use at most 128 MiB of HBM per device.

```python
import math
import jax
import jax.numpy as jnp
import numpy as np
from jax import lax

CI = 32
CJ = 16
CK = 128
FCAP = 2048
NODES_DEV = 16384
SWEEP_PLANES = 128
NJ = 128
FACES = 65536
NODES = 131072
CAP = 512
N_BULK = 8
DEVICES = 32


def diag_values(key):
    spread = jax.random.uniform(jax.random.fold_in(key, 11), (SWEEP_PLANES, 5, NJ, CK), jnp.float32, math.log(0.5), 0.0)
    return jnp.exp(spread)


def decay_rates(key, random_seed_offset):
    slow_share = 0.5
    delayed_worker = jax.random.uniform(jax.random.fold_in(key, random_seed_offset), (1, 5, NJ, CK), jnp.float32) < slow_share
    random_perturbation = jax.random.uniform(jax.random.fold_in(key, random_seed_offset + 1), (SWEEP_PLANES, 5, NJ, CK), jnp.float32, 0.99, 1.0)
    spike_factor = jax.random.uniform(jax.random.fold_in(key, random_seed_offset + 2), (SWEEP_PLANES, 1, 1, 1), jnp.float32) < 2.0 / SWEEP_PLANES
    delay_fraction = math.exp(-0.5 / SWEEP_PLANES)
    return jnp.where(delayed_worker, delay_fraction, 0.92) * random_perturbation * jnp.where(spike_factor, 0.7, 1.0)


def block_eye():
    return jnp.eye(5, dtype=jnp.float32)[None, :, :, None, None]


def draw_diag_inv(key, part):
    scale = diag_values(key)[:, :, None]
    offdiag = jax.random.uniform(jax.random.fold_in(key, 21), (SWEEP_PLANES, 5, 5, NJ, CK), jnp.float32, -0.12, 0.12) * scale
    unit = block_eye()
    return unit * scale + (1.0 - unit) * offdiag


def coupling(key, random_seed_offset):
    gains = (decay_rates(key, random_seed_offset) / diag_values(key))[:, :, None]
    offdiag = jax.random.uniform(jax.random.fold_in(key, random_seed_offset + 10), (SWEEP_PLANES, 5, 5, NJ, CK), jnp.float32, -0.12, 0.12) * gains
    unit = block_eye()
    return -(unit * gains + (1.0 - unit) * offdiag)


def draw_lower_jac(key, part):
    return coupling(key, 31)


def draw_upper_jac(key, part):
    return coupling(key, 51)


def draw_face_count(key, part):
    counts = jax.random.randint(jax.random.fold_in(key, 71), (DEVICES,), FCAP // 3, FCAP + 1)
    place = jax.random.randint(jax.random.fold_in(key, 72), (), 0, DEVICES)
    return counts.at[place].set(FCAP)


def plant(entries, stream_key, smallest, largest):
    dims = entries.shape
    spot = [jax.random.randint(jax.random.fold_in(stream_key, axis), (), 0, dims[axis]) for axis in range(len(dims))]
    entries = entries.at[tuple(spot)].set(smallest)
    longest = dims.index(max(dims))
    spot[longest] = (spot[longest] + 1) % dims[longest]
    return entries.at[tuple(spot)].set(largest)


def level_of(stream_key, shape, pieces, least, high):
    level, own = 1.0, jax.random.fold_in(stream_key, 6)
    for axis_at, shards_of in pieces:
        draws = jnp.exp(jax.random.uniform(jax.random.fold_in(own, axis_at), (shards_of,), jnp.float32, least / len(pieces), high / len(pieces)))
        level = level * jnp.repeat(draws, shape[axis_at] // shards_of).reshape([-1 if axis == axis_at else 1 for axis in range(len(shape))])
    return level


def deal_out(rng, own, number, rows, count, top, most, lean):
    ranking = jax.random.permutation(rng, count)
    packed, ordinary = portions_of(count, rows * top, most, lean, True), portions_of(count, rows * top, most, lean, False)
    places = jnp.arange(count)

    def named(tallies, turn):
        used = int((tallies > 0).sum())
        fixed = max(1, used // 4)
        shifted = fixed + (places - fixed + turn * (used - fixed)) % max(1, count - fixed)
        return jnp.zeros((count,), jnp.int32).at[ranking[jnp.where(places < fixed, places, shifted)]].set(jnp.asarray(tallies, jnp.int32))

    tallies = jnp.where(number % 4 == 0, named(packed, number // 4), named(ordinary, number - number // 4 - 1))
    mixed = jax.random.permutation(jax.random.fold_in(own, 3), count)
    donor, taker = mixed[0:count // 2 * 2:2], mixed[1:count // 2 * 2:2]
    margin = jnp.minimum(tallies[donor] - 1, most - tallies[taker]) // 2
    margin = jnp.where((donor == ranking[0]) | (taker == ranking[0]) | (tallies[taker] == 0), 0, jnp.maximum(margin, 0))
    shifted = jax.random.randint(jax.random.fold_in(own, 4), (count // 2,), 0, 1 << 20) % (margin + 1)
    tallies = tallies.at[donor].add(-shifted).at[taker].add(shifted)
    members = jnp.searchsorted(jnp.cumsum(tallies), jnp.arange(rows * top), side="right").astype(jnp.int32)
    table = members.reshape(top, rows).T
    table = table[jax.random.permutation(jax.random.fold_in(own, 1), rows)]
    turn = jax.random.randint(jax.random.fold_in(own, 2), (rows, 1), 0, top)
    return jnp.take_along_axis(table, (jnp.arange(top)[None, :] + turn) % top, axis=1)


def portions_of(number_of, total, bound, lean, full):
    weights = [(1 << 20) // math.isqrt(standing ** lean) + 1 for standing in range(1, number_of + 1)]
    largest = bound if full else min(bound, max(-(-total // number_of), total * weights[0] // sum(weights)))
    least = 1 if total - largest >= number_of - 1 else 0
    holding, rest = [largest] + [least] * (number_of - 1), total - largest - least * (number_of - 1)
    while rest > 0:
        candidates = [i for i in range(1, number_of) if holding[i] < largest] or [i for i in range(1, number_of) if holding[i] < bound]
        mass, left = sum([weights[i] for i in candidates]), rest
        for i in candidates:
            addition = min(bound - holding[i], max(1, left * weights[i] // mass), rest)
            holding[i] = holding[i] + addition
            rest = rest - addition
    return np.array(holding)


def normal_values(stream_key, dims, scale, most, pieces=(), held_as=jnp.bfloat16):
    array = jax.random.normal(stream_key, dims, jnp.float32) * scale
    if len(pieces) > 0:
        array = level_of(stream_key, dims, pieces, -0.22, 0.18) * array
    return jnp.clip(array, min=-most, max=most).astype(held_as)


def setup_inputs(seed: int = 0) -> dict:
    key_of = jax.random.split(jax.random.key(seed), 12)
    source = normal_values(key_of[0], (SWEEP_PLANES, 5, NJ, CK), 1.0, 6.0, ((0, 4), (2, 8)), jnp.float32)
    psi_old = normal_values(key_of[1], (SWEEP_PLANES, 5, NJ, CK), 1.0, 6.0, ((0, 4), (2, 8)), jnp.float32)
    lateral = jnp.clip(0.1 + 0.5 * jax.random.uniform(key_of[2], (SWEEP_PLANES, 2, NJ, CK), jnp.float32) ** level_of(key_of[2], (SWEEP_PLANES, 2, NJ, CK), ((0, 4), (2, 8)), -0.2, 0.2), 0.1, 0.6)
    lower_jac = draw_lower_jac(jax.random.fold_in(key_of[11], 71), 0)
    upper_jac = draw_upper_jac(jax.random.fold_in(key_of[11], 71), 0)
    diag_inv = draw_diag_inv(jax.random.fold_in(key_of[11], 71), 0)
    face_weight = normal_values(key_of[6], (5, FACES), 1.0, 6.0, ((1, 32),), jnp.float32)
    face_cell = plant(jax.random.randint(key_of[7], (FACES,), 0, CI * CJ * CK), jax.random.fold_in(key_of[7], 1), 0, (CI * CJ * CK) - 1).astype(jnp.int32)
    face_owner_keys = jax.random.split(jax.random.fold_in(key_of[8], 1), FACES // FCAP)
    face_owner_turns = jax.random.permutation(jax.random.fold_in(key_of[8], 3), FACES // FCAP)
    face_owner = jax.vmap(lambda own, number: deal_out(jax.random.fold_in(key_of[8], 2), own, number, FCAP, N_BULK, 1, CAP, 2))(face_owner_keys, face_owner_turns).reshape((FACES, 1))
    face_node = plant(jax.random.randint(key_of[9], (FACES,), 0, NODES_DEV), jax.random.fold_in(key_of[9], 1), 0, NODES_DEV - 1).astype(jnp.int32)
    face_count = draw_face_count(jax.random.fold_in(key_of[11], 71), 0)
    return dict(source=source, psi_old=psi_old, lateral=lateral, lower_jac=lower_jac, upper_jac=upper_jac, diag_inv=diag_inv, face_weight=face_weight, face_cell=face_cell, face_owner=face_owner, face_node=face_node, face_count=face_count)


def matvec(matrix, vector):
    return jnp.sum(matrix * vector[None], axis=1)


def forward_sweep(right_side, lower_jac, diag_inv, start):
    def advance(current, planes):
        rhs_plane, lower_plane, inv_plane = planes
        updated = matvec(inv_plane, rhs_plane - matvec(lower_plane, current))
        return updated, updated
    leaving, fields = lax.scan(advance, start, (right_side, lower_jac, diag_inv))
    return fields


def backward_sweep(forward_field, upper_jac, diag_inv, start):
    def advance(current, planes):
        fwd_plane, upper_plane, inv_plane = planes
        updated = fwd_plane - matvec(inv_plane, matvec(upper_plane, current))
        return updated, updated
    leaving, fields = lax.scan(advance, start, (forward_field, upper_jac, diag_inv), reverse=True)
    return fields


def reference(source, psi_old, lateral, lower_jac, upper_jac, diag_inv, face_weight, face_cell, face_owner, face_node, face_count):
    padded = jnp.pad(psi_old, ((0, 0), (0, 0), (1, 1), (0, 0)))
    right_side = source - lateral[:, 0:1] * padded[:, :, :-2] - lateral[:, 1:2] * padded[:, :, 2:]
    zero_state = jnp.zeros((5, NJ, CK), jnp.float32)
    forward_field = forward_sweep(right_side, lower_jac, diag_inv, zero_state)
    adjoint = backward_sweep(forward_field, upper_jac, diag_inv, zero_state)
    face_index = jnp.arange(FACES, dtype=jnp.int32)
    device = face_index // FCAP
    sweep_pos = device // N_BULK
    bulk_pos = device % N_BULK
    plane_index = face_cell // (CJ * CK)
    rest_index = face_cell % (CJ * CK)
    column_index = rest_index // CK
    depth_index = rest_index % CK
    at_faces = adjoint[sweep_pos * CI + plane_index, :, bulk_pos * CJ + column_index, depth_index]
    partial_value = jnp.sum(at_faces * face_weight.T, axis=1)
    active = (face_index % FCAP) < face_count[device]
    partial_value = jnp.where(active, partial_value, jnp.float32(0.0))
    mesh_node_index = face_owner[:, 0] * NODES_DEV + face_node
    node_sens = jax.ops.segment_sum(partial_value, mesh_node_index, num_segments=NODES)
    return adjoint, node_sens
```

```python
import jax
import jax.numpy as jnp
from jax import lax
from jax.experimental import pallas as pl
from jax.experimental.pallas import tpu as pltpu
from jax.sharding import PartitionSpec as P

NODES_DEV = 16384
LANES = 128
F32 = jnp.float32
BF16 = jnp.bfloat16
VMEM = pltpu.VMEM


def dot5(a, b):
    p = [x * y for x, y in zip(a, b)]
    return ((p[0] + p[1]) + (p[2] + p[3])) + p[4]


def block(ref, at, rows):
    return [[ref[at, c, d, rows, :] for d in range(5)] for c in range(5)]


def halves(width):
    return [pl.ds(8 * h, 8) for h in range(width // 8)]


def in_vmem(value):
    return pltpu.with_memory_space_constraint(value, VMEM)


def in_hbm(value):
    return pltpu.with_memory_space_constraint(value, pltpu.HBM)


def vmem_specs(n):
    return [pl.BlockSpec(memory_space=VMEM)] * n


def ratio_and_total(coupled, inv, ratio_ref, total_ref, at, width):
    for rows in halves(width):
        j = block(coupled, at, rows)
        ratio = []
        for c in range(5):
            d = [inv[at, c, e, rows, :] for e in range(5)]
            ratio.append([dot5(d, [j[e][x] for e in range(5)]) for x in range(5)])
        old = [[total_ref[e, x, rows, :] for x in range(5)] for e in range(5)]
        new = [[dot5(ratio[c], [old[e][x] for e in range(5)]) for x in range(5)] for c in range(5)]
        for c in range(5):
            for x in range(5):
                ratio_ref[at, c, x, rows, :] = ratio[c][x]
                total_ref[c, x, rows, :] = new[c][x]


def set_identity(total_ref, planes):
    sign = 1.0 if planes % 2 == 0 else -1.0
    for c in range(5):
        for d in range(5):
            total_ref[c, d] = jnp.full(total_ref.shape[2:], sign if c == d else 0.0, F32)


def forward_matrices(coupled, inv):
    planes, width = coupled.shape[0], coupled.shape[3]

    def kernel(coupled_hbm, inv_hbm, ratio_ref, inv_ref, total_ref, buf, sems):
        def copies(i):
            return (
                pltpu.make_async_copy(inv_hbm.at[i], inv_ref.at[i], sems.at[0, i]),
                pltpu.make_async_copy(coupled_hbm.at[i], buf.at[i], sems.at[1, i]),
            )

        for i in range(planes):
            for copy in copies(i):
                copy.start()
        set_identity(total_ref, planes)

        def body(i, carry):
            for copy in copies(i):
                copy.wait()
            ratio_and_total(buf, inv_ref, ratio_ref, total_ref, i, width)
            return carry

        lax.fori_loop(0, planes, body, 0)

    return pl.pallas_call(
        kernel,
        out_shape=(
            VMEM(coupled.shape, F32),
            VMEM(inv.shape, F32),
            jax.ShapeDtypeStruct(coupled.shape[1:], F32),
        ),
        in_specs=[pl.BlockSpec(memory_space=pltpu.HBM)] * 2,
        out_specs=tuple(vmem_specs(3)),
        scratch_shapes=[VMEM(coupled.shape, F32), pltpu.SemaphoreType.DMA((2, planes))],
        compiler_params=pltpu.CompilerParams(vmem_limit_bytes=10 << 20),
        name="forward_matrices",
    )(in_hbm(coupled), in_hbm(inv))


def backward_matrices(coupled, inv):
    planes, width = coupled.shape[0], coupled.shape[3]

    def kernel(coupled_ref, inv_ref, ratio_ref, total_ref):
        set_identity(total_ref, planes)

        def body(t, carry):
            ratio_and_total(coupled_ref, inv_ref, ratio_ref, total_ref, planes - 1 - t, width)
            return carry

        lax.fori_loop(0, planes, body, 0)

    return pl.pallas_call(
        kernel,
        out_shape=(VMEM(coupled.shape, F32), jax.ShapeDtypeStruct(coupled.shape[1:], F32)),
        in_specs=vmem_specs(2),
        out_specs=tuple(vmem_specs(2)),
        compiler_params=pltpu.CompilerParams(vmem_limit_bytes=4 << 20),
        cost_estimate=pl.CostEstimate(flops=4_000_000, bytes_accessed=20_000_000, transcendentals=0),
        name="backward_matrices",
    )(in_vmem(coupled), in_vmem(inv))


def local_forward(odd, source, psi, lateral, first, second, ratio, inv):
    planes, width = source.shape[0], source.shape[2]

    def kernel(odd_ref, source_ref, psi_ref, lateral_ref, first_ref, second_ref, ratio_ref, inv_ref,
               scaled_ref, leaving_ref):
        is_odd = odd_ref[0] == 1

        def body(i, state):
            one, two = first_ref[i], second_ref[i]
            low = jnp.where(is_odd, one, two)
            high = jnp.where(is_odd, two, one)
            below, above = lateral_ref[i, 0], lateral_ref[i, 1]
            right = []
            for c in range(5):
                here = psi_ref[i, c]
                down = jnp.concatenate([low[c:c + 1], here[:width - 1]], axis=0)
                up = jnp.concatenate([here[1:], high[c:c + 1]], axis=0)
                right.append(source_ref[i, c] - below * down - above * up)
            out = []
            for h, rows in enumerate(halves(width)):
                r = [v[8 * h:8 * h + 8] for v in right]
                d = block(inv_ref, i, rows)
                e = block(ratio_ref, i, rows)
                g = [dot5(d[c], r) for c in range(5)]
                f = [g[c] - dot5(e[c], state[h]) for c in range(5)]
                out.append((g, f))
            for h, rows in enumerate(halves(width)):
                for c in range(5):
                    scaled_ref[i, c, rows, :] = out[h][0][c]
            return [f for _, f in out]

        zero = [[jnp.zeros((8, LANES), F32)] * 5 for _ in halves(width)]
        state = lax.fori_loop(0, planes, body, zero)
        for h, rows in enumerate(halves(width)):
            for c in range(5):
                leaving_ref[c, rows, :] = state[h][c]

    return pl.pallas_call(
        kernel,
        out_shape=(VMEM(source.shape, F32), jax.ShapeDtypeStruct(source.shape[1:], F32)),
        in_specs=[pl.BlockSpec(memory_space=pltpu.SMEM)] + vmem_specs(7),
        out_specs=tuple(vmem_specs(2)),
        compiler_params=pltpu.CompilerParams(vmem_limit_bytes=4 << 20),
        name="local_forward",
    )(odd, in_vmem(source), in_vmem(psi), in_vmem(lateral), in_vmem(first), in_vmem(second),
      in_vmem(ratio), in_vmem(inv))


def forward_then_back(scaled, entering, ratio, back_ratio):
    planes, width = scaled.shape[0], scaled.shape[2]

    def kernel(scaled_ref, entering_ref, ratio_ref, back_ref, field_ref, leaving_ref):
        def ahead(i, state):
            out = []
            for h, rows in enumerate(halves(width)):
                e = block(ratio_ref, i, rows)
                out.append([scaled_ref[i, c, rows, :] - dot5(e[c], state[h]) for c in range(5)])
            for h, rows in enumerate(halves(width)):
                for c in range(5):
                    field_ref[i, c, rows, :] = out[h][c]
            return out

        start = [[entering_ref[c, rows, :] for c in range(5)] for rows in halves(width)]
        lax.fori_loop(0, planes, ahead, start)

        def back(t, state):
            i = planes - 1 - t
            out = []
            for h, rows in enumerate(halves(width)):
                e = block(back_ref, i, rows)
                out.append([field_ref[i, c, rows, :] - dot5(e[c], state[h]) for c in range(5)])
            return out

        zero = [[jnp.zeros((8, LANES), F32)] * 5 for _ in halves(width)]
        state = lax.fori_loop(0, planes, back, zero)
        for h, rows in enumerate(halves(width)):
            for c in range(5):
                leaving_ref[c, rows, :] = state[h][c]

    return pl.pallas_call(
        kernel,
        out_shape=(VMEM(scaled.shape, F32), jax.ShapeDtypeStruct(scaled.shape[1:], F32)),
        in_specs=vmem_specs(4),
        out_specs=tuple(vmem_specs(2)),
        compiler_params=pltpu.CompilerParams(vmem_limit_bytes=4 << 20),
        name="forward_then_back",
    )(in_vmem(scaled), in_vmem(entering), in_vmem(ratio), in_vmem(back_ratio))


def face_tables(count, cell, owner, node, weight, rows_of_cells, owners):
    face_rows = cell.shape[0]
    slots = face_rows * LANES
    cap = 2 * slots // owners
    bucket_rows = 2 * face_rows

    def kernel(count_ref, cell_ref, owner_ref, node_ref, weight_ref,
               row_hot_ref, picked_ref, low_hot_ref, high_hot_ref, nodes_ref):
        lane = lax.broadcasted_iota(jnp.int32, (LANES, LANES), 1)
        sub = lax.broadcasted_iota(jnp.int32, (LANES, LANES), 0)
        strict = (sub < lane).astype(F32).astype(BF16)
        ones = jnp.ones((LANES, LANES), BF16)
        rank = jnp.zeros((face_rows, LANES), F32)
        own = owner_ref[...]
        for o in range(owners):
            mask = (own == o).astype(F32)
            before = jnp.dot(mask.astype(BF16), strict, preferred_element_type=F32)
            totals = jnp.dot(mask.astype(BF16), ones, preferred_element_type=F32)
            fs = lax.broadcasted_iota(jnp.int32, (face_rows, face_rows), 0)
            fl = lax.broadcasted_iota(jnp.int32, (face_rows, face_rows), 1)
            lower = (fl < fs).astype(F32).astype(BF16)
            offset = jnp.dot(lower, totals.astype(BF16), preferred_element_type=F32)
            rank = rank + mask * (before + offset + float(o * cap))
        slot = rank.astype(jnp.int32)
        slot_high, slot_low = slot // LANES, slot % LANES
        high_iota = lax.broadcasted_iota(jnp.int32, (bucket_rows, LANES), 0)
        nodes = jnp.zeros((bucket_rows, LANES), F32)
        cells = cell_ref[...]
        live = lax.broadcasted_iota(jnp.int32, (face_rows, LANES), 0) * LANES + lax.broadcasted_iota(
            jnp.int32, (face_rows, LANES), 1) < count_ref[0]
        nodes_all = node_ref[...]
        for f in range(face_rows):
            at = slice(f, f + 1)
            parts = [
                (cells[at] // LANES).astype(F32),
                (cells[at] % LANES).astype(F32),
                slot_low[at].astype(F32),
                (nodes_all[at] // LANES).astype(F32),
                (nodes_all[at] % LANES).astype(F32),
            ]
            for c in range(5):
                w = weight_ref[c:c + 1, f * LANES:(f + 1) * LANES]
                parts.append(jnp.where(live[at], w, 0.0))
            parts.append(jnp.zeros((LANES - len(parts), LANES), F32))
            columns = jnp.transpose(jnp.concatenate(parts, axis=0))

            def spread(k):
                return jnp.broadcast_to(columns[:, k:k + 1], (LANES, LANES))

            lane_f = lane.astype(F32)
            row = spread(0)
            here = pl.ds(f * LANES, LANES)
            for k in range(rows_of_cells // LANES):
                row_hot_ref[here, k * LANES:(k + 1) * LANES] = jnp.where(
                    row == lane_f + float(k * LANES), 1.0, 0.0).astype(BF16)
            picked = spread(1) == lane_f
            for c in range(5):
                picked_ref[here, c * LANES:(c + 1) * LANES] = jnp.where(picked, spread(5 + c), 0.0)
            low = jnp.where(spread(2) == lane_f, 1.0, 0.0)
            low_hot_ref[here, :] = low
            high = jnp.where(high_iota == slot_high[at], 1.0, 0.0).astype(BF16)
            high_hot_ref[:, f * LANES:(f + 1) * LANES] = high
            nodes = nodes + LANES * jnp.dot(high, (low * spread(3)).astype(BF16), preferred_element_type=F32)
            nodes = nodes + jnp.dot(high, (low * spread(4)).astype(BF16), preferred_element_type=F32)
        nodes_ref[...] = nodes

    return pl.pallas_call(
        kernel,
        out_shape=(
            VMEM((slots, rows_of_cells), BF16),
            VMEM((slots, 5 * LANES), F32),
            VMEM((slots, LANES), F32),
            VMEM((bucket_rows, slots), BF16),
            VMEM((bucket_rows, LANES), F32),
        ),
        in_specs=[pl.BlockSpec(memory_space=pltpu.SMEM)] + vmem_specs(4),
        out_specs=tuple(vmem_specs(5)),
        compiler_params=pltpu.CompilerParams(vmem_limit_bytes=8 << 20),
        cost_estimate=pl.CostEstimate(flops=4_000_000, bytes_accessed=20_000_000, transcendentals=0),
        name="face_tables",
    )(count, cell, owner, node, weight)


def split(value):
    high = value.astype(BF16)
    return high, (value - high.astype(F32)).astype(BF16)


def backward_and_faces(field, entering, back_ratio, tables, devices, owners):
    row_hot, picked, low_hot, high_hot, nodes = tables
    planes, width = field.shape[0], field.shape[2]
    cells = planes * width
    slots = row_hot.shape[0]
    bucket_rows = nodes.shape[0]
    rows_each = bucket_rows // owners
    chunk = 256

    def kernel(field_ref, entering_ref, back_ref, row_hot_ref, picked_ref, low_hot_ref, high_hot_ref,
               nodes_ref, adjoint_ref, send_ref, halves_ref):
        def back(t, state):
            i = planes - 1 - t
            out = []
            for h, rows in enumerate(halves(width)):
                e = block(back_ref, i, rows)
                out.append([field_ref[i, c, rows, :] - dot5(e[c], state[h]) for c in range(5)])
            for h, rows in enumerate(halves(width)):
                for c in range(5):
                    adjoint_ref[i, c, rows, :] = out[h][c]
            at = pl.multiple_of(i * width, width)
            for c in range(5):
                high, low = split(jnp.concatenate([o[c] for o in out], axis=0))
                halves_ref[pl.ds(at, width), c * LANES:(c + 1) * LANES] = high
                halves_ref[pl.ds(cells + at, width), c * LANES:(c + 1) * LANES] = low
            return out

        start = [[entering_ref[c, rows, :] for c in range(5)] for rows in halves(width)]
        lax.fori_loop(0, planes, back, start)
        ones = jnp.ones((LANES, LANES), BF16)
        values = jnp.zeros((bucket_rows, LANES), F32)
        for k in range(slots // chunk):
            here = slice(k * chunk, (k + 1) * chunk)
            hot = row_hot_ref[here, :]
            rows = jnp.dot(hot, halves_ref[:cells, :], preferred_element_type=F32)
            rows = rows + jnp.dot(hot, halves_ref[cells:, :], preferred_element_type=F32)
            scaled = rows * picked_ref[here, :]
            total = scaled[:, :LANES]
            for c in range(1, 5):
                total = total + scaled[:, c * LANES:(c + 1) * LANES]
            high, low = split(total)
            value = jnp.dot(high, ones, preferred_element_type=F32) + jnp.dot(
                low, ones, preferred_element_type=F32)
            high, low = split(value * low_hot_ref[here, :])
            place = high_hot_ref[:, here]
            values = values + (jnp.dot(place, high, preferred_element_type=F32)
                               + jnp.dot(place, low, preferred_element_type=F32))
        for d in range(devices):
            o = d % owners
            send_ref[d, :rows_each, :] = values[o * rows_each:(o + 1) * rows_each]
            send_ref[d, rows_each:, :] = nodes_ref[o * rows_each:(o + 1) * rows_each, :]

    return pl.pallas_call(
        kernel,
        out_shape=(
            jax.ShapeDtypeStruct(field.shape, F32),
            jax.ShapeDtypeStruct((devices, 2 * rows_each, LANES), F32),
        ),
        in_specs=vmem_specs(8),
        out_specs=tuple(vmem_specs(2)),
        scratch_shapes=[VMEM((2 * cells, 5 * LANES), BF16)],
        compiler_params=pltpu.CompilerParams(vmem_limit_bytes=16 << 20),
        name="backward_and_faces",
    )(in_vmem(field), in_vmem(entering), in_vmem(back_ratio), in_vmem(row_hot), in_vmem(picked),
      in_vmem(low_hot), in_vmem(high_hot), in_vmem(nodes))


def node_sums(got):
    devices, rows2, _ = got.shape
    rows_each = rows2 // 2
    side = NODES_DEV // LANES

    def kernel(got_ref, out_ref):
        sub = lax.broadcasted_iota(jnp.int32, (LANES, LANES), 0)
        side_iota = lax.broadcasted_iota(jnp.int32, (side, LANES), 0)

        def body(d, total):
            lefts, rights = [], []
            for r in range(rows_each):
                value = got_ref[d, r:r + 1, :]
                node = got_ref[d, rows_each + r:rows_each + r + 1, :].astype(jnp.int32)
                lefts.append(jnp.where(side_iota == node // LANES, 1.0, 0.0).astype(BF16))
                hot = sub == node % LANES
                high, low = split(value)
                rights.append(jnp.concatenate([
                    jnp.where(hot, high.astype(F32), 0.0).astype(BF16),
                    jnp.where(hot, low.astype(F32), 0.0).astype(BF16)], axis=0))
            left = jnp.concatenate(lefts, axis=1)
            right = jnp.concatenate(rights, axis=1)
            return total + lax.dot_general(left, right, (((1,), (1,)), ((), ())),
                                           preferred_element_type=F32)

        total = lax.fori_loop(0, devices, body, jnp.zeros((side, 2 * LANES), F32))
        out_ref[...] = total[:, :LANES] + total[:, LANES:]

    return pl.pallas_call(
        kernel,
        out_shape=jax.ShapeDtypeStruct((side, LANES), F32),
        in_specs=vmem_specs(1),
        out_specs=pl.BlockSpec(memory_space=VMEM),
        compiler_params=pltpu.CompilerParams(vmem_limit_bytes=8 << 20),
        name="node_sums",
    )(in_vmem(got))


def matvec(matrix, vector):
    return jnp.sum(matrix * vector[None], axis=1)


def matmat(matrix, other):
    return jnp.sum(matrix[:, :, None] * other[None], axis=1)


def relay(total, leaving, backward):
    size = lax.axis_size("sweep")
    index = lax.axis_index("sweep")
    stages = size.bit_length() - 1
    entering = jnp.zeros_like(leaving)
    reach = None
    for stage in range(stages):
        step = 1 << stage
        last = stage == stages - 1
        pairs = [(i, i ^ step) for i in range(size)]
        after = ((index // step) % 2) == (0 if backward else 1)
        other = lax.ppermute(leaving, "sweep", pairs)
        other_total = None if last else lax.ppermute(total, "sweep", pairs)
        gain = other if reach is None else matvec(reach, other)
        entering = jnp.where(after, entering + gain, entering)
        if not last:
            if reach is None:
                eye = jnp.eye(5, dtype=F32)[:, :, None, None]
                reach = jnp.where(after, other_total, jnp.broadcast_to(eye, total.shape))
            else:
                reach = jnp.where(after, matmat(reach, other_total), reach)
            near = jnp.where(after, total, other_total)
            far = jnp.where(after, other_total, total)
            leaving = jnp.where(after, leaving, other) + matvec(near, jnp.where(after, other, leaving))
            if stage + 1 < stages - 1:
                total = matmat(near, far)
    return entering


def per_device(source, psi_old, lateral, lower_jac, upper_jac, diag_inv, face_weight, face_cell,
               face_owner, face_node, face_count):
    bulk = lax.axis_size("bulk")
    devices = bulk * lax.axis_size("sweep")
    width = source.shape[2]
    odd = lax.axis_index("bulk") % 2
    low_pairs = [(i, i ^ 1) for i in range(bulk) if i ^ 1 < bulk]
    high_pairs = [(i, j) for i in range(bulk) for j in [i + 1 if i % 2 else i - 1] if 0 <= j < bulk]
    edge = lax.dynamic_index_in_dim(psi_old, jnp.where(odd == 1, 0, width - 1), 2, keepdims=False)
    first = lax.ppermute(edge, "bulk", low_pairs)
    edge = lax.dynamic_index_in_dim(psi_old, jnp.where(odd == 1, width - 1, 0), 2, keepdims=False)
    second = lax.ppermute(edge, "bulk", high_pairs)

    ratio, inv, total = forward_matrices(lower_jac, diag_inv)
    scaled, leaving = local_forward(odd.reshape(1), source, psi_old, lateral, first, second, ratio, inv)
    entering = relay(total, leaving, False)
    back_ratio, back_total = backward_matrices(upper_jac, inv)
    field, leaving = forward_then_back(scaled, entering, ratio, back_ratio)
    entering = relay(back_total, leaving, True)

    slots = face_cell.shape[0]
    rows = (slots // LANES, LANES)
    tables = face_tables(face_count, face_cell.reshape(rows), face_owner.reshape(rows),
                         face_node.reshape(rows), face_weight, source.shape[0] * width, bulk)
    adjoint, send = backward_and_faces(field, entering, back_ratio, tables, devices, bulk)
    got = lax.all_to_all(send, ("sweep", "bulk"), 0, 0, tiled=True)
    return adjoint, node_sums(got).reshape(NODES_DEV)


def solution(mesh):
    placed = (
        P("sweep", None, "bulk", None),
        P("sweep", None, "bulk", None),
        P("sweep", None, "bulk", None),
        P("sweep", None, None, "bulk", None),
        P("sweep", None, None, "bulk", None),
        P("sweep", None, None, "bulk", None),
        P(None, ("sweep", "bulk")),
        P(("sweep", "bulk")),
        P(("sweep", "bulk"), None),
        P(("sweep", "bulk")),
        P(("sweep", "bulk")),
    )
    return jax.shard_map(
        per_device,
        mesh=mesh,
        in_specs=placed,
        out_specs=(P("sweep", None, "bulk", None), P("bulk")),
        check_vma=False,
    )
```

```python
import jax
import jax.numpy as jnp
from jax import lax
from jax.experimental import pallas as pl
from jax.experimental.pallas import tpu as pltpu
from jax.sharding import PartitionSpec as P

NODES_DEV = 16384
LANES = 128
F32 = jnp.float32
BF16 = jnp.bfloat16
VMEM = pltpu.VMEM


def dot5(a, b):
    p = [x * y for x, y in zip(a, b)]
    return ((p[0] + p[1]) + (p[2] + p[3])) + p[4]


def block(ref, at, rows):
    return [[ref[at, c, d, rows, :] for d in range(5)] for c in range(5)]


def halves(width):
    return [pl.ds(8 * h, 8) for h in range(width // 8)]


def in_vmem(value):
    return pltpu.with_memory_space_constraint(value, VMEM)


def vmem_specs(n):
    return [pl.BlockSpec(memory_space=VMEM)] * n


def ratio_of(coupled, inv, at, rows):
    j = block(coupled, at, rows)
    d = block(inv, at, rows)
    return [[dot5(d[c], [j[e][x] for e in range(5)]) for x in range(5)] for c in range(5)], d


def next_total(ratio, total_ref, rows):
    old = [[total_ref[e, x, rows, :] for x in range(5)] for e in range(5)]
    return [[dot5(ratio[c], [old[e][x] for e in range(5)]) for x in range(5)] for c in range(5)]


def keep_matrices(ratio, total, ratio_ref, total_ref, at, rows):
    for c in range(5):
        for x in range(5):
            ratio_ref[at, c, x, rows, :] = ratio[c][x]
            total_ref[c, x, rows, :] = total[c][x]


def set_identity(total_ref, planes):
    sign = 1.0 if planes % 2 == 0 else -1.0
    for c in range(5):
        for d in range(5):
            total_ref[c, d] = jnp.full(total_ref.shape[2:], sign if c == d else 0.0, F32)


def edge_rows(psi):
    planes, fields, width, _ = psi.shape
    shape = (planes, fields, LANES)

    def kernel(psi_ref, low_ref, high_ref):
        is_odd = lax.rem(lax.axis_index("bulk"), 2) == 1
        for i in range(planes):
            head = psi_ref[i, :, 0, :]
            tail = psi_ref[i, :, width - 1, :]
            low_ref[i] = jnp.where(is_odd, head, tail)
            high_ref[i] = jnp.where(is_odd, tail, head)

    return pl.pallas_call(
        kernel,
        out_shape=(jax.ShapeDtypeStruct(shape, F32), jax.ShapeDtypeStruct(shape, F32)),
        in_specs=vmem_specs(1),
        out_specs=tuple(vmem_specs(2)),
        compiler_params=pltpu.CompilerParams(vmem_limit_bytes=4 << 20),
        cost_estimate=pl.CostEstimate(flops=4_000_000, bytes_accessed=60_000_000, transcendentals=0),
        name="edge_rows",
    )(in_vmem(psi))


def forward_local(source, psi, lateral, first, second, coupled, inv):
    planes, width = source.shape[0], source.shape[2]

    def kernel(source_ref, psi_ref, lateral_ref, first_ref, second_ref, coupled_ref, inv_ref,
               ratio_ref, total_ref, scaled_ref, leaving_ref):
        is_odd = lax.rem(lax.axis_index("bulk"), 2) == 1
        set_identity(total_ref, planes)

        def body(i, state):
            one, two = first_ref[i], second_ref[i]
            low = jnp.where(is_odd, one, two)
            high = jnp.where(is_odd, two, one)
            below, above = lateral_ref[i, 0], lateral_ref[i, 1]
            right = []
            for c in range(5):
                here = psi_ref[i, c]
                down = jnp.concatenate([low[c:c + 1], here[:width - 1]], axis=0)
                up = jnp.concatenate([here[1:], high[c:c + 1]], axis=0)
                right.append(source_ref[i, c] - below * down - above * up)
            out = []
            for h, rows in enumerate(halves(width)):
                r = [v[8 * h:8 * h + 8] for v in right]
                ratio, d = ratio_of(coupled_ref, inv_ref, i, rows)
                scaled = [dot5(d[c], r) for c in range(5)]
                out.append([scaled[c] - dot5(ratio[c], state[h]) for c in range(5)])
                total = next_total(ratio, total_ref, rows)
                keep_matrices(ratio, total, ratio_ref, total_ref, i, rows)
                for c in range(5):
                    scaled_ref[i, c, rows, :] = scaled[c]
            return out

        zero = [[jnp.zeros((8, LANES), F32)] * 5 for _ in halves(width)]
        state = lax.fori_loop(0, planes, body, zero)
        for h, rows in enumerate(halves(width)):
            for c in range(5):
                leaving_ref[c, rows, :] = state[h][c]

    return pl.pallas_call(
        kernel,
        out_shape=(
            VMEM(coupled.shape, F32),
            jax.ShapeDtypeStruct(coupled.shape[1:], F32),
            VMEM(source.shape, F32),
            jax.ShapeDtypeStruct(source.shape[1:], F32),
        ),
        in_specs=vmem_specs(7),
        out_specs=tuple(vmem_specs(4)),
        compiler_params=pltpu.CompilerParams(vmem_limit_bytes=4 << 20),
        name="forward_local",
    )(*[in_vmem(v) for v in (source, psi, lateral, first, second, coupled, inv)])


def backward_matrices(coupled, inv):
    planes, width = coupled.shape[0], coupled.shape[3]

    def kernel(coupled_ref, inv_ref, ratio_ref, total_ref):
        set_identity(total_ref, planes)

        def body(t, carry):
            at = planes - 1 - t
            for rows in halves(width):
                ratio, _ = ratio_of(coupled_ref, inv_ref, at, rows)
                keep_matrices(ratio, next_total(ratio, total_ref, rows), ratio_ref, total_ref, at, rows)
            return carry

        lax.fori_loop(0, planes, body, 0)

    return pl.pallas_call(
        kernel,
        out_shape=(VMEM(coupled.shape, F32), jax.ShapeDtypeStruct(coupled.shape[1:], F32)),
        in_specs=vmem_specs(2),
        out_specs=tuple(vmem_specs(2)),
        compiler_params=pltpu.CompilerParams(vmem_limit_bytes=4 << 20),
        cost_estimate=pl.CostEstimate(flops=4_000_000, bytes_accessed=20_000_000, transcendentals=0),
        name="backward_matrices",
    )(in_vmem(coupled), in_vmem(inv))


def forward_then_back(scaled, arriving, ratio, back_ratio):
    planes, width = scaled.shape[0], scaled.shape[2]

    def kernel(scaled_ref, near_ref, reach_ref, other_ref, ratio_ref, back_ref, field_ref, leaving_ref):
        def ahead(i, state):
            out = []
            for h, rows in enumerate(halves(width)):
                e = block(ratio_ref, i, rows)
                out.append([scaled_ref[i, c, rows, :] - dot5(e[c], state[h]) for c in range(5)])
            for h, rows in enumerate(halves(width)):
                for c in range(5):
                    field_ref[i, c, rows, :] = out[h][c]
            return out

        start = last_join(near_ref, reach_ref, other_ref, False, width)
        lax.fori_loop(0, planes, ahead, start)

        def back(t, state):
            i = planes - 1 - t
            out = []
            for h, rows in enumerate(halves(width)):
                e = block(back_ref, i, rows)
                out.append([field_ref[i, c, rows, :] - dot5(e[c], state[h]) for c in range(5)])
            return out

        zero = [[jnp.zeros((8, LANES), F32)] * 5 for _ in halves(width)]
        state = lax.fori_loop(0, planes, back, zero)
        for h, rows in enumerate(halves(width)):
            for c in range(5):
                leaving_ref[c, rows, :] = state[h][c]

    return pl.pallas_call(
        kernel,
        out_shape=(VMEM(scaled.shape, F32), jax.ShapeDtypeStruct(scaled.shape[1:], F32)),
        in_specs=vmem_specs(6),
        out_specs=tuple(vmem_specs(2)),
        compiler_params=pltpu.CompilerParams(vmem_limit_bytes=4 << 20),
        name="forward_then_back",
    )(in_vmem(scaled), *[in_vmem(v) for v in arriving], in_vmem(ratio), in_vmem(back_ratio))


def face_slots(owner, node, owners):
    face_rows = owner.shape[0]
    cap = 2 * face_rows * LANES // owners
    bucket_rows = 2 * face_rows

    def kernel(owner_ref, node_ref, slot_ref, nodes_ref):
        sub = lax.broadcasted_iota(jnp.int32, (LANES, LANES), 0)
        lane = lax.broadcasted_iota(jnp.int32, (LANES, LANES), 1)
        strict = (sub < lane).astype(F32).astype(BF16)
        ones = jnp.ones((LANES, LANES), BF16)
        fs = lax.broadcasted_iota(jnp.int32, (face_rows, face_rows), 0)
        fl = lax.broadcasted_iota(jnp.int32, (face_rows, face_rows), 1)
        lower = (fl < fs).astype(F32).astype(BF16)
        own = owner_ref[...]
        masks = [(own == o).astype(F32) for o in range(owners)]
        stacked = jnp.concatenate(masks, axis=0).astype(BF16)
        before = jnp.dot(stacked, strict, preferred_element_type=F32)
        totals = jnp.dot(stacked, ones, preferred_element_type=F32).astype(BF16)
        rank = jnp.zeros((face_rows, LANES), F32)
        for o in range(owners):
            here = slice(o * face_rows, (o + 1) * face_rows)
            offset = jnp.dot(lower, totals[here], preferred_element_type=F32)
            rank = rank + masks[o] * (before[here] + offset + float(o * cap))
        slot = rank.astype(jnp.int32)
        slot_ref[...] = slot
        nodes = node_ref[...]
        high = (nodes // LANES).astype(F32)
        low = (nodes % LANES).astype(F32)
        parts = place_in_slots(slot, [high, low], bucket_rows)
        nodes_ref[...] = float(LANES) * parts[0] + parts[1]

    return pl.pallas_call(
        kernel,
        out_shape=(VMEM((face_rows, LANES), jnp.int32), VMEM((bucket_rows, LANES), F32)),
        in_specs=vmem_specs(2),
        out_specs=tuple(vmem_specs(2)),
        compiler_params=pltpu.CompilerParams(vmem_limit_bytes=4 << 20),
        cost_estimate=pl.CostEstimate(flops=4_000_000, bytes_accessed=10_000_000, transcendentals=0),
        name="face_slots",
    )(in_vmem(owner), in_vmem(node))


def split(value):
    high = value.astype(BF16)
    return high, (value - high.astype(F32)).astype(BF16)


def place_in_slots(slot, parts, bucket_rows):
    face_rows = slot.shape[0]
    high = (slot // LANES).astype(F32).astype(BF16)
    low = (slot % LANES).astype(F32).astype(BF16)
    parts = [p.astype(BF16) for p in parts]
    high_iota = lax.broadcasted_iota(jnp.int32, (bucket_rows, LANES), 0).astype(F32).astype(BF16)
    low_iota = lax.broadcasted_iota(jnp.int32, (LANES, LANES), 0).astype(F32).astype(BF16)
    zero = jnp.zeros((bucket_rows, LANES), BF16)
    lefts, rights = [], []
    for f in range(face_rows):

        def spread(value, rows):
            return jnp.broadcast_to(value[f:f + 1], (rows, LANES))

        hot = high_iota == spread(high, bucket_rows)
        lefts.append(jnp.concatenate([jnp.where(hot, spread(p, bucket_rows), zero) for p in parts], axis=0))
        rights.append(jnp.where(low_iota == spread(low, LANES), jnp.ones((LANES, LANES), BF16),
                                jnp.zeros((LANES, LANES), BF16)))
    out = lax.dot_general(jnp.concatenate(lefts, axis=1), jnp.concatenate(rights, axis=1),
                          (((1,), (1,)), ((), ())), preferred_element_type=F32)
    return [out[k * bucket_rows:(k + 1) * bucket_rows] for k in range(len(parts))]


def backward_and_faces(field, arriving, back_ratio, count, cell, weight, slot, nodes, devices, owners):
    planes, width = field.shape[0], field.shape[2]
    face_rows = cell.shape[0]
    bucket_rows = nodes.shape[0]
    rows_each = bucket_rows // owners
    group = 2
    piece = 4
    batch = 8

    def kernel(count_ref, field_ref, near_ref, reach_ref, other_ref, back_ref, cell_ref, weight_ref,
               slot_ref, nodes_ref, adjoint_hbm, send_ref, adjoint_ref, parts_ref, value_ref, sems):
        def write(k):
            return pltpu.make_async_copy(adjoint_ref.at[pl.ds(k * batch, batch)],
                                         adjoint_hbm.at[pl.ds(k * batch, batch)], sems.at[k])

        def back(t, state):
            i = planes - 1 - t
            out = []
            for h, rows in enumerate(halves(width)):
                e = block(back_ref, i, rows)
                out.append([field_ref[i, c, rows, :] - dot5(e[c], state[h]) for c in range(5)])
            for h, rows in enumerate(halves(width)):
                for c in range(5):
                    adjoint_ref[i, c, rows, :] = out[h][c]
            for c in range(5):
                high, low = split(jnp.concatenate([o[c] for o in out], axis=0))
                at = pl.ds(pl.multiple_of((i * 5 + c) * width, width), width)
                parts_ref[at, :LANES] = high
                parts_ref[at, LANES:] = low
            return out

        state = last_join(near_ref, reach_ref, other_ref, True, width)
        for k in reversed(range(planes // batch)):
            first = planes - (k + 1) * batch
            state = lax.fori_loop(first, first + batch, back, state)
            write(k).start()

        lane_iota = lax.broadcasted_iota(jnp.int32, (LANES, LANES), 0).astype(F32).astype(BF16)
        sub8 = lax.broadcasted_iota(jnp.int32, (8, LANES), 0)

        def gather(g, carry):
            cells = [cell_ref[pl.ds(g * group + u, 1), :] for u in range(group)]
            hots, offs = [], []
            for at in cells:
                lanes = jnp.broadcast_to((at % LANES).astype(F32), (LANES, LANES)).astype(BF16)
                hots.append(jnp.where(lane_iota == lanes, jnp.ones((LANES, LANES), BF16),
                                      jnp.zeros((LANES, LANES), BF16)))
                offs.append(jnp.broadcast_to(at // LANES, (8, LANES)) - sub8)
            hot = jnp.concatenate(hots, axis=1)
            hot = jnp.concatenate([hot, hot], axis=0)
            found = [[jnp.zeros((8, LANES), F32)] * 5 for _ in range(group)]
            for p in range(0, planes, piece):
                got = jnp.dot(parts_ref[p * 5 * width:(p + piece) * 5 * width, :], hot,
                              preferred_element_type=F32)
                for i in range(piece):
                    for h in range(width // 8):
                        for u in range(group):
                            mask = offs[u] == (p + i) * width + 8 * h
                            for c in range(5):
                                row = (i * 5 + c) * width + 8 * h
                                found[u][c] = jnp.where(mask, got[row:row + 8, u * LANES:(u + 1) * LANES],
                                                        found[u][c])
            weights = weight_ref[:, pl.ds(pl.multiple_of(g * (group * LANES), group * LANES), group * LANES)]
            for u in range(group):
                w = [jnp.broadcast_to(weights[c:c + 1, u * LANES:(u + 1) * LANES], (8, LANES)) for c in range(5)]
                value_ref[pl.ds(g * group + u, 1), :] = jnp.sum(dot5(w, found[u]), axis=0, keepdims=True)
            return carry

        lax.fori_loop(0, face_rows // group, gather, 0)
        live = lax.broadcasted_iota(jnp.int32, (face_rows, LANES), 0) * LANES + lax.broadcasted_iota(
            jnp.int32, (face_rows, LANES), 1) < count_ref[0]
        high, low = split(jnp.where(live, value_ref[...], 0.0))
        placed = place_in_slots(slot_ref[...], [high, low], bucket_rows)
        values = placed[0] + placed[1]
        for o in range(owners):
            here = slice(o * rows_each, (o + 1) * rows_each)
            both = jnp.concatenate([values[here], nodes_ref[here, :]], axis=0)
            for d in range(o, devices, owners):
                send_ref[d] = both
        for k in range(planes // batch):
            write(k).wait()

    return pl.pallas_call(
        kernel,
        out_shape=(
            jax.ShapeDtypeStruct(field.shape, F32),
            jax.ShapeDtypeStruct((devices, 2 * rows_each, LANES), F32),
        ),
        in_specs=[pl.BlockSpec(memory_space=pltpu.SMEM)] + vmem_specs(9),
        out_specs=(pl.BlockSpec(memory_space=pltpu.HBM), pl.BlockSpec(memory_space=VMEM)),
        scratch_shapes=[
            VMEM(field.shape, F32),
            VMEM((planes * 5 * width, 2 * LANES), BF16),
            VMEM((face_rows, LANES), F32),
            pltpu.SemaphoreType.DMA((planes // batch,)),
        ],
        compiler_params=pltpu.CompilerParams(vmem_limit_bytes=12 << 20),
        name="backward_and_faces",
    )(count, in_vmem(field), *[in_vmem(v) for v in arriving], in_vmem(back_ratio), in_vmem(cell),
      in_vmem(weight), in_vmem(slot), in_vmem(nodes))


def node_sums(got):
    devices, rows2, _ = got.shape
    rows_each = rows2 // 2
    side = NODES_DEV // LANES
    batch = 32 // rows_each

    def kernel(got_ref, out_ref):
        iota = lax.broadcasted_iota(jnp.int32, (LANES, LANES), 0).astype(F32).astype(BF16)
        side_iota = lax.broadcasted_iota(jnp.int32, (side, LANES), 0).astype(F32).astype(BF16)
        ones, zero = jnp.ones((LANES, LANES), BF16), jnp.zeros((LANES, LANES), BF16)
        side_zero = jnp.zeros((side, LANES), BF16)

        def body(t, total):
            lefts, rights = [], []
            for u in range(batch):
                d = t * batch + u
                node = got_ref[d, rows_each:, :].astype(jnp.int32)
                node_high = (node // LANES).astype(F32).astype(BF16)
                node_low = (node % LANES).astype(F32).astype(BF16)
                high, low = split(got_ref[d, :rows_each, :])
                for r in range(rows_each):

                    def spread(value, rows):
                        return jnp.broadcast_to(value[r:r + 1], (rows, LANES))

                    hot = side_iota == spread(node_high, side)
                    lefts.append(jnp.concatenate([
                        jnp.where(hot, spread(high, side), side_zero),
                        jnp.where(hot, spread(low, side), side_zero)], axis=0))
                    rights.append(jnp.where(iota == spread(node_low, LANES), ones, zero))
            return total + lax.dot_general(
                jnp.concatenate(lefts, axis=1), jnp.concatenate(rights, axis=1),
                (((1,), (1,)), ((), ())), preferred_element_type=F32)

        total = lax.fori_loop(0, devices // batch, body, jnp.zeros((2 * side, LANES), F32))
        out_ref[...] = total[:side] + total[side:]

    return pl.pallas_call(
        kernel,
        out_shape=jax.ShapeDtypeStruct((side, LANES), F32),
        in_specs=vmem_specs(1),
        out_specs=pl.BlockSpec(memory_space=VMEM),
        compiler_params=pltpu.CompilerParams(vmem_limit_bytes=8 << 20),
        name="node_sums",
    )(in_vmem(got))


def comes_after(stage, backward):
    bit = lax.rem(lax.div(lax.axis_index("sweep"), 1 << stage), 2)
    return bit == (0 if backward else 1)


def matvec(matrix, vector):
    return [dot5(row, vector) for row in matrix]


def matmat(matrix, other):
    return [[dot5(row, [other[e][x] for e in range(5)]) for x in range(5)] for row in matrix]


def load_matrix(ref, rows):
    return [[ref[c, d, rows, :] for d in range(5)] for c in range(5)]


def load_vector(ref, rows):
    return [ref[c, rows, :] for c in range(5)]


def pick(flag, one, two):
    if isinstance(one, list):
        return [pick(flag, a, b) for a, b in zip(one, two)]
    return jnp.where(flag, one, two)


def last_join(near_ref, reach_ref, other_ref, backward, width):
    after = comes_after(lax.axis_size("sweep").bit_length() - 2, backward)
    start = []
    for rows in halves(width):
        near = load_vector(near_ref, rows)
        gain = matvec(load_matrix(reach_ref, rows), load_vector(other_ref, rows))
        start.append([n + jnp.where(after, g, 0.0) for n, g in zip(near, gain)])
    return start


def join(stage, backward, near, reach, leaving, total, other, other_total, carry_total):
    first = near is None
    width = leaving.shape[1]
    outs = [leaving.shape, total.shape, leaving.shape] + ([total.shape] if carry_total else [])

    def kernel(*refs):
        ins, out = refs[:len(operands)], refs[len(operands):]
        after = comes_after(stage, backward)
        for rows in halves(width):
            own, theirs = load_vector(ins[0], rows), load_vector(ins[2], rows)
            own_total, their_total = load_matrix(ins[1], rows), load_matrix(ins[3], rows)
            if first:
                entering = theirs
                through = their_total
                before = [jnp.zeros((8, LANES), F32)] * 5
                unit = [[jnp.full((8, LANES), 1.0 if c == d else 0.0, F32) for d in range(5)] for c in range(5)]
            else:
                before, unit = load_vector(ins[4], rows), load_matrix(ins[5], rows)
                entering = [a + b for a, b in zip(before, matvec(unit, theirs))]
                through = matmat(unit, their_total)
            entering, through = pick(after, entering, before), pick(after, through, unit)
            downstream = pick(after, own_total, their_total)
            sent = matvec(downstream, pick(after, theirs, own))
            sent = [a + b for a, b in zip(pick(after, own, theirs), sent)]
            for c in range(5):
                out[0][c, rows, :] = entering[c]
                out[2][c, rows, :] = sent[c]
                for d in range(5):
                    out[1][c, d, rows, :] = through[c][d]
            if carry_total:
                whole = matmat(downstream, pick(after, their_total, own_total))
                for c in range(5):
                    for d in range(5):
                        out[3][c, d, rows, :] = whole[c][d]

    operands = [leaving, total, other, other_total] + ([] if first else [near, reach])
    return pl.pallas_call(
        kernel,
        out_shape=tuple(jax.ShapeDtypeStruct(shape, F32) for shape in outs),
        in_specs=vmem_specs(len(operands)),
        out_specs=tuple(vmem_specs(len(outs))),
        compiler_params=pltpu.CompilerParams(vmem_limit_bytes=4 << 20),
        name="join",
    )(*[in_vmem(v) for v in operands])


def relay(total, leaving, backward):
    size = lax.axis_size("sweep")
    stages = size.bit_length() - 1
    near = reach = None
    for stage in range(stages):
        pairs = [(i, i ^ (1 << stage)) for i in range(size)]
        other = lax.ppermute(leaving, "sweep", pairs)
        if stage == stages - 1:
            return (near, reach, other), leaving
        other_total = lax.ppermute(total, "sweep", pairs)
        carry_total = stage + 2 < stages
        joined = join(stage, backward, near, reach, leaving, total, other, other_total, carry_total)
        near, reach, leaving = joined[:3]
        if carry_total:
            total = joined[3]


def per_device(source, psi_old, lateral, lower_jac, upper_jac, diag_inv, face_weight, face_cell,
               face_owner, face_node, face_count):
    bulk = lax.axis_size("bulk")
    devices = bulk * lax.axis_size("sweep")
    low_pairs = [(i, i ^ 1) for i in range(bulk) if i ^ 1 < bulk]
    high_pairs = [(i, j) for i in range(bulk) for j in [i + 1 if i % 2 else i - 1] if 0 <= j < bulk]
    low_edge, high_edge = edge_rows(psi_old)
    first = lax.ppermute(low_edge, "bulk", low_pairs)
    second = lax.ppermute(high_edge, "bulk", high_pairs)

    ratio, total, scaled, leaving = forward_local(source, psi_old, lateral, first, second, lower_jac, diag_inv)
    arriving, joined = relay(total, leaving, False)
    upper_jac, joined = lax.optimization_barrier((upper_jac, joined))
    back_ratio, back_total = backward_matrices(upper_jac, diag_inv)
    field, leaving = forward_then_back(scaled, arriving, ratio, back_ratio)
    back_total, leaving = lax.optimization_barrier((back_total, leaving))
    arriving, _ = relay(back_total, leaving, True)

    slots = face_cell.shape[0]
    rows = (slots // LANES, LANES)
    slot, nodes = face_slots(face_owner.reshape(rows), face_node.reshape(rows), bulk)
    adjoint, send = backward_and_faces(field, arriving, back_ratio, face_count, face_cell.reshape(rows),
                                       face_weight, slot, nodes, devices, bulk)
    got = lax.all_to_all(send, ("sweep", "bulk"), 0, 0, tiled=True)
    return adjoint, node_sums(got).reshape(NODES_DEV)


def solution(mesh):
    placed = (
        P("sweep", None, "bulk", None),
        P("sweep", None, "bulk", None),
        P("sweep", None, "bulk", None),
        P("sweep", None, None, "bulk", None),
        P("sweep", None, None, "bulk", None),
        P("sweep", None, None, "bulk", None),
        P(None, ("sweep", "bulk")),
        P(("sweep", "bulk")),
        P(("sweep", "bulk"), None),
        P(("sweep", "bulk")),
        P(("sweep", "bulk")),
    )
    return jax.shard_map(
        per_device,
        mesh=mesh,
        in_specs=placed,
        out_specs=(P("sweep", None, "bulk", None), P("bulk")),
        check_vma=False,
    )
```

```python
import jax
import jax.numpy as jnp
from jax import lax
from jax.experimental import pallas as pl
from jax.experimental.pallas import tpu as pltpu
from jax.sharding import PartitionSpec as P

NODES_DEV = 16384
LANES = 128
F32 = jnp.float32
BF16 = jnp.bfloat16
VMEM = pltpu.VMEM


def dot5(a, b):
    p = [x * y for x, y in zip(a, b)]
    return ((p[0] + p[1]) + (p[2] + p[3])) + p[4]


def block(ref, at, rows):
    return [[ref[at, c, d, rows, :] for d in range(5)] for c in range(5)]


def halves(width):
    return [pl.ds(8 * h, 8) for h in range(width // 8)]


def in_vmem(value):
    return pltpu.with_memory_space_constraint(value, VMEM)


def in_hbm(value):
    return pltpu.with_memory_space_constraint(value, pltpu.HBM)


def vmem_specs(n):
    return [pl.BlockSpec(memory_space=VMEM)] * n


def ratio_of(coupled, inv, at, rows):
    j = block(coupled, at, rows)
    d = block(inv, at, rows)
    return [[dot5(d[c], [j[e][x] for e in range(5)]) for x in range(5)] for c in range(5)], d


def next_total(ratio, total_ref, rows):
    old = [[total_ref[e, x, rows, :] for x in range(5)] for e in range(5)]
    return [[dot5(ratio[c], [old[e][x] for e in range(5)]) for x in range(5)] for c in range(5)]


def keep_matrices(ratio, total, ratio_ref, total_ref, at, rows):
    for c in range(5):
        for x in range(5):
            ratio_ref[at, c, x, rows, :] = ratio[c][x]
            total_ref[c, x, rows, :] = total[c][x]


def set_identity(total_ref, planes):
    sign = 1.0 if planes % 2 == 0 else -1.0
    for c in range(5):
        for d in range(5):
            total_ref[c, d] = jnp.full(total_ref.shape[2:], sign if c == d else 0.0, F32)


def edge_rows(psi):
    planes, fields, width, _ = psi.shape
    shape = (planes, fields, LANES)

    def kernel(psi_hbm, low_ref, high_ref, head_ref, tail_ref, sems):
        copies = [
            pltpu.make_async_copy(psi_hbm.at[:, :, 0, :], head_ref, sems.at[0]),
            pltpu.make_async_copy(psi_hbm.at[:, :, width - 1, :], tail_ref, sems.at[1]),
        ]
        for copy in copies:
            copy.start()
        is_odd = lax.rem(lax.axis_index("bulk"), 2) == 1
        for copy in copies:
            copy.wait()
        for i in range(planes):
            head, tail = head_ref[i], tail_ref[i]
            low_ref[i] = jnp.where(is_odd, head, tail)
            high_ref[i] = jnp.where(is_odd, tail, head)

    return pl.pallas_call(
        kernel,
        out_shape=(jax.ShapeDtypeStruct(shape, F32), jax.ShapeDtypeStruct(shape, F32)),
        in_specs=[pl.BlockSpec(memory_space=pltpu.HBM)],
        out_specs=tuple(vmem_specs(2)),
        scratch_shapes=[VMEM(shape, F32), VMEM(shape, F32), pltpu.SemaphoreType.DMA((2,))],
        compiler_params=pltpu.CompilerParams(vmem_limit_bytes=4 << 20),
        cost_estimate=pl.CostEstimate(flops=10_000_000_000, bytes_accessed=20_000_000, transcendentals=0),
        name="edge_rows",
    )(in_hbm(psi))


def forward_local(source, psi, lateral, first, second, coupled, inv):
    planes, width = source.shape[0], source.shape[2]

    def kernel(source_ref, psi_ref, lateral_ref, first_ref, second_ref, coupled_ref, inv_ref,
               ratio_ref, total_ref, scaled_ref, leaving_ref):
        is_odd = lax.rem(lax.axis_index("bulk"), 2) == 1
        set_identity(total_ref, planes)

        def body(i, state):
            one, two = first_ref[i], second_ref[i]
            low = jnp.where(is_odd, one, two)
            high = jnp.where(is_odd, two, one)
            below, above = lateral_ref[i, 0], lateral_ref[i, 1]
            right = []
            for c in range(5):
                here = psi_ref[i, c]
                down = jnp.concatenate([low[c:c + 1], here[:width - 1]], axis=0)
                up = jnp.concatenate([here[1:], high[c:c + 1]], axis=0)
                right.append(source_ref[i, c] - below * down - above * up)
            out = []
            for h, rows in enumerate(halves(width)):
                r = [v[8 * h:8 * h + 8] for v in right]
                ratio, d = ratio_of(coupled_ref, inv_ref, i, rows)
                scaled = [dot5(d[c], r) for c in range(5)]
                out.append([scaled[c] - dot5(ratio[c], state[h]) for c in range(5)])
                total = next_total(ratio, total_ref, rows)
                keep_matrices(ratio, total, ratio_ref, total_ref, i, rows)
                for c in range(5):
                    scaled_ref[i, c, rows, :] = scaled[c]
            return out

        zero = [[jnp.zeros((8, LANES), F32)] * 5 for _ in halves(width)]
        state = lax.fori_loop(0, planes, body, zero)
        for h, rows in enumerate(halves(width)):
            for c in range(5):
                leaving_ref[c, rows, :] = state[h][c]

    return pl.pallas_call(
        kernel,
        out_shape=(
            VMEM(coupled.shape, F32),
            jax.ShapeDtypeStruct(coupled.shape[1:], F32),
            VMEM(source.shape, F32),
            jax.ShapeDtypeStruct(source.shape[1:], F32),
        ),
        in_specs=vmem_specs(7),
        out_specs=tuple(vmem_specs(4)),
        compiler_params=pltpu.CompilerParams(vmem_limit_bytes=4 << 20),
        name="forward_local",
    )(*[in_vmem(v) for v in (source, psi, lateral, first, second, coupled, inv)])


def backward_matrices(coupled, inv):
    planes, width = coupled.shape[0], coupled.shape[3]

    def kernel(coupled_ref, inv_ref, ratio_ref, total_ref):
        set_identity(total_ref, planes)

        def body(t, carry):
            at = planes - 1 - t
            for rows in halves(width):
                ratio, _ = ratio_of(coupled_ref, inv_ref, at, rows)
                keep_matrices(ratio, next_total(ratio, total_ref, rows), ratio_ref, total_ref, at, rows)
            return carry

        lax.fori_loop(0, planes, body, 0)

    return pl.pallas_call(
        kernel,
        out_shape=(VMEM(coupled.shape, F32), jax.ShapeDtypeStruct(coupled.shape[1:], F32)),
        in_specs=vmem_specs(2),
        out_specs=tuple(vmem_specs(2)),
        compiler_params=pltpu.CompilerParams(vmem_limit_bytes=4 << 20),
        cost_estimate=pl.CostEstimate(flops=4_000_000, bytes_accessed=20_000_000, transcendentals=0),
        name="backward_matrices",
    )(in_vmem(coupled), in_vmem(inv))


def forward_then_back(scaled, arriving, ratio, back_ratio):
    planes, width = scaled.shape[0], scaled.shape[2]

    def kernel(scaled_ref, near_ref, reach_ref, other_ref, ratio_ref, back_ref, field_ref, leaving_ref):
        def ahead(i, state):
            out = []
            for h, rows in enumerate(halves(width)):
                e = block(ratio_ref, i, rows)
                out.append([scaled_ref[i, c, rows, :] - dot5(e[c], state[h]) for c in range(5)])
            for h, rows in enumerate(halves(width)):
                for c in range(5):
                    field_ref[i, c, rows, :] = out[h][c]
            return out

        start = last_join(near_ref, reach_ref, other_ref, False, width)
        lax.fori_loop(0, planes, ahead, start)

        def back(t, state):
            i = planes - 1 - t
            out = []
            for h, rows in enumerate(halves(width)):
                e = block(back_ref, i, rows)
                out.append([field_ref[i, c, rows, :] - dot5(e[c], state[h]) for c in range(5)])
            return out

        zero = [[jnp.zeros((8, LANES), F32)] * 5 for _ in halves(width)]
        state = lax.fori_loop(0, planes, back, zero)
        for h, rows in enumerate(halves(width)):
            for c in range(5):
                leaving_ref[c, rows, :] = state[h][c]

    return pl.pallas_call(
        kernel,
        out_shape=(VMEM(scaled.shape, F32), jax.ShapeDtypeStruct(scaled.shape[1:], F32)),
        in_specs=vmem_specs(6),
        out_specs=tuple(vmem_specs(2)),
        compiler_params=pltpu.CompilerParams(vmem_limit_bytes=4 << 20),
        name="forward_then_back",
    )(in_vmem(scaled), *[in_vmem(v) for v in arriving], in_vmem(ratio), in_vmem(back_ratio))


def face_slots(owner, node, owners):
    face_rows = owner.shape[0]
    cap = 2 * face_rows * LANES // owners
    bucket_rows = 2 * face_rows

    def kernel(owner_ref, node_ref, slot_ref, nodes_ref):
        sub = lax.broadcasted_iota(jnp.int32, (LANES, LANES), 0)
        lane = lax.broadcasted_iota(jnp.int32, (LANES, LANES), 1)
        strict = (sub < lane).astype(F32).astype(BF16)
        ones = jnp.ones((LANES, LANES), BF16)
        fs = lax.broadcasted_iota(jnp.int32, (face_rows, face_rows), 0)
        fl = lax.broadcasted_iota(jnp.int32, (face_rows, face_rows), 1)
        lower = (fl < fs).astype(F32).astype(BF16)
        own = owner_ref[...]
        masks = [(own == o).astype(F32) for o in range(owners)]
        stacked = jnp.concatenate(masks, axis=0).astype(BF16)
        before = jnp.dot(stacked, strict, preferred_element_type=F32)
        totals = jnp.dot(stacked, ones, preferred_element_type=F32).astype(BF16)
        rank = jnp.zeros((face_rows, LANES), F32)
        for o in range(owners):
            here = slice(o * face_rows, (o + 1) * face_rows)
            offset = jnp.dot(lower, totals[here], preferred_element_type=F32)
            rank = rank + masks[o] * (before[here] + offset + float(o * cap))
        slot = rank.astype(jnp.int32)
        slot_ref[...] = slot
        nodes = node_ref[...]
        high = (nodes // LANES).astype(F32)
        low = (nodes % LANES).astype(F32)
        parts = place_in_slots(slot, [high, low], bucket_rows)
        nodes_ref[...] = float(LANES) * parts[0] + parts[1]

    return pl.pallas_call(
        kernel,
        out_shape=(VMEM((face_rows, LANES), jnp.int32), VMEM((bucket_rows, LANES), F32)),
        in_specs=vmem_specs(2),
        out_specs=tuple(vmem_specs(2)),
        compiler_params=pltpu.CompilerParams(vmem_limit_bytes=4 << 20),
        cost_estimate=pl.CostEstimate(flops=4_000_000, bytes_accessed=10_000_000, transcendentals=0),
        name="face_slots",
    )(in_vmem(owner), in_vmem(node))


def split(value):
    high = value.astype(BF16)
    return high, (value - high.astype(F32)).astype(BF16)


def place_in_slots(slot, parts, bucket_rows):
    face_rows = slot.shape[0]
    high = (slot // LANES).astype(F32).astype(BF16)
    low = (slot % LANES).astype(F32).astype(BF16)
    parts = [p.astype(BF16) for p in parts]
    high_iota = lax.broadcasted_iota(jnp.int32, (bucket_rows, LANES), 0).astype(F32).astype(BF16)
    low_iota = lax.broadcasted_iota(jnp.int32, (LANES, LANES), 0).astype(F32).astype(BF16)
    zero = jnp.zeros((bucket_rows, LANES), BF16)
    lefts, rights = [], []
    for f in range(face_rows):

        def spread(value, rows):
            return jnp.broadcast_to(value[f:f + 1], (rows, LANES))

        hot = high_iota == spread(high, bucket_rows)
        lefts.append(jnp.concatenate([jnp.where(hot, spread(p, bucket_rows), zero) for p in parts], axis=0))
        rights.append(jnp.where(low_iota == spread(low, LANES), jnp.ones((LANES, LANES), BF16),
                                jnp.zeros((LANES, LANES), BF16)))
    out = lax.dot_general(jnp.concatenate(lefts, axis=1), jnp.concatenate(rights, axis=1),
                          (((1,), (1,)), ((), ())), preferred_element_type=F32)
    return [out[k * bucket_rows:(k + 1) * bucket_rows] for k in range(len(parts))]


def backward_and_faces(field, arriving, back_ratio, count, cell, weight, slot, nodes, devices, owners):
    planes, width = field.shape[0], field.shape[2]
    face_rows = cell.shape[0]
    bucket_rows = nodes.shape[0]
    rows_each = bucket_rows // owners
    group = 2
    piece = 4
    batch = 8

    def kernel(count_ref, field_ref, near_ref, reach_ref, other_ref, back_ref, cell_ref, weight_ref,
               slot_ref, nodes_ref, adjoint_hbm, send_ref, adjoint_ref, parts_ref, value_ref, sems):
        def write(k):
            return pltpu.make_async_copy(adjoint_ref.at[pl.ds(k * batch, batch)],
                                         adjoint_hbm.at[pl.ds(k * batch, batch)], sems.at[k])

        def back(t, state):
            i = planes - 1 - t
            out = []
            for h, rows in enumerate(halves(width)):
                e = block(back_ref, i, rows)
                out.append([field_ref[i, c, rows, :] - dot5(e[c], state[h]) for c in range(5)])
            for h, rows in enumerate(halves(width)):
                for c in range(5):
                    adjoint_ref[i, c, rows, :] = out[h][c]
            for c in range(5):
                high, low = split(jnp.concatenate([o[c] for o in out], axis=0))
                at = pl.ds(pl.multiple_of((i * 5 + c) * width, width), width)
                parts_ref[at, :LANES] = high
                parts_ref[at, LANES:] = low
            return out

        state = last_join(near_ref, reach_ref, other_ref, True, width)
        for k in reversed(range(planes // batch)):
            first = planes - (k + 1) * batch
            state = lax.fori_loop(first, first + batch, back, state)
            write(k).start()

        lane_iota = lax.broadcasted_iota(jnp.int32, (LANES, LANES), 0).astype(F32).astype(BF16)
        sub8 = lax.broadcasted_iota(jnp.int32, (8, LANES), 0)

        def gather(g, carry):
            cells = [cell_ref[pl.ds(g * group + u, 1), :] for u in range(group)]
            hots, offs = [], []
            for at in cells:
                lanes = jnp.broadcast_to((at % LANES).astype(F32), (LANES, LANES)).astype(BF16)
                hots.append(jnp.where(lane_iota == lanes, jnp.ones((LANES, LANES), BF16),
                                      jnp.zeros((LANES, LANES), BF16)))
                offs.append(jnp.broadcast_to(at // LANES, (8, LANES)) - sub8)
            hot = jnp.concatenate(hots, axis=1)
            hot = jnp.concatenate([hot, hot], axis=0)
            found = [[jnp.zeros((8, LANES), F32)] * 5 for _ in range(group)]
            for p in range(0, planes, piece):
                got = jnp.dot(parts_ref[p * 5 * width:(p + piece) * 5 * width, :], hot,
                              preferred_element_type=F32)
                for i in range(piece):
                    for h in range(width // 8):
                        for u in range(group):
                            mask = offs[u] == (p + i) * width + 8 * h
                            for c in range(5):
                                row = (i * 5 + c) * width + 8 * h
                                found[u][c] = jnp.where(mask, got[row:row + 8, u * LANES:(u + 1) * LANES],
                                                        found[u][c])
            weights = weight_ref[:, pl.ds(pl.multiple_of(g * (group * LANES), group * LANES), group * LANES)]
            for u in range(group):
                w = [jnp.broadcast_to(weights[c:c + 1, u * LANES:(u + 1) * LANES], (8, LANES)) for c in range(5)]
                value_ref[pl.ds(g * group + u, 1), :] = jnp.sum(dot5(w, found[u]), axis=0, keepdims=True)
            return carry

        lax.fori_loop(0, face_rows // group, gather, 0)
        live = lax.broadcasted_iota(jnp.int32, (face_rows, LANES), 0) * LANES + lax.broadcasted_iota(
            jnp.int32, (face_rows, LANES), 1) < count_ref[0]
        high, low = split(jnp.where(live, value_ref[...], 0.0))
        placed = place_in_slots(slot_ref[...], [high, low], bucket_rows)
        values = placed[0] + placed[1]
        for o in range(owners):
            here = slice(o * rows_each, (o + 1) * rows_each)
            both = jnp.concatenate([values[here], nodes_ref[here, :]], axis=0)
            for d in range(o, devices, owners):
                send_ref[d] = both
        for k in range(planes // batch):
            write(k).wait()

    return pl.pallas_call(
        kernel,
        out_shape=(
            jax.ShapeDtypeStruct(field.shape, F32),
            jax.ShapeDtypeStruct((devices, 2 * rows_each, LANES), F32),
        ),
        in_specs=[pl.BlockSpec(memory_space=pltpu.SMEM)] + vmem_specs(9),
        out_specs=(pl.BlockSpec(memory_space=pltpu.HBM), pl.BlockSpec(memory_space=VMEM)),
        scratch_shapes=[
            VMEM(field.shape, F32),
            VMEM((planes * 5 * width, 2 * LANES), BF16),
            VMEM((face_rows, LANES), F32),
            pltpu.SemaphoreType.DMA((planes // batch,)),
        ],
        compiler_params=pltpu.CompilerParams(vmem_limit_bytes=12 << 20),
        name="backward_and_faces",
    )(count, in_vmem(field), *[in_vmem(v) for v in arriving], in_vmem(back_ratio), in_vmem(cell),
      in_vmem(weight), in_vmem(slot), in_vmem(nodes))


def node_sums(got):
    devices, rows2, _ = got.shape
    rows_each = rows2 // 2
    side = NODES_DEV // LANES
    batch = 32 // rows_each

    def kernel(got_ref, out_ref):
        iota = lax.broadcasted_iota(jnp.int32, (LANES, LANES), 0).astype(F32).astype(BF16)
        side_iota = lax.broadcasted_iota(jnp.int32, (side, LANES), 0).astype(F32).astype(BF16)
        ones, zero = jnp.ones((LANES, LANES), BF16), jnp.zeros((LANES, LANES), BF16)
        side_zero = jnp.zeros((side, LANES), BF16)

        def body(t, total):
            lefts, rights = [], []
            for u in range(batch):
                d = t * batch + u
                node = got_ref[d, rows_each:, :].astype(jnp.int32)
                node_high = (node // LANES).astype(F32).astype(BF16)
                node_low = (node % LANES).astype(F32).astype(BF16)
                high, low = split(got_ref[d, :rows_each, :])
                for r in range(rows_each):

                    def spread(value, rows):
                        return jnp.broadcast_to(value[r:r + 1], (rows, LANES))

                    hot = side_iota == spread(node_high, side)
                    lefts.append(jnp.concatenate([
                        jnp.where(hot, spread(high, side), side_zero),
                        jnp.where(hot, spread(low, side), side_zero)], axis=0))
                    rights.append(jnp.where(iota == spread(node_low, LANES), ones, zero))
            return total + lax.dot_general(
                jnp.concatenate(lefts, axis=1), jnp.concatenate(rights, axis=1),
                (((1,), (1,)), ((), ())), preferred_element_type=F32)

        total = lax.fori_loop(0, devices // batch, body, jnp.zeros((2 * side, LANES), F32))
        out_ref[...] = total[:side] + total[side:]

    return pl.pallas_call(
        kernel,
        out_shape=jax.ShapeDtypeStruct((side, LANES), F32),
        in_specs=vmem_specs(1),
        out_specs=pl.BlockSpec(memory_space=VMEM),
        compiler_params=pltpu.CompilerParams(vmem_limit_bytes=8 << 20),
        name="node_sums",
    )(in_vmem(got))


def comes_after(stage, backward):
    bit = lax.rem(lax.div(lax.axis_index("sweep"), 1 << stage), 2)
    return bit == (0 if backward else 1)


def matvec(matrix, vector):
    return [dot5(row, vector) for row in matrix]


def matmat(matrix, other):
    return [[dot5(row, [other[e][x] for e in range(5)]) for x in range(5)] for row in matrix]


def load_matrix(ref, rows):
    return [[ref[c, d, rows, :] for d in range(5)] for c in range(5)]


def load_vector(ref, rows):
    return [ref[c, rows, :] for c in range(5)]


def pick(flag, one, two):
    if isinstance(one, list):
        return [pick(flag, a, b) for a, b in zip(one, two)]
    return jnp.where(flag, one, two)


def last_join(near_ref, reach_ref, other_ref, backward, width):
    after = comes_after(lax.axis_size("sweep").bit_length() - 2, backward)
    start = []
    for rows in halves(width):
        near = load_vector(near_ref, rows)
        gain = matvec(load_matrix(reach_ref, rows), load_vector(other_ref, rows))
        start.append([n + jnp.where(after, g, 0.0) for n, g in zip(near, gain)])
    return start


def join(stage, backward, near, reach, leaving, total, other, other_total, carry_total):
    first = near is None
    width = leaving.shape[1]
    outs = [leaving.shape, total.shape, leaving.shape] + ([total.shape] if carry_total else [])

    def kernel(*refs):
        ins, out = refs[:len(operands)], refs[len(operands):]
        after = comes_after(stage, backward)
        for rows in halves(width):
            own, theirs = load_vector(ins[0], rows), load_vector(ins[2], rows)
            own_total, their_total = load_matrix(ins[1], rows), load_matrix(ins[3], rows)
            if first:
                entering = theirs
                through = their_total
                before = [jnp.zeros((8, LANES), F32)] * 5
                unit = [[jnp.full((8, LANES), 1.0 if c == d else 0.0, F32) for d in range(5)] for c in range(5)]
            else:
                before, unit = load_vector(ins[4], rows), load_matrix(ins[5], rows)
                entering = [a + b for a, b in zip(before, matvec(unit, theirs))]
                through = matmat(unit, their_total)
            entering, through = pick(after, entering, before), pick(after, through, unit)
            downstream = pick(after, own_total, their_total)
            sent = matvec(downstream, pick(after, theirs, own))
            sent = [a + b for a, b in zip(pick(after, own, theirs), sent)]
            for c in range(5):
                out[0][c, rows, :] = entering[c]
                out[2][c, rows, :] = sent[c]
                for d in range(5):
                    out[1][c, d, rows, :] = through[c][d]
            if carry_total:
                whole = matmat(downstream, pick(after, their_total, own_total))
                for c in range(5):
                    for d in range(5):
                        out[3][c, d, rows, :] = whole[c][d]

    operands = [leaving, total, other, other_total] + ([] if first else [near, reach])
    return pl.pallas_call(
        kernel,
        out_shape=tuple(jax.ShapeDtypeStruct(shape, F32) for shape in outs),
        in_specs=vmem_specs(len(operands)),
        out_specs=tuple(vmem_specs(len(outs))),
        compiler_params=pltpu.CompilerParams(vmem_limit_bytes=4 << 20),
        name="join",
    )(*[in_vmem(v) for v in operands])


def relay(total, leaving, backward):
    size = lax.axis_size("sweep")
    stages = size.bit_length() - 1
    near = reach = None
    for stage in range(stages):
        pairs = [(i, i ^ (1 << stage)) for i in range(size)]
        other = lax.ppermute(leaving, "sweep", pairs)
        if stage == stages - 1:
            return (near, reach, other), leaving
        other_total = lax.ppermute(total, "sweep", pairs)
        carry_total = stage + 2 < stages
        joined = join(stage, backward, near, reach, leaving, total, other, other_total, carry_total)
        near, reach, leaving = joined[:3]
        if carry_total:
            total = joined[3]


def per_device(source, psi_old, lateral, lower_jac, upper_jac, diag_inv, face_weight, face_cell,
               face_owner, face_node, face_count):
    bulk = lax.axis_size("bulk")
    devices = bulk * lax.axis_size("sweep")
    low_pairs = [(i, i ^ 1) for i in range(bulk) if i ^ 1 < bulk]
    high_pairs = [(i, j) for i in range(bulk) for j in [i + 1 if i % 2 else i - 1] if 0 <= j < bulk]
    low_edge, high_edge = edge_rows(psi_old)
    first = lax.ppermute(low_edge, "bulk", low_pairs)
    second = lax.ppermute(high_edge, "bulk", high_pairs)

    ratio, total, scaled, leaving = forward_local(source, psi_old, lateral, first, second, lower_jac, diag_inv)
    arriving, joined = relay(total, leaving, False)
    upper_jac, joined = lax.optimization_barrier((upper_jac, joined))
    back_ratio, back_total = backward_matrices(upper_jac, diag_inv)
    field, leaving = forward_then_back(scaled, arriving, ratio, back_ratio)
    back_total, leaving = lax.optimization_barrier((back_total, leaving))
    arriving, _ = relay(back_total, leaving, True)

    slots = face_cell.shape[0]
    rows = (slots // LANES, LANES)
    slot, nodes = face_slots(face_owner.reshape(rows), face_node.reshape(rows), bulk)
    adjoint, send = backward_and_faces(field, arriving, back_ratio, face_count, face_cell.reshape(rows),
                                       face_weight, slot, nodes, devices, bulk)
    got = lax.all_to_all(send, ("sweep", "bulk"), 0, 0, tiled=True)
    return adjoint, node_sums(got).reshape(NODES_DEV)


def solution(mesh):
    placed = (
        P("sweep", None, "bulk", None),
        P("sweep", None, "bulk", None),
        P("sweep", None, "bulk", None),
        P("sweep", None, None, "bulk", None),
        P("sweep", None, None, "bulk", None),
        P("sweep", None, None, "bulk", None),
        P(None, ("sweep", "bulk")),
        P(("sweep", "bulk")),
        P(("sweep", "bulk"), None),
        P(("sweep", "bulk")),
        P(("sweep", "bulk")),
    )
    return jax.shard_map(
        per_device,
        mesh=mesh,
        in_specs=placed,
        out_specs=(P("sweep", None, "bulk", None), P("bulk")),
        check_vma=False,
    )
```

```python
import jax
import jax.numpy as jnp
from jax import lax
from jax.experimental import pallas as pl
from jax.experimental.pallas import tpu as pltpu
from jax.sharding import PartitionSpec as P

NODES_DEV = 16384
LANES = 128
F32 = jnp.float32
BF16 = jnp.bfloat16
VMEM = pltpu.VMEM


def dot5(a, b):
    p = [x * y for x, y in zip(a, b)]
    return ((p[0] + p[1]) + (p[2] + p[3])) + p[4]


def block(ref, at, rows):
    return [[ref[at, c, d, rows, :] for d in range(5)] for c in range(5)]


def halves(width):
    return [pl.ds(8 * h, 8) for h in range(width // 8)]


def in_vmem(value):
    return pltpu.with_memory_space_constraint(value, VMEM)


def in_hbm(value):
    return pltpu.with_memory_space_constraint(value, pltpu.HBM)


def vmem_specs(n):
    return [pl.BlockSpec(memory_space=VMEM)] * n


def ratio_of(coupled, inv, at, rows):
    j = block(coupled, at, rows)
    d = block(inv, at, rows)
    return [[dot5(d[c], [j[e][x] for e in range(5)]) for x in range(5)] for c in range(5)]


def next_total(ratio, total_ref, rows):
    old = [[total_ref[e, x, rows, :] for x in range(5)] for e in range(5)]
    return [[dot5(ratio[c], [old[e][x] for e in range(5)]) for x in range(5)] for c in range(5)]


def keep_matrices(ratio, total, ratio_ref, total_ref, at, rows):
    for c in range(5):
        for x in range(5):
            ratio_ref[at, c, x, rows, :] = ratio[c][x]
            total_ref[c, x, rows, :] = total[c][x]


def set_identity(total_ref, planes):
    sign = 1.0 if planes % 2 == 0 else -1.0
    for c in range(5):
        for d in range(5):
            total_ref[c, d] = jnp.full(total_ref.shape[2:], sign if c == d else 0.0, F32)


def edge_rows(psi):
    planes, fields, width, _ = psi.shape
    shape = (fields * planes, LANES)

    def kernel(psi_hbm, low_ref, high_ref, head_ref, tail_ref, sems):
        copies = []
        for c in range(fields):
            rows = pl.ds(c * planes, planes)
            copies.append(pltpu.make_async_copy(psi_hbm.at[:, c, 0, :], head_ref.at[rows], sems.at[0, c]))
            copies.append(pltpu.make_async_copy(psi_hbm.at[:, c, width - 1, :], tail_ref.at[rows], sems.at[1, c]))
        for copy in copies:
            copy.start()
        is_odd = lax.rem(lax.axis_index("bulk"), 2) == 1
        for copy in copies:
            copy.wait()
        head, tail = head_ref[...], tail_ref[...]
        low_ref[...] = jnp.where(is_odd, head, tail)
        high_ref[...] = jnp.where(is_odd, tail, head)

    return pl.pallas_call(
        kernel,
        out_shape=(jax.ShapeDtypeStruct(shape, F32), jax.ShapeDtypeStruct(shape, F32)),
        in_specs=[pl.BlockSpec(memory_space=pltpu.HBM)],
        out_specs=tuple(vmem_specs(2)),
        scratch_shapes=[VMEM(shape, F32), VMEM(shape, F32), pltpu.SemaphoreType.DMA((2, fields))],
        compiler_params=pltpu.CompilerParams(vmem_limit_bytes=4 << 20),
        cost_estimate=pl.CostEstimate(flops=10_000_000_000, bytes_accessed=20_000_000, transcendentals=0),
        name="edge_rows",
    )(in_hbm(psi))


def forward_local(source, psi, lateral, first, second, ratio, inv):
    planes, width = source.shape[0], source.shape[2]

    def kernel(source_ref, psi_ref, lateral_ref, first_ref, second_ref, ratio_ref, inv_ref,
               scaled_ref, leaving_ref):
        is_odd = lax.rem(lax.axis_index("bulk"), 2) == 1

        def body(i, state):
            below, above = lateral_ref[i, 0], lateral_ref[i, 1]
            right = []
            for c in range(5):
                one = first_ref[pl.ds(c * planes + i, 1), :]
                two = second_ref[pl.ds(c * planes + i, 1), :]
                here = psi_ref[i, c]
                down = jnp.concatenate([jnp.where(is_odd, one, two), here[:width - 1]], axis=0)
                up = jnp.concatenate([here[1:], jnp.where(is_odd, two, one)], axis=0)
                right.append(source_ref[i, c] - below * down - above * up)
            out = []
            for h, rows in enumerate(halves(width)):
                r = [v[8 * h:8 * h + 8] for v in right]
                d = block(inv_ref, i, rows)
                e = block(ratio_ref, i, rows)
                g = [dot5(d[c], r) for c in range(5)]
                out.append((g, [g[c] - dot5(e[c], state[h]) for c in range(5)]))
            for h, rows in enumerate(halves(width)):
                for c in range(5):
                    scaled_ref[i, c, rows, :] = out[h][0][c]
            return [f for _, f in out]

        zero = [[jnp.zeros((8, LANES), F32)] * 5 for _ in halves(width)]
        state = lax.fori_loop(0, planes, body, zero)
        for h, rows in enumerate(halves(width)):
            for c in range(5):
                leaving_ref[c, rows, :] = state[h][c]

    return pl.pallas_call(
        kernel,
        out_shape=(VMEM(source.shape, F32), jax.ShapeDtypeStruct(source.shape[1:], F32)),
        in_specs=vmem_specs(7),
        out_specs=tuple(vmem_specs(2)),
        compiler_params=pltpu.CompilerParams(vmem_limit_bytes=4 << 20),
        name="forward_local",
    )(*[in_vmem(v) for v in (source, psi, lateral, first, second, ratio, inv)])


def matrices(coupled, inv, backward, name):
    planes, width = coupled.shape[0], coupled.shape[3]

    def kernel(coupled_ref, inv_ref, ratio_ref, total_ref):
        set_identity(total_ref, planes)

        def body(t, carry):
            at = planes - 1 - t if backward else t
            for rows in halves(width):
                ratio = ratio_of(coupled_ref, inv_ref, at, rows)
                keep_matrices(ratio, next_total(ratio, total_ref, rows), ratio_ref, total_ref, at, rows)
            return carry

        lax.fori_loop(0, planes, body, 0, unroll=2)

    return pl.pallas_call(
        kernel,
        out_shape=(VMEM(coupled.shape, F32), jax.ShapeDtypeStruct(coupled.shape[1:], F32)),
        in_specs=vmem_specs(2),
        out_specs=tuple(vmem_specs(2)),
        compiler_params=pltpu.CompilerParams(vmem_limit_bytes=4 << 20),
        cost_estimate=pl.CostEstimate(flops=5_000_000_000, bytes_accessed=20_000_000, transcendentals=0),
        name=name,
    )(in_vmem(coupled), in_vmem(inv))


def forward_then_back(scaled, arriving, ratio, back_ratio):
    planes, width = scaled.shape[0], scaled.shape[2]

    def kernel(scaled_ref, near_ref, reach_ref, other_ref, ratio_ref, back_ref, field_ref, leaving_ref):
        def ahead(i, state):
            out = []
            for h, rows in enumerate(halves(width)):
                e = block(ratio_ref, i, rows)
                out.append([scaled_ref[i, c, rows, :] - dot5(e[c], state[h]) for c in range(5)])
            for h, rows in enumerate(halves(width)):
                for c in range(5):
                    field_ref[i, c, rows, :] = out[h][c]
            return out

        start = last_join(near_ref, reach_ref, other_ref, False, width)
        lax.fori_loop(0, planes, ahead, start)

        def back(t, state):
            i = planes - 1 - t
            out = []
            for h, rows in enumerate(halves(width)):
                e = block(back_ref, i, rows)
                out.append([field_ref[i, c, rows, :] - dot5(e[c], state[h]) for c in range(5)])
            return out

        zero = [[jnp.zeros((8, LANES), F32)] * 5 for _ in halves(width)]
        state = lax.fori_loop(0, planes, back, zero)
        for h, rows in enumerate(halves(width)):
            for c in range(5):
                leaving_ref[c, rows, :] = state[h][c]

    return pl.pallas_call(
        kernel,
        out_shape=(VMEM(scaled.shape, F32), jax.ShapeDtypeStruct(scaled.shape[1:], F32)),
        in_specs=vmem_specs(6),
        out_specs=tuple(vmem_specs(2)),
        compiler_params=pltpu.CompilerParams(vmem_limit_bytes=4 << 20),
        name="forward_then_back",
    )(in_vmem(scaled), *[in_vmem(v) for v in arriving], in_vmem(ratio), in_vmem(back_ratio))


def face_slots(owner, node, owners):
    face_rows = owner.shape[0]
    cap = 2 * face_rows * LANES // owners
    bucket_rows = 2 * face_rows

    def kernel(owner_ref, node_ref, slot_ref, nodes_ref):
        sub = lax.broadcasted_iota(jnp.int32, (LANES, LANES), 0)
        lane = lax.broadcasted_iota(jnp.int32, (LANES, LANES), 1)
        strict = (sub < lane).astype(F32).astype(BF16)
        ones = jnp.ones((LANES, LANES), BF16)
        fs = lax.broadcasted_iota(jnp.int32, (face_rows, face_rows), 0)
        fl = lax.broadcasted_iota(jnp.int32, (face_rows, face_rows), 1)
        lower = (fl < fs).astype(F32).astype(BF16)
        own = owner_ref[...]
        masks = [(own == o).astype(F32) for o in range(owners)]
        stacked = jnp.concatenate(masks, axis=0).astype(BF16)
        before = jnp.dot(stacked, strict, preferred_element_type=F32)
        totals = jnp.dot(stacked, ones, preferred_element_type=F32).astype(BF16)
        rank = jnp.zeros((face_rows, LANES), F32)
        for o in range(owners):
            here = slice(o * face_rows, (o + 1) * face_rows)
            offset = jnp.dot(lower, totals[here], preferred_element_type=F32)
            rank = rank + masks[o] * (before[here] + offset + float(o * cap))
        slot = rank.astype(jnp.int32)
        slot_ref[...] = slot
        nodes = node_ref[...]
        high = (nodes // LANES).astype(F32)
        low = (nodes % LANES).astype(F32)
        parts = place_in_slots(slot, [high, low], bucket_rows)
        nodes_ref[...] = float(LANES) * parts[0] + parts[1]

    return pl.pallas_call(
        kernel,
        out_shape=(VMEM((face_rows, LANES), jnp.int32), VMEM((bucket_rows, LANES), F32)),
        in_specs=vmem_specs(2),
        out_specs=tuple(vmem_specs(2)),
        compiler_params=pltpu.CompilerParams(vmem_limit_bytes=4 << 20),
        cost_estimate=pl.CostEstimate(flops=4_000_000, bytes_accessed=10_000_000, transcendentals=0),
        name="face_slots",
    )(in_vmem(owner), in_vmem(node))


def split(value):
    high = value.astype(BF16)
    return high, (value - high.astype(F32)).astype(BF16)


def place_in_slots(slot, parts, bucket_rows):
    face_rows = slot.shape[0]
    high = (slot // LANES).astype(F32).astype(BF16)
    low = (slot % LANES).astype(F32).astype(BF16)
    parts = [p.astype(BF16) for p in parts]
    high_iota = lax.broadcasted_iota(jnp.int32, (bucket_rows, LANES), 0).astype(F32).astype(BF16)
    low_iota = lax.broadcasted_iota(jnp.int32, (LANES, LANES), 0).astype(F32).astype(BF16)
    zero = jnp.zeros((bucket_rows, LANES), BF16)
    lefts, rights = [], []
    for f in range(face_rows):

        def spread(value, rows):
            return jnp.broadcast_to(value[f:f + 1], (rows, LANES))

        hot = high_iota == spread(high, bucket_rows)
        lefts.append(jnp.concatenate([jnp.where(hot, spread(p, bucket_rows), zero) for p in parts], axis=0))
        rights.append(jnp.where(low_iota == spread(low, LANES), jnp.ones((LANES, LANES), BF16),
                                jnp.zeros((LANES, LANES), BF16)))
    out = lax.dot_general(jnp.concatenate(lefts, axis=1), jnp.concatenate(rights, axis=1),
                          (((1,), (1,)), ((), ())), preferred_element_type=F32)
    return [out[k * bucket_rows:(k + 1) * bucket_rows] for k in range(len(parts))]


def backward_and_faces(field, arriving, back_ratio, count, cell, weight, slot, nodes, devices, owners):
    planes, width = field.shape[0], field.shape[2]
    face_rows = cell.shape[0]
    bucket_rows = nodes.shape[0]
    rows_each = bucket_rows // owners
    group = 2
    piece = 4
    batch = 8

    def kernel(count_ref, field_ref, near_ref, reach_ref, other_ref, back_ref, cell_ref, weight_ref,
               slot_ref, nodes_ref, adjoint_hbm, send_ref, adjoint_ref, parts_ref, value_ref, sems):
        def write(k):
            return pltpu.make_async_copy(adjoint_ref.at[pl.ds(k * batch, batch)],
                                         adjoint_hbm.at[pl.ds(k * batch, batch)], sems.at[k])

        def back(t, state):
            i = planes - 1 - t
            out = []
            for h, rows in enumerate(halves(width)):
                e = block(back_ref, i, rows)
                out.append([field_ref[i, c, rows, :] - dot5(e[c], state[h]) for c in range(5)])
            for h, rows in enumerate(halves(width)):
                for c in range(5):
                    adjoint_ref[i, c, rows, :] = out[h][c]
            for c in range(5):
                high, low = split(jnp.concatenate([o[c] for o in out], axis=0))
                at = pl.ds(pl.multiple_of((i * 5 + c) * width, width), width)
                parts_ref[at, :LANES] = high
                parts_ref[at, LANES:] = low
            return out

        state = last_join(near_ref, reach_ref, other_ref, True, width)
        for k in reversed(range(planes // batch)):
            first = planes - (k + 1) * batch
            state = lax.fori_loop(first, first + batch, back, state)
            write(k).start()

        lane_iota = lax.broadcasted_iota(jnp.int32, (LANES, LANES), 0).astype(F32).astype(BF16)
        sub8 = lax.broadcasted_iota(jnp.int32, (8, LANES), 0)

        def gather(g, carry):
            cells = [cell_ref[pl.ds(g * group + u, 1), :] for u in range(group)]
            hots, offs = [], []
            for at in cells:
                lanes = jnp.broadcast_to((at % LANES).astype(F32), (LANES, LANES)).astype(BF16)
                hots.append(jnp.where(lane_iota == lanes, jnp.ones((LANES, LANES), BF16),
                                      jnp.zeros((LANES, LANES), BF16)))
                offs.append(jnp.broadcast_to(at // LANES, (8, LANES)) - sub8)
            hot = jnp.concatenate(hots, axis=1)
            hot = jnp.concatenate([hot, hot], axis=0)
            found = [[jnp.zeros((8, LANES), F32)] * 5 for _ in range(group)]
            for p in range(0, planes, piece):
                got = jnp.dot(parts_ref[p * 5 * width:(p + piece) * 5 * width, :], hot,
                              preferred_element_type=F32)
                for i in range(piece):
                    for h in range(width // 8):
                        for u in range(group):
                            mask = offs[u] == (p + i) * width + 8 * h
                            for c in range(5):
                                row = (i * 5 + c) * width + 8 * h
                                found[u][c] = jnp.where(mask, got[row:row + 8, u * LANES:(u + 1) * LANES],
                                                        found[u][c])
            weights = weight_ref[:, pl.ds(pl.multiple_of(g * (group * LANES), group * LANES), group * LANES)]
            for u in range(group):
                w = [jnp.broadcast_to(weights[c:c + 1, u * LANES:(u + 1) * LANES], (8, LANES)) for c in range(5)]
                value_ref[pl.ds(g * group + u, 1), :] = jnp.sum(dot5(w, found[u]), axis=0, keepdims=True)
            return carry

        lax.fori_loop(0, face_rows // group, gather, 0)
        live = lax.broadcasted_iota(jnp.int32, (face_rows, LANES), 0) * LANES + lax.broadcasted_iota(
            jnp.int32, (face_rows, LANES), 1) < count_ref[0]
        high, low = split(jnp.where(live, value_ref[...], 0.0))
        placed = place_in_slots(slot_ref[...], [high, low], bucket_rows)
        values = placed[0] + placed[1]
        for o in range(owners):
            here = slice(o * rows_each, (o + 1) * rows_each)
            both = jnp.concatenate([values[here], nodes_ref[here, :]], axis=0)
            for d in range(o, devices, owners):
                send_ref[d] = both
        for k in range(planes // batch):
            write(k).wait()

    return pl.pallas_call(
        kernel,
        out_shape=(
            jax.ShapeDtypeStruct(field.shape, F32),
            jax.ShapeDtypeStruct((devices, 2 * rows_each, LANES), F32),
        ),
        in_specs=[pl.BlockSpec(memory_space=pltpu.SMEM)] + vmem_specs(9),
        out_specs=(pl.BlockSpec(memory_space=pltpu.HBM), pl.BlockSpec(memory_space=VMEM)),
        scratch_shapes=[
            VMEM(field.shape, F32),
            VMEM((planes * 5 * width, 2 * LANES), BF16),
            VMEM((face_rows, LANES), F32),
            pltpu.SemaphoreType.DMA((planes // batch,)),
        ],
        compiler_params=pltpu.CompilerParams(vmem_limit_bytes=12 << 20),
        name="backward_and_faces",
    )(count, in_vmem(field), *[in_vmem(v) for v in arriving], in_vmem(back_ratio), in_vmem(cell),
      in_vmem(weight), in_vmem(slot), in_vmem(nodes))


def node_sums(got):
    devices, rows2, _ = got.shape
    rows_each = rows2 // 2
    side = NODES_DEV // LANES
    batch = 32 // rows_each

    def kernel(got_ref, out_ref):
        iota = lax.broadcasted_iota(jnp.int32, (LANES, LANES), 0).astype(F32).astype(BF16)
        side_iota = lax.broadcasted_iota(jnp.int32, (side, LANES), 0).astype(F32).astype(BF16)
        ones, zero = jnp.ones((LANES, LANES), BF16), jnp.zeros((LANES, LANES), BF16)
        side_zero = jnp.zeros((side, LANES), BF16)

        def body(t, total):
            lefts, rights = [], []
            for u in range(batch):
                d = t * batch + u
                node = got_ref[d, rows_each:, :].astype(jnp.int32)
                node_high = (node // LANES).astype(F32).astype(BF16)
                node_low = (node % LANES).astype(F32).astype(BF16)
                high, low = split(got_ref[d, :rows_each, :])
                for r in range(rows_each):

                    def spread(value, rows):
                        return jnp.broadcast_to(value[r:r + 1], (rows, LANES))

                    hot = side_iota == spread(node_high, side)
                    lefts.append(jnp.concatenate([
                        jnp.where(hot, spread(high, side), side_zero),
                        jnp.where(hot, spread(low, side), side_zero)], axis=0))
                    rights.append(jnp.where(iota == spread(node_low, LANES), ones, zero))
            return total + lax.dot_general(
                jnp.concatenate(lefts, axis=1), jnp.concatenate(rights, axis=1),
                (((1,), (1,)), ((), ())), preferred_element_type=F32)

        total = lax.fori_loop(0, devices // batch, body, jnp.zeros((2 * side, LANES), F32))
        out_ref[...] = total[:side] + total[side:]

    return pl.pallas_call(
        kernel,
        out_shape=jax.ShapeDtypeStruct((side, LANES), F32),
        in_specs=vmem_specs(1),
        out_specs=pl.BlockSpec(memory_space=VMEM),
        compiler_params=pltpu.CompilerParams(vmem_limit_bytes=8 << 20),
        name="node_sums",
    )(in_vmem(got))


def comes_after(stage, backward):
    bit = lax.rem(lax.div(lax.axis_index("sweep"), 1 << stage), 2)
    return bit == (0 if backward else 1)


def matvec(matrix, vector):
    return [dot5(row, vector) for row in matrix]


def matmat(matrix, other):
    return [[dot5(row, [other[e][x] for e in range(5)]) for x in range(5)] for row in matrix]


def load_matrix(ref, rows):
    return [[ref[c, d, rows, :] for d in range(5)] for c in range(5)]


def load_vector(ref, rows):
    return [ref[c, rows, :] for c in range(5)]


def pick(flag, one, two):
    if isinstance(one, list):
        return [pick(flag, a, b) for a, b in zip(one, two)]
    return jnp.where(flag, one, two)


def last_join(near_ref, reach_ref, other_ref, backward, width):
    after = comes_after(lax.axis_size("sweep").bit_length() - 2, backward)
    start = []
    for rows in halves(width):
        near = load_vector(near_ref, rows)
        gain = matvec(load_matrix(reach_ref, rows), load_vector(other_ref, rows))
        start.append([n + jnp.where(after, g, 0.0) for n, g in zip(near, gain)])
    return start


def join(stage, backward, near, reach, leaving, total, other, other_total, carry_total):
    first = near is None
    width = leaving.shape[1]
    outs = [leaving.shape, total.shape, leaving.shape] + ([total.shape] if carry_total else [])

    def kernel(*refs):
        ins, out = refs[:len(operands)], refs[len(operands):]
        after = comes_after(stage, backward)
        for rows in halves(width):
            own, theirs = load_vector(ins[0], rows), load_vector(ins[2], rows)
            own_total, their_total = load_matrix(ins[1], rows), load_matrix(ins[3], rows)
            if first:
                entering = theirs
                through = their_total
                before = [jnp.zeros((8, LANES), F32)] * 5
                unit = [[jnp.full((8, LANES), 1.0 if c == d else 0.0, F32) for d in range(5)] for c in range(5)]
            else:
                before, unit = load_vector(ins[4], rows), load_matrix(ins[5], rows)
                entering = [a + b for a, b in zip(before, matvec(unit, theirs))]
                through = matmat(unit, their_total)
            entering, through = pick(after, entering, before), pick(after, through, unit)
            downstream = pick(after, own_total, their_total)
            sent = matvec(downstream, pick(after, theirs, own))
            sent = [a + b for a, b in zip(pick(after, own, theirs), sent)]
            for c in range(5):
                out[0][c, rows, :] = entering[c]
                out[2][c, rows, :] = sent[c]
                for d in range(5):
                    out[1][c, d, rows, :] = through[c][d]
            if carry_total:
                whole = matmat(downstream, pick(after, their_total, own_total))
                for c in range(5):
                    for d in range(5):
                        out[3][c, d, rows, :] = whole[c][d]

    operands = [leaving, total, other, other_total] + ([] if first else [near, reach])
    return pl.pallas_call(
        kernel,
        out_shape=tuple(jax.ShapeDtypeStruct(shape, F32) for shape in outs),
        in_specs=vmem_specs(len(operands)),
        out_specs=tuple(vmem_specs(len(outs))),
        compiler_params=pltpu.CompilerParams(vmem_limit_bytes=4 << 20),
        name="join",
    )(*[in_vmem(v) for v in operands])


def relay(total, leaving, backward):
    size = lax.axis_size("sweep")
    stages = size.bit_length() - 1
    near = reach = None
    for stage in range(stages):
        pairs = [(i, i ^ (1 << stage)) for i in range(size)]
        other = lax.ppermute(leaving, "sweep", pairs)
        if stage == stages - 1:
            return (near, reach, other), leaving
        other_total = lax.ppermute(total, "sweep", pairs)
        carry_total = stage + 2 < stages
        joined = join(stage, backward, near, reach, leaving, total, other, other_total, carry_total)
        near, reach, leaving = joined[:3]
        if carry_total:
            total = joined[3]


def per_device(source, psi_old, lateral, lower_jac, upper_jac, diag_inv, face_weight, face_cell,
               face_owner, face_node, face_count):
    bulk = lax.axis_size("bulk")
    devices = bulk * lax.axis_size("sweep")
    low_pairs = [(i, i ^ 1) for i in range(bulk) if i ^ 1 < bulk]
    high_pairs = [(i, j) for i in range(bulk) for j in [i + 1 if i % 2 else i - 1] if 0 <= j < bulk]
    low_edge, high_edge = edge_rows(psi_old)
    low_edge, high_edge, lower_jac = lax.optimization_barrier((low_edge, high_edge, lower_jac))
    first = lax.ppermute(low_edge, "bulk", low_pairs)
    second = lax.ppermute(high_edge, "bulk", high_pairs)

    ratio, total = matrices(lower_jac, diag_inv, False, "forward_matrices")
    scaled, leaving = forward_local(source, psi_old, lateral, first, second, ratio, diag_inv)
    total, leaving = lax.optimization_barrier((total, leaving))
    arriving, joined = relay(total, leaving, False)
    upper_jac, joined = lax.optimization_barrier((upper_jac, joined))
    back_ratio, back_total = matrices(upper_jac, diag_inv, True, "backward_matrices")
    field, leaving = forward_then_back(scaled, arriving, ratio, back_ratio)
    back_total, leaving = lax.optimization_barrier((back_total, leaving))
    arriving, _ = relay(back_total, leaving, True)

    slots = face_cell.shape[0]
    rows = (slots // LANES, LANES)
    slot, nodes = face_slots(face_owner.reshape(rows), face_node.reshape(rows), bulk)
    adjoint, send = backward_and_faces(field, arriving, back_ratio, face_count, face_cell.reshape(rows),
                                       face_weight, slot, nodes, devices, bulk)
    got = lax.all_to_all(send, ("sweep", "bulk"), 0, 0, tiled=True)
    return adjoint, node_sums(got).reshape(NODES_DEV)


def solution(mesh):
    placed = (
        P("sweep", None, "bulk", None),
        P("sweep", None, "bulk", None),
        P("sweep", None, "bulk", None),
        P("sweep", None, None, "bulk", None),
        P("sweep", None, None, "bulk", None),
        P("sweep", None, None, "bulk", None),
        P(None, ("sweep", "bulk")),
        P(("sweep", "bulk")),
        P(("sweep", "bulk"), None),
        P(("sweep", "bulk")),
        P(("sweep", "bulk")),
    )
    return jax.shard_map(
        per_device,
        mesh=mesh,
        in_specs=placed,
        out_specs=(P("sweep", None, "bulk", None), P("bulk")),
        check_vma=False,
    )
```

```python
import jax
import jax.numpy as jnp
from jax import lax
from jax.experimental import pallas as pl
from jax.experimental.pallas import tpu as pltpu
from jax.sharding import PartitionSpec as P

NODES_DEV = 16384
LANES = 128
F32 = jnp.float32
BF16 = jnp.bfloat16
VMEM = pltpu.VMEM


def dot5(a, b):
    p = [x * y for x, y in zip(a, b)]
    return ((p[0] + p[1]) + (p[2] + p[3])) + p[4]


def block(ref, at, rows):
    return [[ref[at, c, d, rows, :] for d in range(5)] for c in range(5)]


def halves(width):
    return [pl.ds(8 * h, 8) for h in range(width // 8)]


def in_vmem(value):
    return pltpu.with_memory_space_constraint(value, VMEM)


def in_hbm(value):
    return pltpu.with_memory_space_constraint(value, pltpu.HBM)


def vmem_specs(n):
    return [pl.BlockSpec(memory_space=VMEM)] * n


def ratio_of(coupled, inv, at, rows):
    j = block(coupled, at, rows)
    d = block(inv, at, rows)
    return [[dot5(d[c], [j[e][x] for e in range(5)]) for x in range(5)] for c in range(5)]


def next_total(ratio, total_ref, rows):
    old = [[total_ref[e, x, rows, :] for x in range(5)] for e in range(5)]
    return [[dot5(ratio[c], [old[e][x] for e in range(5)]) for x in range(5)] for c in range(5)]


def keep_matrices(ratio, total, ratio_ref, total_ref, at, rows):
    for c in range(5):
        for x in range(5):
            ratio_ref[at, c, x, rows, :] = ratio[c][x]
            total_ref[c, x, rows, :] = total[c][x]


def set_identity(total_ref, planes):
    sign = 1.0 if planes % 2 == 0 else -1.0
    for c in range(5):
        for d in range(5):
            total_ref[c, d] = jnp.full(total_ref.shape[2:], sign if c == d else 0.0, F32)


def edge_rows(psi):
    planes, fields, width, _ = psi.shape
    shape = (fields * planes, LANES)

    def kernel(psi_hbm, low_ref, high_ref, head_ref, tail_ref, sems):
        copies = []
        for c in range(fields):
            rows = pl.ds(c * planes, planes)
            copies.append(pltpu.make_async_copy(psi_hbm.at[:, c, 0, :], head_ref.at[rows], sems.at[0, c]))
            copies.append(pltpu.make_async_copy(psi_hbm.at[:, c, width - 1, :], tail_ref.at[rows], sems.at[1, c]))
        for copy in copies:
            copy.start()
        is_odd = lax.rem(lax.axis_index("bulk"), 2) == 1
        for copy in copies:
            copy.wait()
        head, tail = head_ref[...], tail_ref[...]
        low_ref[...] = jnp.where(is_odd, head, tail)
        high_ref[...] = jnp.where(is_odd, tail, head)

    return pl.pallas_call(
        kernel,
        out_shape=(jax.ShapeDtypeStruct(shape, F32), jax.ShapeDtypeStruct(shape, F32)),
        in_specs=[pl.BlockSpec(memory_space=pltpu.HBM)],
        out_specs=tuple(vmem_specs(2)),
        scratch_shapes=[VMEM(shape, F32), VMEM(shape, F32), pltpu.SemaphoreType.DMA((2, fields))],
        compiler_params=pltpu.CompilerParams(vmem_limit_bytes=4 << 20),
        cost_estimate=pl.CostEstimate(flops=10_000_000_000, bytes_accessed=20_000_000, transcendentals=0),
        name="edge_rows",
    )(in_hbm(psi))


def forward_local(source, psi, lateral, first, second, ratio, inv):
    planes, width = source.shape[0], source.shape[2]

    def kernel(source_ref, psi_ref, lateral_ref, first_ref, second_ref, ratio_ref, inv_ref,
               scaled_ref, leaving_ref):
        is_odd = lax.rem(lax.axis_index("bulk"), 2) == 1

        def body(i, state):
            below, above = lateral_ref[i, 0], lateral_ref[i, 1]
            right = []
            for c in range(5):
                one = first_ref[pl.ds(c * planes + i, 1), :]
                two = second_ref[pl.ds(c * planes + i, 1), :]
                here = psi_ref[i, c]
                down = jnp.concatenate([jnp.where(is_odd, one, two), here[:width - 1]], axis=0)
                up = jnp.concatenate([here[1:], jnp.where(is_odd, two, one)], axis=0)
                right.append(source_ref[i, c] - below * down - above * up)
            out = []
            for h, rows in enumerate(halves(width)):
                r = [v[8 * h:8 * h + 8] for v in right]
                d = block(inv_ref, i, rows)
                e = block(ratio_ref, i, rows)
                g = [dot5(d[c], r) for c in range(5)]
                out.append((g, [g[c] - dot5(e[c], state[h]) for c in range(5)]))
            for h, rows in enumerate(halves(width)):
                for c in range(5):
                    scaled_ref[i, c, rows, :] = out[h][0][c]
            return [f for _, f in out]

        zero = [[jnp.zeros((8, LANES), F32)] * 5 for _ in halves(width)]
        state = lax.fori_loop(0, planes, body, zero, unroll=2)
        for h, rows in enumerate(halves(width)):
            for c in range(5):
                leaving_ref[c, rows, :] = state[h][c]

    return pl.pallas_call(
        kernel,
        out_shape=(VMEM(source.shape, F32), jax.ShapeDtypeStruct(source.shape[1:], F32)),
        in_specs=vmem_specs(7),
        out_specs=tuple(vmem_specs(2)),
        compiler_params=pltpu.CompilerParams(vmem_limit_bytes=4 << 20),
        name="forward_local",
    )(*[in_vmem(v) for v in (source, psi, lateral, first, second, ratio, inv)])


def matrices(coupled, inv, backward, name):
    planes, width = coupled.shape[0], coupled.shape[3]

    def kernel(coupled_ref, inv_ref, ratio_ref, total_ref):
        set_identity(total_ref, planes)

        def body(t, carry):
            at = planes - 1 - t if backward else t
            for rows in halves(width):
                ratio = ratio_of(coupled_ref, inv_ref, at, rows)
                keep_matrices(ratio, next_total(ratio, total_ref, rows), ratio_ref, total_ref, at, rows)
            return carry

        lax.fori_loop(0, planes, body, 0, unroll=2)

    return pl.pallas_call(
        kernel,
        out_shape=(VMEM(coupled.shape, F32), jax.ShapeDtypeStruct(coupled.shape[1:], F32)),
        in_specs=vmem_specs(2),
        out_specs=tuple(vmem_specs(2)),
        compiler_params=pltpu.CompilerParams(vmem_limit_bytes=4 << 20),
        cost_estimate=pl.CostEstimate(flops=5_000_000_000, bytes_accessed=20_000_000, transcendentals=0),
        name=name,
    )(in_vmem(coupled), in_vmem(inv))


def forward_then_back(scaled, arriving, ratio, back_ratio):
    planes, width = scaled.shape[0], scaled.shape[2]

    def kernel(scaled_ref, near_ref, reach_ref, other_ref, ratio_ref, back_ref, field_ref, leaving_ref):
        def ahead(i, state):
            out = []
            for h, rows in enumerate(halves(width)):
                e = block(ratio_ref, i, rows)
                out.append([scaled_ref[i, c, rows, :] - dot5(e[c], state[h]) for c in range(5)])
            for h, rows in enumerate(halves(width)):
                for c in range(5):
                    field_ref[i, c, rows, :] = out[h][c]
            return out

        start = last_join(near_ref, reach_ref, other_ref, False, width)
        lax.fori_loop(0, planes, ahead, start, unroll=4)

        def back(t, state):
            i = planes - 1 - t
            out = []
            for h, rows in enumerate(halves(width)):
                e = block(back_ref, i, rows)
                out.append([field_ref[i, c, rows, :] - dot5(e[c], state[h]) for c in range(5)])
            return out

        zero = [[jnp.zeros((8, LANES), F32)] * 5 for _ in halves(width)]
        state = lax.fori_loop(0, planes, back, zero, unroll=4)
        for h, rows in enumerate(halves(width)):
            for c in range(5):
                leaving_ref[c, rows, :] = state[h][c]

    return pl.pallas_call(
        kernel,
        out_shape=(VMEM(scaled.shape, F32), jax.ShapeDtypeStruct(scaled.shape[1:], F32)),
        in_specs=vmem_specs(6),
        out_specs=tuple(vmem_specs(2)),
        compiler_params=pltpu.CompilerParams(vmem_limit_bytes=4 << 20),
        name="forward_then_back",
    )(in_vmem(scaled), *[in_vmem(v) for v in arriving], in_vmem(ratio), in_vmem(back_ratio))


def face_slots(owner, node, owners):
    face_rows = owner.shape[0]
    cap = 2 * face_rows * LANES // owners
    bucket_rows = 2 * face_rows

    def kernel(owner_ref, node_ref, slot_ref, nodes_ref):
        sub = lax.broadcasted_iota(jnp.int32, (LANES, LANES), 0)
        lane = lax.broadcasted_iota(jnp.int32, (LANES, LANES), 1)
        strict = (sub < lane).astype(F32).astype(BF16)
        ones = jnp.ones((LANES, LANES), BF16)
        fs = lax.broadcasted_iota(jnp.int32, (face_rows, face_rows), 0)
        fl = lax.broadcasted_iota(jnp.int32, (face_rows, face_rows), 1)
        lower = (fl < fs).astype(F32).astype(BF16)
        own = owner_ref[...]
        masks = [(own == o).astype(F32) for o in range(owners)]
        stacked = jnp.concatenate(masks, axis=0).astype(BF16)
        before = jnp.dot(stacked, strict, preferred_element_type=F32)
        totals = jnp.dot(stacked, ones, preferred_element_type=F32).astype(BF16)
        rank = jnp.zeros((face_rows, LANES), F32)
        for o in range(owners):
            here = slice(o * face_rows, (o + 1) * face_rows)
            offset = jnp.dot(lower, totals[here], preferred_element_type=F32)
            rank = rank + masks[o] * (before[here] + offset + float(o * cap))
        slot = rank.astype(jnp.int32)
        slot_ref[...] = slot
        nodes = node_ref[...]
        high = (nodes // LANES).astype(F32)
        low = (nodes % LANES).astype(F32)
        parts = place_in_slots(slot, [high, low], bucket_rows)
        nodes_ref[...] = float(LANES) * parts[0] + parts[1]

    return pl.pallas_call(
        kernel,
        out_shape=(VMEM((face_rows, LANES), jnp.int32), VMEM((bucket_rows, LANES), F32)),
        in_specs=vmem_specs(2),
        out_specs=tuple(vmem_specs(2)),
        compiler_params=pltpu.CompilerParams(vmem_limit_bytes=4 << 20),
        cost_estimate=pl.CostEstimate(flops=4_000_000, bytes_accessed=10_000_000, transcendentals=0),
        name="face_slots",
    )(in_vmem(owner), in_vmem(node))


def spread(row, rows):
    tile = jnp.broadcast_to(row, (16, LANES)).astype(BF16)
    return jnp.concatenate([tile] * (rows // 16), axis=0)


def split(value):
    high = value.astype(BF16)
    return high, (value - high.astype(F32)).astype(BF16)


def place_in_slots(slot, parts, bucket_rows):
    face_rows = slot.shape[0]
    high = (slot // LANES).astype(F32)
    low = (slot % LANES).astype(F32)
    parts = [p.astype(F32) for p in parts]
    high_iota = lax.broadcasted_iota(jnp.int32, (bucket_rows, LANES), 0).astype(F32).astype(BF16)
    low_iota = lax.broadcasted_iota(jnp.int32, (LANES, LANES), 0).astype(F32).astype(BF16)
    ones, none = jnp.ones((LANES, LANES), BF16), jnp.zeros((LANES, LANES), BF16)
    zero = jnp.zeros((bucket_rows, LANES), BF16)
    lefts, rights = [], []
    for f in range(face_rows):
        row = slice(f, f + 1)
        hot = high_iota == spread(high[row], bucket_rows)
        lefts.append(jnp.concatenate(
            [jnp.where(hot, spread(p[row], bucket_rows), zero) for p in parts], axis=0))
        rights.append(jnp.where(low_iota == spread(low[row], LANES), ones, none))
    out = lax.dot_general(jnp.concatenate(lefts, axis=1), jnp.concatenate(rights, axis=1),
                          (((1,), (1,)), ((), ())), preferred_element_type=F32)
    return [out[k * bucket_rows:(k + 1) * bucket_rows] for k in range(len(parts))]


def backward_and_faces(field, arriving, back_ratio, count, cell, weight, slot, nodes, devices, owners):
    planes, width = field.shape[0], field.shape[2]
    face_rows = cell.shape[0]
    bucket_rows = nodes.shape[0]
    rows_each = bucket_rows // owners
    group = 2
    piece = 4
    batch = 8

    def kernel(count_ref, field_ref, near_ref, reach_ref, other_ref, back_ref, cell_ref, weight_ref,
               slot_ref, nodes_ref, adjoint_hbm, send_ref, adjoint_ref, parts_ref, value_ref, sems):
        def write(k):
            return pltpu.make_async_copy(adjoint_ref.at[pl.ds(k * batch, batch)],
                                         adjoint_hbm.at[pl.ds(k * batch, batch)], sems.at[k])

        def back(t, state):
            i = planes - 1 - t
            out = []
            for h, rows in enumerate(halves(width)):
                e = block(back_ref, i, rows)
                out.append([field_ref[i, c, rows, :] - dot5(e[c], state[h]) for c in range(5)])
            for h, rows in enumerate(halves(width)):
                for c in range(5):
                    adjoint_ref[i, c, rows, :] = out[h][c]
            for c in range(5):
                high, low = split(jnp.concatenate([o[c] for o in out], axis=0))
                at = pl.ds(pl.multiple_of((i * 5 + c) * width, width), width)
                parts_ref[at, :LANES] = high
                parts_ref[at, LANES:] = low
            return out

        state = last_join(near_ref, reach_ref, other_ref, True, width)
        for k in reversed(range(planes // batch)):
            first = planes - (k + 1) * batch
            state = lax.fori_loop(first, first + batch, back, state, unroll=4)
            write(k).start()

        lane_iota = lax.broadcasted_iota(jnp.int32, (LANES, LANES), 0).astype(F32).astype(BF16)
        sub8 = lax.broadcasted_iota(jnp.int32, (8, LANES), 0)

        def gather(g, carry):
            cells = [cell_ref[pl.ds(g * group + u, 1), :] for u in range(group)]
            hots, offs = [], []
            for at in cells:
                lanes = spread((at % LANES).astype(F32), LANES)
                hots.append(jnp.where(lane_iota == lanes, jnp.ones((LANES, LANES), BF16),
                                      jnp.zeros((LANES, LANES), BF16)))
                offs.append(jnp.broadcast_to(at // LANES, (8, LANES)) - sub8)
            hot = jnp.concatenate(hots, axis=1)
            hot = jnp.concatenate([hot, hot], axis=0)
            found = [[jnp.zeros((8, LANES), F32)] * 5 for _ in range(group)]
            for p in range(0, planes, piece):
                got = jnp.dot(parts_ref[p * 5 * width:(p + piece) * 5 * width, :], hot,
                              preferred_element_type=F32)
                for i in range(piece):
                    for h in range(width // 8):
                        for u in range(group):
                            mask = offs[u] == (p + i) * width + 8 * h
                            for c in range(5):
                                row = (i * 5 + c) * width + 8 * h
                                found[u][c] = jnp.where(mask, got[row:row + 8, u * LANES:(u + 1) * LANES],
                                                        found[u][c])
            weights = weight_ref[:, pl.ds(pl.multiple_of(g * (group * LANES), group * LANES), group * LANES)]
            for u in range(group):
                w = [jnp.broadcast_to(weights[c:c + 1, u * LANES:(u + 1) * LANES], (8, LANES)) for c in range(5)]
                value_ref[pl.ds(g * group + u, 1), :] = jnp.sum(dot5(w, found[u]), axis=0, keepdims=True)
            return carry

        lax.fori_loop(0, face_rows // group, gather, 0, unroll=4)
        live = lax.broadcasted_iota(jnp.int32, (face_rows, LANES), 0) * LANES + lax.broadcasted_iota(
            jnp.int32, (face_rows, LANES), 1) < count_ref[0]
        high, low = split(jnp.where(live, value_ref[...], 0.0))
        placed = place_in_slots(slot_ref[...], [high, low], bucket_rows)
        values = placed[0] + placed[1]
        for o in range(owners):
            here = slice(o * rows_each, (o + 1) * rows_each)
            both = jnp.concatenate([values[here], nodes_ref[here, :]], axis=0)
            for d in range(o, devices, owners):
                send_ref[d] = both
        for k in range(planes // batch):
            write(k).wait()

    return pl.pallas_call(
        kernel,
        out_shape=(
            jax.ShapeDtypeStruct(field.shape, F32),
            jax.ShapeDtypeStruct((devices, 2 * rows_each, LANES), F32),
        ),
        in_specs=[pl.BlockSpec(memory_space=pltpu.SMEM)] + vmem_specs(9),
        out_specs=(pl.BlockSpec(memory_space=pltpu.HBM), pl.BlockSpec(memory_space=VMEM)),
        scratch_shapes=[
            VMEM(field.shape, F32),
            VMEM((planes * 5 * width, 2 * LANES), BF16),
            VMEM((face_rows, LANES), F32),
            pltpu.SemaphoreType.DMA((planes // batch,)),
        ],
        compiler_params=pltpu.CompilerParams(vmem_limit_bytes=12 << 20),
        name="backward_and_faces",
    )(count, in_vmem(field), *[in_vmem(v) for v in arriving], in_vmem(back_ratio), in_vmem(cell),
      in_vmem(weight), in_vmem(slot), in_vmem(nodes))


def node_sums(got):
    devices, rows2, _ = got.shape
    rows_each = rows2 // 2
    side = NODES_DEV // LANES
    batch = min(devices, 128 // rows_each)

    def kernel(got_ref, out_ref):
        iota = lax.broadcasted_iota(jnp.int32, (LANES, LANES), 0).astype(F32).astype(BF16)
        side_iota = lax.broadcasted_iota(jnp.int32, (side, LANES), 0).astype(F32).astype(BF16)
        ones, zero = jnp.ones((LANES, LANES), BF16), jnp.zeros((LANES, LANES), BF16)
        side_zero = jnp.zeros((side, LANES), BF16)

        def body(t, total):
            lefts, rights = [], []
            for u in range(batch):
                d = t * batch + u
                for r in range(rows_each):
                    value = got_ref[d, r:r + 1, :]
                    node = got_ref[d, rows_each + r:rows_each + r + 1, :].astype(jnp.int32)
                    high = value.astype(BF16).astype(F32)
                    hot = side_iota == spread((node // LANES).astype(F32), side)
                    lefts.append(jnp.concatenate([
                        jnp.where(hot, spread(high, side), side_zero),
                        jnp.where(hot, spread(value - high, side), side_zero)], axis=0))
                    rights.append(jnp.where(iota == spread((node % LANES).astype(F32), LANES), ones, zero))
            return total + lax.dot_general(
                jnp.concatenate(lefts, axis=1), jnp.concatenate(rights, axis=1),
                (((1,), (1,)), ((), ())), preferred_element_type=F32)

        total = jnp.zeros((2 * side, LANES), F32)
        if batch == devices:
            total = body(0, total)
        else:
            total = lax.fori_loop(0, devices // batch, body, total)
        out_ref[...] = total[:side] + total[side:]

    return pl.pallas_call(
        kernel,
        out_shape=jax.ShapeDtypeStruct((side, LANES), F32),
        in_specs=vmem_specs(1),
        out_specs=pl.BlockSpec(memory_space=VMEM),
        compiler_params=pltpu.CompilerParams(vmem_limit_bytes=24 << 20),
        name="node_sums",
    )(in_vmem(got))


def comes_after(stage, backward):
    bit = lax.rem(lax.div(lax.axis_index("sweep"), 1 << stage), 2)
    return bit == (0 if backward else 1)


def matvec(matrix, vector):
    return [dot5(row, vector) for row in matrix]


def matmat(matrix, other):
    return [[dot5(row, [other[e][x] for e in range(5)]) for x in range(5)] for row in matrix]


def load_matrix(ref, rows):
    return [[ref[c, d, rows, :] for d in range(5)] for c in range(5)]


def load_vector(ref, rows):
    return [ref[c, rows, :] for c in range(5)]


def pick(flag, one, two):
    if isinstance(one, list):
        return [pick(flag, a, b) for a, b in zip(one, two)]
    return jnp.where(flag, one, two)


def last_join(near_ref, reach_ref, other_ref, backward, width):
    after = comes_after(lax.axis_size("sweep").bit_length() - 2, backward)
    start = []
    for rows in halves(width):
        near = load_vector(near_ref, rows)
        gain = matvec(load_matrix(reach_ref, rows), load_vector(other_ref, rows))
        start.append([n + jnp.where(after, g, 0.0) for n, g in zip(near, gain)])
    return start


def join(stage, backward, near, reach, leaving, total, other, other_total, carry_total):
    first = near is None
    width = leaving.shape[1]
    outs = [leaving.shape, total.shape, leaving.shape] + ([total.shape] if carry_total else [])

    def kernel(*refs):
        ins, out = refs[:len(operands)], refs[len(operands):]
        after = comes_after(stage, backward)
        for rows in halves(width):
            own, theirs = load_vector(ins[0], rows), load_vector(ins[2], rows)
            own_total, their_total = load_matrix(ins[1], rows), load_matrix(ins[3], rows)
            if first:
                entering = theirs
                through = their_total
                before = [jnp.zeros((8, LANES), F32)] * 5
                unit = [[jnp.full((8, LANES), 1.0 if c == d else 0.0, F32) for d in range(5)] for c in range(5)]
            else:
                before, unit = load_vector(ins[4], rows), load_matrix(ins[5], rows)
                entering = [a + b for a, b in zip(before, matvec(unit, theirs))]
                through = matmat(unit, their_total)
            entering, through = pick(after, entering, before), pick(after, through, unit)
            downstream = pick(after, own_total, their_total)
            sent = matvec(downstream, pick(after, theirs, own))
            sent = [a + b for a, b in zip(pick(after, own, theirs), sent)]
            for c in range(5):
                out[0][c, rows, :] = entering[c]
                out[2][c, rows, :] = sent[c]
                for d in range(5):
                    out[1][c, d, rows, :] = through[c][d]
            if carry_total:
                whole = matmat(downstream, pick(after, their_total, own_total))
                for c in range(5):
                    for d in range(5):
                        out[3][c, d, rows, :] = whole[c][d]

    operands = [leaving, total, other, other_total] + ([] if first else [near, reach])
    return pl.pallas_call(
        kernel,
        out_shape=tuple(jax.ShapeDtypeStruct(shape, F32) for shape in outs),
        in_specs=vmem_specs(len(operands)),
        out_specs=tuple(vmem_specs(len(outs))),
        compiler_params=pltpu.CompilerParams(vmem_limit_bytes=4 << 20),
        name="join",
    )(*[in_vmem(v) for v in operands])


def relay(total, leaving, backward):
    size = lax.axis_size("sweep")
    stages = size.bit_length() - 1
    near = reach = None
    for stage in range(stages):
        pairs = [(i, i ^ (1 << stage)) for i in range(size)]
        other = lax.ppermute(leaving, "sweep", pairs)
        if stage == stages - 1:
            return (near, reach, other), leaving
        other_total = lax.ppermute(total, "sweep", pairs)
        carry_total = stage + 2 < stages
        joined = join(stage, backward, near, reach, leaving, total, other, other_total, carry_total)
        near, reach, leaving = joined[:3]
        if carry_total:
            total = joined[3]


def per_device(source, psi_old, lateral, lower_jac, upper_jac, diag_inv, face_weight, face_cell,
               face_owner, face_node, face_count):
    bulk = lax.axis_size("bulk")
    devices = bulk * lax.axis_size("sweep")
    low_pairs = [(i, i ^ 1) for i in range(bulk) if i ^ 1 < bulk]
    high_pairs = [(i, j) for i in range(bulk) for j in [i + 1 if i % 2 else i - 1] if 0 <= j < bulk]
    low_edge, high_edge = edge_rows(psi_old)
    low_edge, high_edge, lower_jac = lax.optimization_barrier((low_edge, high_edge, lower_jac))
    first = lax.ppermute(low_edge, "bulk", low_pairs)
    second = lax.ppermute(high_edge, "bulk", high_pairs)

    ratio, total = matrices(lower_jac, diag_inv, False, "forward_matrices")
    scaled, leaving = forward_local(source, psi_old, lateral, first, second, ratio, diag_inv)
    total, leaving = lax.optimization_barrier((total, leaving))
    arriving, joined = relay(total, leaving, False)
    upper_jac, joined = lax.optimization_barrier((upper_jac, joined))
    back_ratio, back_total = matrices(upper_jac, diag_inv, True, "backward_matrices")
    field, leaving = forward_then_back(scaled, arriving, ratio, back_ratio)
    back_total, leaving = lax.optimization_barrier((back_total, leaving))
    arriving, _ = relay(back_total, leaving, True)

    slots = face_cell.shape[0]
    rows = (slots // LANES, LANES)
    slot, nodes = face_slots(face_owner.reshape(rows), face_node.reshape(rows), bulk)
    adjoint, send = backward_and_faces(field, arriving, back_ratio, face_count, face_cell.reshape(rows),
                                       face_weight, slot, nodes, devices, bulk)
    got = lax.all_to_all(send, ("sweep", "bulk"), 0, 0, tiled=True)
    return adjoint, node_sums(got).reshape(NODES_DEV)


def solution(mesh):
    placed = (
        P("sweep", None, "bulk", None),
        P("sweep", None, "bulk", None),
        P("sweep", None, "bulk", None),
        P("sweep", None, None, "bulk", None),
        P("sweep", None, None, "bulk", None),
        P("sweep", None, None, "bulk", None),
        P(None, ("sweep", "bulk")),
        P(("sweep", "bulk")),
        P(("sweep", "bulk"), None),
        P(("sweep", "bulk")),
        P(("sweep", "bulk")),
    )
    return jax.shard_map(
        per_device,
        mesh=mesh,
        in_specs=placed,
        out_specs=(P("sweep", None, "bulk", None), P("bulk")),
        check_vma=False,
    )
```

```python
import jax
import jax.numpy as jnp
from jax import lax
from jax.experimental import pallas as pl
from jax.experimental.pallas import tpu as pltpu
from jax.sharding import PartitionSpec as P

NODES_DEV = 16384
LANES = 128
F32 = jnp.float32
BF16 = jnp.bfloat16
VMEM = pltpu.VMEM


def dot5(a, b):
    p = [x * y for x, y in zip(a, b)]
    return ((p[0] + p[1]) + (p[2] + p[3])) + p[4]


def block(ref, at, rows):
    return [[ref[at, c, d, rows, :] for d in range(5)] for c in range(5)]


def halves(width):
    return [pl.ds(8 * h, 8) for h in range(width // 8)]


def in_vmem(value):
    return pltpu.with_memory_space_constraint(value, VMEM)


def in_hbm(value):
    return pltpu.with_memory_space_constraint(value, pltpu.HBM)


def vmem_specs(n):
    return [pl.BlockSpec(memory_space=VMEM)] * n


def ratio_of(coupled, inv, at, rows):
    j = block(coupled, at, rows)
    d = block(inv, at, rows)
    return [[dot5(d[c], [j[e][x] for e in range(5)]) for x in range(5)] for c in range(5)]


def next_total(ratio, total_ref, rows):
    old = [[total_ref[e, x, rows, :] for x in range(5)] for e in range(5)]
    return [[dot5(ratio[c], [old[e][x] for e in range(5)]) for x in range(5)] for c in range(5)]


def keep_matrices(ratio, total, ratio_ref, total_ref, at, rows):
    for c in range(5):
        for x in range(5):
            ratio_ref[at, c, x, rows, :] = ratio[c][x]
            total_ref[c, x, rows, :] = total[c][x]


def keep_map(map_ref, total_ref, leaving, width):
    map_ref[:5] = total_ref[...]
    for h, rows in enumerate(halves(width)):
        for c in range(5):
            map_ref[5, c, rows, :] = leaving[h][c]


def set_identity(total_ref, planes):
    sign = 1.0 if planes % 2 == 0 else -1.0
    for c in range(5):
        for d in range(5):
            total_ref[c, d] = jnp.full(total_ref.shape[2:], sign if c == d else 0.0, F32)


def edge_rows(psi):
    planes, fields, width, _ = psi.shape
    shape = (fields * planes, LANES)

    def kernel(psi_hbm, low_ref, high_ref, head_ref, tail_ref, sems):
        copies = []
        for c in range(fields):
            rows = pl.ds(c * planes, planes)
            copies.append(pltpu.make_async_copy(psi_hbm.at[:, c, 0, :], head_ref.at[rows], sems.at[0, c]))
            copies.append(pltpu.make_async_copy(psi_hbm.at[:, c, width - 1, :], tail_ref.at[rows], sems.at[1, c]))
        for copy in copies:
            copy.start()
        is_odd = lax.rem(lax.axis_index("bulk"), 2) == 1
        for copy in copies:
            copy.wait()
        head, tail = head_ref[...], tail_ref[...]
        low_ref[...] = jnp.where(is_odd, head, tail)
        high_ref[...] = jnp.where(is_odd, tail, head)

    return pl.pallas_call(
        kernel,
        out_shape=(jax.ShapeDtypeStruct(shape, F32), jax.ShapeDtypeStruct(shape, F32)),
        in_specs=[pl.BlockSpec(memory_space=pltpu.HBM)],
        out_specs=tuple(vmem_specs(2)),
        scratch_shapes=[VMEM(shape, F32), VMEM(shape, F32), pltpu.SemaphoreType.DMA((2, fields))],
        compiler_params=pltpu.CompilerParams(vmem_limit_bytes=4 << 20),
        cost_estimate=pl.CostEstimate(flops=10_000_000_000, bytes_accessed=20_000_000, transcendentals=0),
        name="edge_rows",
    )(in_hbm(psi))


def forward_local(source, psi, lateral, first, second, ratio, inv, total):
    planes, width = source.shape[0], source.shape[2]

    def kernel(source_ref, psi_ref, lateral_ref, first_ref, second_ref, ratio_ref, inv_ref, total_ref,
               scaled_ref, map_ref):
        is_odd = lax.rem(lax.axis_index("bulk"), 2) == 1

        def body(i, state):
            below, above = lateral_ref[i, 0], lateral_ref[i, 1]
            right = []
            for c in range(5):
                one = first_ref[pl.ds(c * planes + i, 1), :]
                two = second_ref[pl.ds(c * planes + i, 1), :]
                here = psi_ref[i, c]
                down = jnp.concatenate([jnp.where(is_odd, one, two), here[:width - 1]], axis=0)
                up = jnp.concatenate([here[1:], jnp.where(is_odd, two, one)], axis=0)
                right.append(source_ref[i, c] - below * down - above * up)
            out = []
            for h, rows in enumerate(halves(width)):
                r = [v[8 * h:8 * h + 8] for v in right]
                d = block(inv_ref, i, rows)
                e = block(ratio_ref, i, rows)
                g = [dot5(d[c], r) for c in range(5)]
                out.append((g, [g[c] - dot5(e[c], state[h]) for c in range(5)]))
            for h, rows in enumerate(halves(width)):
                for c in range(5):
                    scaled_ref[i, c, rows, :] = out[h][0][c]
            return [f for _, f in out]

        zero = [[jnp.zeros((8, LANES), F32)] * 5 for _ in halves(width)]
        state = lax.fori_loop(0, planes, body, zero, unroll=2)
        keep_map(map_ref, total_ref, state, width)

    return pl.pallas_call(
        kernel,
        out_shape=(VMEM(source.shape, F32), jax.ShapeDtypeStruct((6,) + source.shape[1:], F32)),
        in_specs=vmem_specs(8),
        out_specs=tuple(vmem_specs(2)),
        compiler_params=pltpu.CompilerParams(vmem_limit_bytes=4 << 20),
        name="forward_local",
    )(*[in_vmem(v) for v in (source, psi, lateral, first, second, ratio, inv, total)])


def matrices(coupled, inv, backward, name):
    planes, width = coupled.shape[0], coupled.shape[3]

    def kernel(coupled_ref, inv_ref, ratio_ref, total_ref):
        set_identity(total_ref, planes)

        def body(t, carry):
            at = planes - 1 - t if backward else t
            for rows in halves(width):
                ratio = ratio_of(coupled_ref, inv_ref, at, rows)
                keep_matrices(ratio, next_total(ratio, total_ref, rows), ratio_ref, total_ref, at, rows)
            return carry

        lax.fori_loop(0, planes, body, 0, unroll=2)

    return pl.pallas_call(
        kernel,
        out_shape=(VMEM(coupled.shape, F32), jax.ShapeDtypeStruct(coupled.shape[1:], F32)),
        in_specs=vmem_specs(2),
        out_specs=tuple(vmem_specs(2)),
        compiler_params=pltpu.CompilerParams(vmem_limit_bytes=4 << 20),
        cost_estimate=pl.CostEstimate(flops=5_000_000_000, bytes_accessed=20_000_000, transcendentals=0),
        name=name,
    )(in_vmem(coupled), in_vmem(inv))


def forward_then_back(scaled, arriving, ratio, back_ratio, back_total):
    planes, width = scaled.shape[0], scaled.shape[2]

    def kernel(scaled_ref, near_ref, reach_ref, other_ref, ratio_ref, back_ref, total_ref,
               field_ref, map_ref):
        def ahead(i, state):
            out = []
            for h, rows in enumerate(halves(width)):
                e = block(ratio_ref, i, rows)
                out.append([scaled_ref[i, c, rows, :] - dot5(e[c], state[h]) for c in range(5)])
            for h, rows in enumerate(halves(width)):
                for c in range(5):
                    field_ref[i, c, rows, :] = out[h][c]
            return out

        start = last_join(near_ref, reach_ref, other_ref, False, width)
        lax.fori_loop(0, planes, ahead, start, unroll=4)

        def back(t, state):
            i = planes - 1 - t
            out = []
            for h, rows in enumerate(halves(width)):
                e = block(back_ref, i, rows)
                out.append([field_ref[i, c, rows, :] - dot5(e[c], state[h]) for c in range(5)])
            return out

        zero = [[jnp.zeros((8, LANES), F32)] * 5 for _ in halves(width)]
        state = lax.fori_loop(0, planes, back, zero, unroll=4)
        keep_map(map_ref, total_ref, state, width)

    return pl.pallas_call(
        kernel,
        out_shape=(VMEM(scaled.shape, F32), jax.ShapeDtypeStruct((6,) + scaled.shape[1:], F32)),
        in_specs=vmem_specs(7),
        out_specs=tuple(vmem_specs(2)),
        compiler_params=pltpu.CompilerParams(vmem_limit_bytes=4 << 20),
        name="forward_then_back",
    )(*[in_vmem(v) for v in (scaled, *arriving, ratio, back_ratio, back_total)])


def face_slots(owner, node, owners):
    face_rows = owner.shape[0]
    cap = 2 * face_rows * LANES // owners
    bucket_rows = 2 * face_rows

    def kernel(owner_ref, node_ref, slot_ref, nodes_ref):
        sub = lax.broadcasted_iota(jnp.int32, (LANES, LANES), 0)
        lane = lax.broadcasted_iota(jnp.int32, (LANES, LANES), 1)
        strict = (sub < lane).astype(F32).astype(BF16)
        ones = jnp.ones((LANES, LANES), BF16)
        fs = lax.broadcasted_iota(jnp.int32, (face_rows, face_rows), 0)
        fl = lax.broadcasted_iota(jnp.int32, (face_rows, face_rows), 1)
        lower = (fl < fs).astype(F32).astype(BF16)
        own = owner_ref[...]
        masks = [(own == o).astype(F32) for o in range(owners)]
        stacked = jnp.concatenate(masks, axis=0).astype(BF16)
        before = jnp.dot(stacked, strict, preferred_element_type=F32)
        totals = jnp.dot(stacked, ones, preferred_element_type=F32).astype(BF16)
        rank = jnp.zeros((face_rows, LANES), F32)
        for o in range(owners):
            here = slice(o * face_rows, (o + 1) * face_rows)
            offset = jnp.dot(lower, totals[here], preferred_element_type=F32)
            rank = rank + masks[o] * (before[here] + offset + float(o * cap))
        slot = rank.astype(jnp.int32)
        slot_ref[...] = slot
        nodes = node_ref[...]
        high = (nodes // LANES).astype(F32)
        low = (nodes % LANES).astype(F32)
        parts = place_in_slots(slot, [high, low], bucket_rows)
        nodes_ref[...] = float(LANES) * parts[0] + parts[1]

    return pl.pallas_call(
        kernel,
        out_shape=(VMEM((face_rows, LANES), jnp.int32), VMEM((bucket_rows, LANES), F32)),
        in_specs=vmem_specs(2),
        out_specs=tuple(vmem_specs(2)),
        compiler_params=pltpu.CompilerParams(vmem_limit_bytes=4 << 20),
        cost_estimate=pl.CostEstimate(flops=4_000_000, bytes_accessed=10_000_000, transcendentals=0),
        name="face_slots",
    )(in_vmem(owner), in_vmem(node))


def spread(row, rows):
    tile = jnp.broadcast_to(row, (16, LANES)).astype(BF16)
    return jnp.concatenate([tile] * (rows // 16), axis=0)


def split(value):
    high = value.astype(BF16)
    return high, (value - high.astype(F32)).astype(BF16)


def place_in_slots(slot, parts, bucket_rows):
    face_rows = slot.shape[0]
    high = (slot // LANES).astype(F32)
    low = (slot % LANES).astype(F32)
    parts = [p.astype(F32) for p in parts]
    high_iota = lax.broadcasted_iota(jnp.int32, (bucket_rows, LANES), 0).astype(F32).astype(BF16)
    low_iota = lax.broadcasted_iota(jnp.int32, (LANES, LANES), 0).astype(F32).astype(BF16)
    ones, none = jnp.ones((LANES, LANES), BF16), jnp.zeros((LANES, LANES), BF16)
    zero = jnp.zeros((bucket_rows, LANES), BF16)
    lefts, rights = [], []
    for f in range(face_rows):
        row = slice(f, f + 1)
        hot = high_iota == spread(high[row], bucket_rows)
        lefts.append(jnp.concatenate(
            [jnp.where(hot, spread(p[row], bucket_rows), zero) for p in parts], axis=0))
        rights.append(jnp.where(low_iota == spread(low[row], LANES), ones, none))
    out = lax.dot_general(jnp.concatenate(lefts, axis=1), jnp.concatenate(rights, axis=1),
                          (((1,), (1,)), ((), ())), preferred_element_type=F32)
    return [out[k * bucket_rows:(k + 1) * bucket_rows] for k in range(len(parts))]


def backward_and_faces(field, arriving, back_ratio, count, cell, weight, slot, nodes, devices, owners):
    planes, width = field.shape[0], field.shape[2]
    face_rows = cell.shape[0]
    bucket_rows = nodes.shape[0]
    rows_each = bucket_rows // owners
    group = 2
    piece = 4
    batch = 8

    def kernel(count_ref, field_ref, near_ref, reach_ref, other_ref, back_ref, cell_ref, weight_ref,
               slot_ref, nodes_ref, adjoint_hbm, send_ref, adjoint_ref, parts_ref, value_ref, sems):
        def write(k):
            return pltpu.make_async_copy(adjoint_ref.at[pl.ds(k * batch, batch)],
                                         adjoint_hbm.at[pl.ds(k * batch, batch)], sems.at[k])

        def back(t, state):
            i = planes - 1 - t
            out = []
            for h, rows in enumerate(halves(width)):
                e = block(back_ref, i, rows)
                out.append([field_ref[i, c, rows, :] - dot5(e[c], state[h]) for c in range(5)])
            for h, rows in enumerate(halves(width)):
                for c in range(5):
                    adjoint_ref[i, c, rows, :] = out[h][c]
            for c in range(5):
                high, low = split(jnp.concatenate([o[c] for o in out], axis=0))
                at = pl.ds(pl.multiple_of((i * 5 + c) * width, width), width)
                parts_ref[at, :LANES] = high
                parts_ref[at, LANES:] = low
            return out

        state = last_join(near_ref, reach_ref, other_ref, True, width)
        for k in reversed(range(planes // batch)):
            first = planes - (k + 1) * batch
            state = lax.fori_loop(first, first + batch, back, state, unroll=4)
            write(k).start()

        lane_iota = lax.broadcasted_iota(jnp.int32, (LANES, LANES), 0).astype(F32).astype(BF16)
        sub8 = lax.broadcasted_iota(jnp.int32, (8, LANES), 0)

        def gather(g, carry):
            cells = [cell_ref[pl.ds(g * group + u, 1), :] for u in range(group)]
            hots, offs = [], []
            for at in cells:
                lanes = spread((at % LANES).astype(F32), LANES)
                hots.append(jnp.where(lane_iota == lanes, jnp.ones((LANES, LANES), BF16),
                                      jnp.zeros((LANES, LANES), BF16)))
                offs.append(jnp.broadcast_to(at // LANES, (8, LANES)) - sub8)
            hot = jnp.concatenate(hots, axis=1)
            hot = jnp.concatenate([hot, hot], axis=0)
            found = [[jnp.zeros((8, LANES), F32)] * 5 for _ in range(group)]
            for p in range(0, planes, piece):
                got = jnp.dot(parts_ref[p * 5 * width:(p + piece) * 5 * width, :], hot,
                              preferred_element_type=F32)
                for i in range(piece):
                    for h in range(width // 8):
                        for u in range(group):
                            mask = offs[u] == (p + i) * width + 8 * h
                            for c in range(5):
                                row = (i * 5 + c) * width + 8 * h
                                found[u][c] = jnp.where(mask, got[row:row + 8, u * LANES:(u + 1) * LANES],
                                                        found[u][c])
            weights = weight_ref[:, pl.ds(pl.multiple_of(g * (group * LANES), group * LANES), group * LANES)]
            for u in range(group):
                w = [jnp.broadcast_to(weights[c:c + 1, u * LANES:(u + 1) * LANES], (8, LANES)) for c in range(5)]
                value_ref[pl.ds(g * group + u, 1), :] = jnp.sum(dot5(w, found[u]), axis=0, keepdims=True)
            return carry

        lax.fori_loop(0, face_rows // group, gather, 0, unroll=4)
        live = lax.broadcasted_iota(jnp.int32, (face_rows, LANES), 0) * LANES + lax.broadcasted_iota(
            jnp.int32, (face_rows, LANES), 1) < count_ref[0]
        high, low = split(jnp.where(live, value_ref[...], 0.0))
        placed = place_in_slots(slot_ref[...], [high, low], bucket_rows)
        values = placed[0] + placed[1]
        for o in range(owners):
            here = slice(o * rows_each, (o + 1) * rows_each)
            both = jnp.concatenate([values[here], nodes_ref[here, :]], axis=0)
            for d in range(o, devices, owners):
                send_ref[d] = both
        for k in range(planes // batch):
            write(k).wait()

    return pl.pallas_call(
        kernel,
        out_shape=(
            jax.ShapeDtypeStruct(field.shape, F32),
            jax.ShapeDtypeStruct((devices, 2 * rows_each, LANES), F32),
        ),
        in_specs=[pl.BlockSpec(memory_space=pltpu.SMEM)] + vmem_specs(9),
        out_specs=(pl.BlockSpec(memory_space=pltpu.HBM), pl.BlockSpec(memory_space=VMEM)),
        scratch_shapes=[
            VMEM(field.shape, F32),
            VMEM((planes * 5 * width, 2 * LANES), BF16),
            VMEM((face_rows, LANES), F32),
            pltpu.SemaphoreType.DMA((planes // batch,)),
        ],
        compiler_params=pltpu.CompilerParams(vmem_limit_bytes=12 << 20),
        name="backward_and_faces",
    )(count, in_vmem(field), *[in_vmem(v) for v in arriving], in_vmem(back_ratio), in_vmem(cell),
      in_vmem(weight), in_vmem(slot), in_vmem(nodes))


def node_sums(got):
    devices, rows2, _ = got.shape
    rows_each = rows2 // 2
    side = NODES_DEV // LANES
    batch = min(devices, 128 // rows_each)

    def kernel(got_ref, out_ref):
        iota = lax.broadcasted_iota(jnp.int32, (LANES, LANES), 0).astype(F32).astype(BF16)
        side_iota = lax.broadcasted_iota(jnp.int32, (side, LANES), 0).astype(F32).astype(BF16)
        ones, zero = jnp.ones((LANES, LANES), BF16), jnp.zeros((LANES, LANES), BF16)
        side_zero = jnp.zeros((side, LANES), BF16)

        def body(t, total):
            lefts, rights = [], []
            for u in range(batch):
                d = t * batch + u
                for r in range(rows_each):
                    value = got_ref[d, r:r + 1, :]
                    node = got_ref[d, rows_each + r:rows_each + r + 1, :].astype(jnp.int32)
                    high = value.astype(BF16).astype(F32)
                    hot = side_iota == spread((node // LANES).astype(F32), side)
                    lefts.append(jnp.concatenate([
                        jnp.where(hot, spread(high, side), side_zero),
                        jnp.where(hot, spread(value - high, side), side_zero)], axis=0))
                    rights.append(jnp.where(iota == spread((node % LANES).astype(F32), LANES), ones, zero))
            return total + lax.dot_general(
                jnp.concatenate(lefts, axis=1), jnp.concatenate(rights, axis=1),
                (((1,), (1,)), ((), ())), preferred_element_type=F32)

        total = jnp.zeros((2 * side, LANES), F32)
        if batch == devices:
            total = body(0, total)
        else:
            total = lax.fori_loop(0, devices // batch, body, total)
        out_ref[...] = total[:side] + total[side:]

    return pl.pallas_call(
        kernel,
        out_shape=jax.ShapeDtypeStruct((side, LANES), F32),
        in_specs=vmem_specs(1),
        out_specs=pl.BlockSpec(memory_space=VMEM),
        compiler_params=pltpu.CompilerParams(vmem_limit_bytes=24 << 20),
        name="node_sums",
    )(in_vmem(got))


def comes_after(stage, backward):
    bit = lax.rem(lax.div(lax.axis_index("sweep"), 1 << stage), 2)
    return bit == (0 if backward else 1)


def matvec(matrix, vector):
    return [dot5(row, vector) for row in matrix]


def matmat(matrix, other):
    return [[dot5(row, [other[e][x] for e in range(5)]) for x in range(5)] for row in matrix]


def load_matrix(ref, rows):
    return [[ref[c, d, rows, :] for d in range(5)] for c in range(5)]


def load_vector(ref, rows):
    return [ref[c, rows, :] for c in range(5)]


def pick(flag, one, two):
    if isinstance(one, list):
        return [pick(flag, a, b) for a, b in zip(one, two)]
    return jnp.where(flag, one, two)


def last_join(near_ref, reach_ref, other_ref, backward, width):
    after = comes_after(lax.axis_size("sweep").bit_length() - 2, backward)
    start = []
    for rows in halves(width):
        near = load_vector(near_ref, rows)
        gain = matvec(load_matrix(reach_ref, rows), load_vector(other_ref, rows))
        start.append([n + jnp.where(after, g, 0.0) for n, g in zip(near, gain)])
    return start


def join(stage, backward, near, reach, own, other, whole):
    first = near is None
    _, _, width, _ = own.shape
    vector = own.shape[1:]
    outs = [vector, (5,) + vector, own.shape if whole else vector]
    operands = [own, other] + ([] if first else [near, reach])

    def kernel(*refs):
        ins, out = refs[:len(operands)], refs[len(operands):]
        after = comes_after(stage, backward)
        for rows in halves(width):
            mine, theirs = load_vector(ins[0].at[5], rows), load_vector(ins[1].at[5], rows)
            my_total, their_total = load_matrix(ins[0], rows), load_matrix(ins[1], rows)
            if first:
                entering = theirs
                through = their_total
                before = [jnp.zeros((8, LANES), F32)] * 5
                unit = [[jnp.full((8, LANES), 1.0 if c == d else 0.0, F32) for d in range(5)] for c in range(5)]
            else:
                before, unit = load_vector(ins[2], rows), load_matrix(ins[3], rows)
                entering = [a + b for a, b in zip(before, matvec(unit, theirs))]
                through = matmat(unit, their_total)
            entering, through = pick(after, entering, before), pick(after, through, unit)
            downstream = pick(after, my_total, their_total)
            sent = matvec(downstream, pick(after, theirs, mine))
            sent = [a + b for a, b in zip(pick(after, mine, theirs), sent)]
            sent_ref = out[2].at[5] if whole else out[2]
            for c in range(5):
                out[0][c, rows, :] = entering[c]
                sent_ref[c, rows, :] = sent[c]
                for d in range(5):
                    out[1][c, d, rows, :] = through[c][d]
            if whole:
                product = matmat(downstream, pick(after, their_total, my_total))
                for c in range(5):
                    for d in range(5):
                        out[2][c, d, rows, :] = product[c][d]

    return pl.pallas_call(
        kernel,
        out_shape=tuple(jax.ShapeDtypeStruct(shape, F32) for shape in outs),
        in_specs=vmem_specs(len(operands)),
        out_specs=tuple(vmem_specs(3)),
        compiler_params=pltpu.CompilerParams(vmem_limit_bytes=4 << 20),
        name="join",
    )(*[in_vmem(v) for v in operands])


def relay(own, backward):
    size = lax.axis_size("sweep")
    stages = size.bit_length() - 1
    near = reach = None
    for stage in range(stages):
        pairs = [(i, i ^ (1 << stage)) for i in range(size)]
        other = lax.ppermute(own, "sweep", pairs)
        if stage == stages - 1:
            return (near, reach, other), own
        near, reach, own = join(stage, backward, near, reach, own, other, stage + 2 < stages)


def per_device(source, psi_old, lateral, lower_jac, upper_jac, diag_inv, face_weight, face_cell,
               face_owner, face_node, face_count):
    bulk = lax.axis_size("bulk")
    devices = bulk * lax.axis_size("sweep")
    low_pairs = [(i, i ^ 1) for i in range(bulk) if i ^ 1 < bulk]
    high_pairs = [(i, j) for i in range(bulk) for j in [i + 1 if i % 2 else i - 1] if 0 <= j < bulk]
    low_edge, high_edge = edge_rows(psi_old)
    low_edge, high_edge, lower_jac = lax.optimization_barrier((low_edge, high_edge, lower_jac))
    first = lax.ppermute(low_edge, "bulk", low_pairs)
    second = lax.ppermute(high_edge, "bulk", high_pairs)

    ratio, total = matrices(lower_jac, diag_inv, False, "forward_matrices")
    scaled, own = forward_local(source, psi_old, lateral, first, second, ratio, diag_inv, total)
    arriving, joined = relay(own, False)
    upper_jac, joined = lax.optimization_barrier((upper_jac, joined))
    back_ratio, back_total = matrices(upper_jac, diag_inv, True, "backward_matrices")
    field, own = forward_then_back(scaled, arriving, ratio, back_ratio, back_total)
    arriving, _ = relay(own, True)

    slots = face_cell.shape[0]
    rows = (slots // LANES, LANES)
    slot, nodes = face_slots(face_owner.reshape(rows), face_node.reshape(rows), bulk)
    adjoint, send = backward_and_faces(field, arriving, back_ratio, face_count, face_cell.reshape(rows),
                                       face_weight, slot, nodes, devices, bulk)
    got = lax.all_to_all(send, ("sweep", "bulk"), 0, 0, tiled=True)
    return adjoint, node_sums(got).reshape(NODES_DEV)


def solution(mesh):
    placed = (
        P("sweep", None, "bulk", None),
        P("sweep", None, "bulk", None),
        P("sweep", None, "bulk", None),
        P("sweep", None, None, "bulk", None),
        P("sweep", None, None, "bulk", None),
        P("sweep", None, None, "bulk", None),
        P(None, ("sweep", "bulk")),
        P(("sweep", "bulk")),
        P(("sweep", "bulk"), None),
        P(("sweep", "bulk")),
        P(("sweep", "bulk")),
    )
    return jax.shard_map(
        per_device,
        mesh=mesh,
        in_specs=placed,
        out_specs=(P("sweep", None, "bulk", None), P("bulk")),
        check_vma=False,
    )
```

```python
import jax
import jax.numpy as jnp
from jax import lax
from jax.experimental import pallas as pl
from jax.experimental.pallas import tpu as pltpu
from jax.sharding import PartitionSpec as P

NODES_DEV = 16384
LANES = 128
F32 = jnp.float32
BF16 = jnp.bfloat16
VMEM = pltpu.VMEM


def dot5(a, b):
    p = [x * y for x, y in zip(a, b)]
    return ((p[0] + p[1]) + (p[2] + p[3])) + p[4]


def block(ref, at, rows):
    return [[ref[at, c, d, rows, :] for d in range(5)] for c in range(5)]


def halves(width):
    return [pl.ds(8 * h, 8) for h in range(width // 8)]


def in_vmem(value):
    return pltpu.with_memory_space_constraint(value, VMEM)


def in_hbm(value):
    return pltpu.with_memory_space_constraint(value, pltpu.HBM)


def vmem_specs(n):
    return [pl.BlockSpec(memory_space=VMEM)] * n


def ratio_of(coupled, inv, at, rows):
    j = block(coupled, at, rows)
    d = block(inv, at, rows)
    return [[dot5(d[c], [j[e][x] for e in range(5)]) for x in range(5)] for c in range(5)]


def next_total(ratio, total_ref, rows):
    old = [[total_ref[e, x, rows, :] for x in range(5)] for e in range(5)]
    return [[dot5(ratio[c], [old[e][x] for e in range(5)]) for x in range(5)] for c in range(5)]


def keep_matrices(ratio, total, ratio_ref, total_ref, at, rows):
    for c in range(5):
        for x in range(5):
            ratio_ref[at, c, x, rows, :] = ratio[c][x]
            total_ref[c, x, rows, :] = total[c][x]


def keep_map(map_ref, total_ref, leaving, width):
    map_ref[:5] = total_ref[...]
    for h, rows in enumerate(halves(width)):
        for c in range(5):
            map_ref[5, c, rows, :] = leaving[h][c]


def set_identity(total_ref, planes):
    sign = 1.0 if planes % 2 == 0 else -1.0
    for c in range(5):
        for d in range(5):
            total_ref[c, d] = jnp.full(total_ref.shape[2:], sign if c == d else 0.0, F32)


def edge_rows(psi):
    planes, fields, width, _ = psi.shape
    shape = (fields * planes, LANES)

    def kernel(psi_hbm, low_ref, high_ref, head_ref, tail_ref, sems):
        copies = []
        for c in range(fields):
            rows = pl.ds(c * planes, planes)
            copies.append(pltpu.make_async_copy(psi_hbm.at[:, c, 0, :], head_ref.at[rows], sems.at[0, c]))
            copies.append(pltpu.make_async_copy(psi_hbm.at[:, c, width - 1, :], tail_ref.at[rows], sems.at[1, c]))
        for copy in copies:
            copy.start()
        is_odd = lax.rem(lax.axis_index("bulk"), 2) == 1
        for copy in copies:
            copy.wait()
        head, tail = head_ref[...], tail_ref[...]
        low_ref[...] = jnp.where(is_odd, head, tail)
        high_ref[...] = jnp.where(is_odd, tail, head)

    return pl.pallas_call(
        kernel,
        out_shape=(jax.ShapeDtypeStruct(shape, F32), jax.ShapeDtypeStruct(shape, F32)),
        in_specs=[pl.BlockSpec(memory_space=pltpu.HBM)],
        out_specs=tuple(vmem_specs(2)),
        scratch_shapes=[VMEM(shape, F32), VMEM(shape, F32), pltpu.SemaphoreType.DMA((2, fields))],
        compiler_params=pltpu.CompilerParams(vmem_limit_bytes=4 << 20),
        cost_estimate=pl.CostEstimate(flops=10_000_000_000, bytes_accessed=20_000_000, transcendentals=0),
        name="edge_rows",
    )(in_hbm(psi))


def forward_local(source, psi, lateral, second, first, ratio, inv, total):
    planes, width = source.shape[0], source.shape[2]

    def kernel(source_ref, psi_ref, lateral_ref, second_ref, first_ref, ratio_ref, inv_ref, total_ref,
               scaled_ref, map_ref):
        is_odd = lax.rem(lax.axis_index("bulk"), 2) == 1

        def body(i, state):
            below, above = lateral_ref[i, 0], lateral_ref[i, 1]
            right = []
            for c in range(5):
                one = first_ref[pl.ds(c * planes + i, 1), :]
                two = second_ref[pl.ds(c * planes + i, 1), :]
                here = psi_ref[i, c]
                down = jnp.concatenate([jnp.where(is_odd, one, two), here[:width - 1]], axis=0)
                up = jnp.concatenate([here[1:], jnp.where(is_odd, two, one)], axis=0)
                right.append(source_ref[i, c] - below * down - above * up)
            out = []
            for h, rows in enumerate(halves(width)):
                r = [v[8 * h:8 * h + 8] for v in right]
                d = block(inv_ref, i, rows)
                e = block(ratio_ref, i, rows)
                g = [dot5(d[c], r) for c in range(5)]
                out.append((g, [g[c] - dot5(e[c], state[h]) for c in range(5)]))
            for h, rows in enumerate(halves(width)):
                for c in range(5):
                    scaled_ref[i, c, rows, :] = out[h][0][c]
            return [f for _, f in out]

        zero = [[jnp.zeros((8, LANES), F32)] * 5 for _ in halves(width)]
        state = lax.fori_loop(0, planes, body, zero, unroll=2)
        keep_map(map_ref, total_ref, state, width)

    return pl.pallas_call(
        kernel,
        out_shape=(VMEM(source.shape, F32), jax.ShapeDtypeStruct((6,) + source.shape[1:], F32)),
        in_specs=vmem_specs(8),
        out_specs=tuple(vmem_specs(2)),
        compiler_params=pltpu.CompilerParams(vmem_limit_bytes=4 << 20),
        name="forward_local",
    )(*[in_vmem(v) for v in (source, psi, lateral, second, first, ratio, inv, total)])


def matrices(coupled, inv, backward, name):
    planes, width = coupled.shape[0], coupled.shape[3]

    def kernel(coupled_ref, inv_ref, ratio_ref, total_ref):
        set_identity(total_ref, planes)

        def body(t, carry):
            at = planes - 1 - t if backward else t
            for rows in halves(width):
                ratio = ratio_of(coupled_ref, inv_ref, at, rows)
                keep_matrices(ratio, next_total(ratio, total_ref, rows), ratio_ref, total_ref, at, rows)
            return carry

        lax.fori_loop(0, planes, body, 0, unroll=2)

    return pl.pallas_call(
        kernel,
        out_shape=(VMEM(coupled.shape, F32), jax.ShapeDtypeStruct(coupled.shape[1:], F32)),
        in_specs=vmem_specs(2),
        out_specs=tuple(vmem_specs(2)),
        compiler_params=pltpu.CompilerParams(vmem_limit_bytes=4 << 20),
        cost_estimate=pl.CostEstimate(flops=5_000_000_000, bytes_accessed=20_000_000, transcendentals=0),
        name=name,
    )(in_vmem(coupled), in_vmem(inv))


def forward_then_back(scaled, arriving, ratio, back_ratio, back_total):
    planes, width = scaled.shape[0], scaled.shape[2]

    def kernel(scaled_ref, near_ref, reach_ref, other_ref, ratio_ref, back_ref, total_ref,
               field_ref, map_ref):
        def ahead(i, state):
            out = []
            for h, rows in enumerate(halves(width)):
                e = block(ratio_ref, i, rows)
                out.append([scaled_ref[i, c, rows, :] - dot5(e[c], state[h]) for c in range(5)])
            for h, rows in enumerate(halves(width)):
                for c in range(5):
                    field_ref[i, c, rows, :] = out[h][c]
            return out

        start = last_join(near_ref, reach_ref, other_ref, False, width)
        lax.fori_loop(0, planes, ahead, start, unroll=4)

        def back(t, state):
            i = planes - 1 - t
            out = []
            for h, rows in enumerate(halves(width)):
                e = block(back_ref, i, rows)
                out.append([field_ref[i, c, rows, :] - dot5(e[c], state[h]) for c in range(5)])
            return out

        zero = [[jnp.zeros((8, LANES), F32)] * 5 for _ in halves(width)]
        state = lax.fori_loop(0, planes, back, zero, unroll=4)
        keep_map(map_ref, total_ref, state, width)

    return pl.pallas_call(
        kernel,
        out_shape=(VMEM(scaled.shape, F32), jax.ShapeDtypeStruct((6,) + scaled.shape[1:], F32)),
        in_specs=vmem_specs(7),
        out_specs=tuple(vmem_specs(2)),
        compiler_params=pltpu.CompilerParams(vmem_limit_bytes=4 << 20),
        name="forward_then_back",
    )(*[in_vmem(v) for v in (scaled, *arriving, ratio, back_ratio, back_total)])


def face_slots(owner, node, owners):
    face_rows = owner.shape[0]
    cap = 2 * face_rows * LANES // owners
    bucket_rows = 2 * face_rows

    def kernel(owner_ref, node_ref, slot_ref, nodes_ref):
        sub = lax.broadcasted_iota(jnp.int32, (LANES, LANES), 0)
        lane = lax.broadcasted_iota(jnp.int32, (LANES, LANES), 1)
        strict = (sub < lane).astype(F32).astype(BF16)
        ones = jnp.ones((LANES, LANES), BF16)
        fs = lax.broadcasted_iota(jnp.int32, (face_rows, face_rows), 0)
        fl = lax.broadcasted_iota(jnp.int32, (face_rows, face_rows), 1)
        lower = (fl < fs).astype(F32).astype(BF16)
        own = owner_ref[...]
        masks = [(own == o).astype(F32) for o in range(owners)]
        stacked = jnp.concatenate(masks, axis=0).astype(BF16)
        before = jnp.dot(stacked, strict, preferred_element_type=F32)
        totals = jnp.dot(stacked, ones, preferred_element_type=F32).astype(BF16)
        rank = jnp.zeros((face_rows, LANES), F32)
        for o in range(owners):
            here = slice(o * face_rows, (o + 1) * face_rows)
            offset = jnp.dot(lower, totals[here], preferred_element_type=F32)
            rank = rank + masks[o] * (before[here] + offset + float(o * cap))
        slot = rank.astype(jnp.int32)
        slot_ref[...] = slot
        nodes = node_ref[...]
        high = (nodes // LANES).astype(F32)
        low = (nodes % LANES).astype(F32)
        parts = place_in_slots(slot, [high, low], bucket_rows)
        nodes_ref[...] = float(LANES) * parts[0] + parts[1]

    return pl.pallas_call(
        kernel,
        out_shape=(VMEM((face_rows, LANES), jnp.int32), VMEM((bucket_rows, LANES), F32)),
        in_specs=vmem_specs(2),
        out_specs=tuple(vmem_specs(2)),
        compiler_params=pltpu.CompilerParams(vmem_limit_bytes=4 << 20),
        cost_estimate=pl.CostEstimate(flops=4_000_000, bytes_accessed=10_000_000, transcendentals=0),
        name="face_slots",
    )(in_vmem(owner), in_vmem(node))


def spread(row, rows):
    tile = jnp.broadcast_to(row, (16, LANES)).astype(BF16)
    return jnp.concatenate([tile] * (rows // 16), axis=0)


def split(value):
    high = value.astype(BF16)
    return high, (value - high.astype(F32)).astype(BF16)


def place_in_slots(slot, parts, bucket_rows):
    face_rows = slot.shape[0]
    high = (slot // LANES).astype(F32)
    low = (slot % LANES).astype(F32)
    parts = [p.astype(F32) for p in parts]
    high_iota = lax.broadcasted_iota(jnp.int32, (bucket_rows, LANES), 0).astype(F32).astype(BF16)
    low_iota = lax.broadcasted_iota(jnp.int32, (LANES, LANES), 0).astype(F32).astype(BF16)
    ones, none = jnp.ones((LANES, LANES), BF16), jnp.zeros((LANES, LANES), BF16)
    zero = jnp.zeros((bucket_rows, LANES), BF16)
    lefts, rights = [], []
    for f in range(face_rows):
        row = slice(f, f + 1)
        hot = high_iota == spread(high[row], bucket_rows)
        lefts.append(jnp.concatenate(
            [jnp.where(hot, spread(p[row], bucket_rows), zero) for p in parts], axis=0))
        rights.append(jnp.where(low_iota == spread(low[row], LANES), ones, none))
    out = lax.dot_general(jnp.concatenate(lefts, axis=1), jnp.concatenate(rights, axis=1),
                          (((1,), (1,)), ((), ())), preferred_element_type=F32)
    return [out[k * bucket_rows:(k + 1) * bucket_rows] for k in range(len(parts))]


def backward_and_faces(field, arriving, back_ratio, count, cell, weight, slot, nodes, devices, owners):
    planes, width = field.shape[0], field.shape[2]
    face_rows = cell.shape[0]
    bucket_rows = nodes.shape[0]
    rows_each = bucket_rows // owners
    group = 2
    piece = 4
    batch = 8

    def kernel(count_ref, field_ref, near_ref, reach_ref, other_ref, back_ref, cell_ref, weight_ref,
               slot_ref, nodes_ref, adjoint_hbm, send_ref, adjoint_ref, parts_ref, value_ref, sems):
        def write(k):
            return pltpu.make_async_copy(adjoint_ref.at[pl.ds(k * batch, batch)],
                                         adjoint_hbm.at[pl.ds(k * batch, batch)], sems.at[k])

        def back(t, state):
            i = planes - 1 - t
            out = []
            for h, rows in enumerate(halves(width)):
                e = block(back_ref, i, rows)
                out.append([field_ref[i, c, rows, :] - dot5(e[c], state[h]) for c in range(5)])
            for h, rows in enumerate(halves(width)):
                for c in range(5):
                    adjoint_ref[i, c, rows, :] = out[h][c]
            for c in range(5):
                high, low = split(jnp.concatenate([o[c] for o in out], axis=0))
                at = pl.ds(pl.multiple_of((i * 5 + c) * width, width), width)
                parts_ref[at, :LANES] = high
                parts_ref[at, LANES:] = low
            return out

        state = last_join(near_ref, reach_ref, other_ref, True, width)
        for k in reversed(range(planes // batch)):
            first = planes - (k + 1) * batch
            state = lax.fori_loop(first, first + batch, back, state, unroll=4)
            write(k).start()

        lane_iota = lax.broadcasted_iota(jnp.int32, (LANES, LANES), 0).astype(F32).astype(BF16)
        sub8 = lax.broadcasted_iota(jnp.int32, (8, LANES), 0)

        def gather(g, carry):
            cells = [cell_ref[pl.ds(g * group + u, 1), :] for u in range(group)]
            hots, offs = [], []
            for at in cells:
                lanes = spread((at % LANES).astype(F32), LANES)
                hots.append(jnp.where(lane_iota == lanes, jnp.ones((LANES, LANES), BF16),
                                      jnp.zeros((LANES, LANES), BF16)))
                offs.append(jnp.broadcast_to(at // LANES, (8, LANES)) - sub8)
            hot = jnp.concatenate(hots, axis=1)
            hot = jnp.concatenate([hot, hot], axis=0)
            found = [[jnp.zeros((8, LANES), F32)] * 5 for _ in range(group)]
            for p in range(0, planes, piece):
                got = jnp.dot(parts_ref[p * 5 * width:(p + piece) * 5 * width, :], hot,
                              preferred_element_type=F32)
                for i in range(piece):
                    for h in range(width // 8):
                        for u in range(group):
                            mask = offs[u] == (p + i) * width + 8 * h
                            for c in range(5):
                                row = (i * 5 + c) * width + 8 * h
                                found[u][c] = jnp.where(mask, got[row:row + 8, u * LANES:(u + 1) * LANES],
                                                        found[u][c])
            weights = weight_ref[:, pl.ds(pl.multiple_of(g * (group * LANES), group * LANES), group * LANES)]
            for u in range(group):
                w = [jnp.broadcast_to(weights[c:c + 1, u * LANES:(u + 1) * LANES], (8, LANES)) for c in range(5)]
                value_ref[pl.ds(g * group + u, 1), :] = jnp.sum(dot5(w, found[u]), axis=0, keepdims=True)
            return carry

        lax.fori_loop(0, face_rows // group, gather, 0, unroll=4)
        live = lax.broadcasted_iota(jnp.int32, (face_rows, LANES), 0) * LANES + lax.broadcasted_iota(
            jnp.int32, (face_rows, LANES), 1) < count_ref[0]
        high, low = split(jnp.where(live, value_ref[...], 0.0))
        placed = place_in_slots(slot_ref[...], [high, low], bucket_rows)
        values = placed[0] + placed[1]
        for o in range(owners):
            here = slice(o * rows_each, (o + 1) * rows_each)
            both = jnp.concatenate([values[here], nodes_ref[here, :]], axis=0)
            for d in range(o, devices, owners):
                send_ref[d] = both
        for k in range(planes // batch):
            write(k).wait()

    return pl.pallas_call(
        kernel,
        out_shape=(
            jax.ShapeDtypeStruct(field.shape, F32),
            jax.ShapeDtypeStruct((devices, 2 * rows_each, LANES), F32),
        ),
        in_specs=[pl.BlockSpec(memory_space=pltpu.SMEM)] + vmem_specs(9),
        out_specs=(pl.BlockSpec(memory_space=pltpu.HBM), pl.BlockSpec(memory_space=VMEM)),
        scratch_shapes=[
            VMEM(field.shape, F32),
            VMEM((planes * 5 * width, 2 * LANES), BF16),
            VMEM((face_rows, LANES), F32),
            pltpu.SemaphoreType.DMA((planes // batch,)),
        ],
        compiler_params=pltpu.CompilerParams(vmem_limit_bytes=12 << 20),
        name="backward_and_faces",
    )(count, in_vmem(field), *[in_vmem(v) for v in arriving], in_vmem(back_ratio), in_vmem(cell),
      in_vmem(weight), in_vmem(slot), in_vmem(nodes))


def node_sums(got):
    devices, rows2, _ = got.shape
    rows_each = rows2 // 2
    side = NODES_DEV // LANES
    batch = min(devices, 128 // rows_each)

    def kernel(got_ref, out_ref):
        iota = lax.broadcasted_iota(jnp.int32, (LANES, LANES), 0).astype(F32).astype(BF16)
        side_iota = lax.broadcasted_iota(jnp.int32, (side, LANES), 0).astype(F32).astype(BF16)
        ones, zero = jnp.ones((LANES, LANES), BF16), jnp.zeros((LANES, LANES), BF16)
        side_zero = jnp.zeros((side, LANES), BF16)

        def body(t, total):
            lefts, rights = [], []
            for u in range(batch):
                d = t * batch + u
                for r in range(rows_each):
                    value = got_ref[d, r:r + 1, :]
                    node = got_ref[d, rows_each + r:rows_each + r + 1, :].astype(jnp.int32)
                    high = value.astype(BF16).astype(F32)
                    hot = side_iota == spread((node // LANES).astype(F32), side)
                    lefts.append(jnp.concatenate([
                        jnp.where(hot, spread(high, side), side_zero),
                        jnp.where(hot, spread(value - high, side), side_zero)], axis=0))
                    rights.append(jnp.where(iota == spread((node % LANES).astype(F32), LANES), ones, zero))
            return total + lax.dot_general(
                jnp.concatenate(lefts, axis=1), jnp.concatenate(rights, axis=1),
                (((1,), (1,)), ((), ())), preferred_element_type=F32)

        total = jnp.zeros((2 * side, LANES), F32)
        if batch == devices:
            total = body(0, total)
        else:
            total = lax.fori_loop(0, devices // batch, body, total)
        out_ref[...] = total[:side] + total[side:]

    return pl.pallas_call(
        kernel,
        out_shape=jax.ShapeDtypeStruct((side, LANES), F32),
        in_specs=vmem_specs(1),
        out_specs=pl.BlockSpec(memory_space=VMEM),
        compiler_params=pltpu.CompilerParams(vmem_limit_bytes=24 << 20),
        name="node_sums",
    )(in_vmem(got))


def comes_after(stage, backward):
    bit = lax.rem(lax.div(lax.axis_index("sweep"), 1 << stage), 2)
    return bit == (0 if backward else 1)


def matvec(matrix, vector):
    return [dot5(row, vector) for row in matrix]


def matmat(matrix, other):
    return [[dot5(row, [other[e][x] for e in range(5)]) for x in range(5)] for row in matrix]


def load_matrix(ref, rows):
    return [[ref[c, d, rows, :] for d in range(5)] for c in range(5)]


def load_vector(ref, rows):
    return [ref[c, rows, :] for c in range(5)]


def pick(flag, one, two):
    if isinstance(one, list):
        return [pick(flag, a, b) for a, b in zip(one, two)]
    return jnp.where(flag, one, two)


def last_join(near_ref, reach_ref, other_ref, backward, width):
    after = comes_after(lax.axis_size("sweep").bit_length() - 2, backward)
    start = []
    for rows in halves(width):
        near = load_vector(near_ref, rows)
        gain = matvec(load_matrix(reach_ref, rows), load_vector(other_ref, rows))
        start.append([n + jnp.where(after, g, 0.0) for n, g in zip(near, gain)])
    return start


def join(stage, backward, near, reach, own, other, whole):
    first = near is None
    _, _, width, _ = own.shape
    vector = own.shape[1:]
    outs = [vector, (5,) + vector, own.shape if whole else vector]
    operands = [own, other] + ([] if first else [near, reach])

    def kernel(*refs):
        ins, out = refs[:len(operands)], refs[len(operands):]
        after = comes_after(stage, backward)
        for rows in halves(width):
            mine, theirs = load_vector(ins[0].at[5], rows), load_vector(ins[1].at[5], rows)
            my_total, their_total = load_matrix(ins[0], rows), load_matrix(ins[1], rows)
            if first:
                entering = theirs
                through = their_total
                before = [jnp.zeros((8, LANES), F32)] * 5
                unit = [[jnp.full((8, LANES), 1.0 if c == d else 0.0, F32) for d in range(5)] for c in range(5)]
            else:
                before, unit = load_vector(ins[2], rows), load_matrix(ins[3], rows)
                entering = [a + b for a, b in zip(before, matvec(unit, theirs))]
                through = matmat(unit, their_total)
            entering, through = pick(after, entering, before), pick(after, through, unit)
            downstream = pick(after, my_total, their_total)
            sent = matvec(downstream, pick(after, theirs, mine))
            sent = [a + b for a, b in zip(pick(after, mine, theirs), sent)]
            sent_ref = out[2].at[5] if whole else out[2]
            for c in range(5):
                out[0][c, rows, :] = entering[c]
                sent_ref[c, rows, :] = sent[c]
                for d in range(5):
                    out[1][c, d, rows, :] = through[c][d]
            if whole:
                product = matmat(downstream, pick(after, their_total, my_total))
                for c in range(5):
                    for d in range(5):
                        out[2][c, d, rows, :] = product[c][d]

    return pl.pallas_call(
        kernel,
        out_shape=tuple(jax.ShapeDtypeStruct(shape, F32) for shape in outs),
        in_specs=vmem_specs(len(operands)),
        out_specs=tuple(vmem_specs(3)),
        compiler_params=pltpu.CompilerParams(vmem_limit_bytes=4 << 20),
        name="join",
    )(*[in_vmem(v) for v in operands])


def relay(own, backward):
    size = lax.axis_size("sweep")
    stages = size.bit_length() - 1
    near = reach = None
    for stage in range(stages):
        pairs = [(i, i ^ (1 << stage)) for i in range(size)]
        other = lax.ppermute(own, "sweep", pairs)
        if stage == stages - 1:
            return (near, reach, other), own
        near, reach, own = join(stage, backward, near, reach, own, other, stage + 2 < stages)


def per_device(source, psi_old, lateral, lower_jac, upper_jac, diag_inv, face_weight, face_cell,
               face_owner, face_node, face_count):
    bulk = lax.axis_size("bulk")
    devices = bulk * lax.axis_size("sweep")
    low_pairs = [(i, i ^ 1) for i in range(bulk) if i ^ 1 < bulk]
    high_pairs = [(i, j) for i in range(bulk) for j in [i + 1 if i % 2 else i - 1] if 0 <= j < bulk]
    low_edge, high_edge = edge_rows(psi_old)
    low_edge, high_edge, lower_jac = lax.optimization_barrier((low_edge, high_edge, lower_jac))
    second = lax.ppermute(high_edge, "bulk", high_pairs)
    first = lax.ppermute(low_edge, "bulk", low_pairs)

    ratio, total = matrices(lower_jac, diag_inv, False, "forward_matrices")
    scaled, own = forward_local(source, psi_old, lateral, second, first, ratio, diag_inv, total)
    arriving, joined = relay(own, False)
    upper_jac, joined = lax.optimization_barrier((upper_jac, joined))
    back_ratio, back_total = matrices(upper_jac, diag_inv, True, "backward_matrices")
    field, own = forward_then_back(scaled, arriving, ratio, back_ratio, back_total)
    arriving, _ = relay(own, True)

    slots = face_cell.shape[0]
    rows = (slots // LANES, LANES)
    slot, nodes = face_slots(face_owner.reshape(rows), face_node.reshape(rows), bulk)
    adjoint, send = backward_and_faces(field, arriving, back_ratio, face_count, face_cell.reshape(rows),
                                       face_weight, slot, nodes, devices, bulk)
    got = lax.all_to_all(send, ("sweep", "bulk"), 0, 0, tiled=True)
    return adjoint, node_sums(got).reshape(NODES_DEV)


def solution(mesh):
    placed = (
        P("sweep", None, "bulk", None),
        P("sweep", None, "bulk", None),
        P("sweep", None, "bulk", None),
        P("sweep", None, None, "bulk", None),
        P("sweep", None, None, "bulk", None),
        P("sweep", None, None, "bulk", None),
        P(None, ("sweep", "bulk")),
        P(("sweep", "bulk")),
        P(("sweep", "bulk"), None),
        P(("sweep", "bulk")),
        P(("sweep", "bulk")),
    )
    return jax.shard_map(
        per_device,
        mesh=mesh,
        in_specs=placed,
        out_specs=(P("sweep", None, "bulk", None), P("bulk")),
        check_vma=False,
    )
```

```python
import jax
import jax.numpy as jnp
from jax import lax
from jax.experimental import pallas as pl
from jax.experimental.pallas import tpu as pltpu
from jax.sharding import PartitionSpec as P

NODES_DEV = 16384
LANES = 128
F32 = jnp.float32
BF16 = jnp.bfloat16
VMEM = pltpu.VMEM


def dot5(a, b):
    p = [x * y for x, y in zip(a, b)]
    return ((p[0] + p[1]) + (p[2] + p[3])) + p[4]


def block(ref, at, rows):
    return [[ref[at, c, d, rows, :] for d in range(5)] for c in range(5)]


def halves(width):
    return [pl.ds(8 * h, 8) for h in range(width // 8)]


def in_vmem(value):
    return pltpu.with_memory_space_constraint(value, VMEM)


def in_hbm(value):
    return pltpu.with_memory_space_constraint(value, pltpu.HBM)


def vmem_specs(n):
    return [pl.BlockSpec(memory_space=VMEM)] * n


def ratio_of(coupled, inv, at, rows):
    j = block(coupled, at, rows)
    d = block(inv, at, rows)
    return [[dot5(d[c], [j[e][x] for e in range(5)]) for x in range(5)] for c in range(5)]


def next_total(ratio, total_ref, rows):
    old = [[total_ref[e, x, rows, :] for x in range(5)] for e in range(5)]
    return [[dot5(ratio[c], [old[e][x] for e in range(5)]) for x in range(5)] for c in range(5)]


def keep_matrices(ratio, total, ratio_ref, total_ref, at, rows):
    for c in range(5):
        for x in range(5):
            ratio_ref[at, c, x, rows, :] = ratio[c][x]
            total_ref[c, x, rows, :] = total[c][x]


def keep_map(map_ref, total_ref, leaving, width):
    map_ref[:5] = total_ref[...]
    for h, rows in enumerate(halves(width)):
        for c in range(5):
            map_ref[5, c, rows, :] = leaving[h][c]


def set_identity(total_ref, planes):
    sign = 1.0 if planes % 2 == 0 else -1.0
    for c in range(5):
        for d in range(5):
            total_ref[c, d] = jnp.full(total_ref.shape[2:], sign if c == d else 0.0, F32)


def edge_rows(psi):
    planes, fields, width, _ = psi.shape
    shape = (fields * planes, LANES)

    def kernel(psi_hbm, low_ref, high_ref, head_ref, tail_ref, sems):
        copies = []
        for c in range(fields):
            rows = pl.ds(c * planes, planes)
            copies.append(pltpu.make_async_copy(psi_hbm.at[:, c, 0, :], head_ref.at[rows], sems.at[0, c]))
            copies.append(pltpu.make_async_copy(psi_hbm.at[:, c, width - 1, :], tail_ref.at[rows], sems.at[1, c]))
        for copy in copies:
            copy.start()
        is_odd = lax.rem(lax.axis_index("bulk"), 2) == 1
        for copy in copies:
            copy.wait()
        head, tail = head_ref[...], tail_ref[...]
        low_ref[...] = jnp.where(is_odd, head, tail)
        high_ref[...] = jnp.where(is_odd, tail, head)

    return pl.pallas_call(
        kernel,
        out_shape=(jax.ShapeDtypeStruct(shape, F32), jax.ShapeDtypeStruct(shape, F32)),
        in_specs=[pl.BlockSpec(memory_space=pltpu.HBM)],
        out_specs=tuple(vmem_specs(2)),
        scratch_shapes=[VMEM(shape, F32), VMEM(shape, F32), pltpu.SemaphoreType.DMA((2, fields))],
        compiler_params=pltpu.CompilerParams(vmem_limit_bytes=4 << 20),
        cost_estimate=pl.CostEstimate(flops=10_000_000_000, bytes_accessed=20_000_000, transcendentals=0),
        name="edge_rows",
    )(in_hbm(psi))


def forward_local(source, psi, lateral, second, first, ratio, inv, total):
    planes, width = source.shape[0], source.shape[2]

    def kernel(source_ref, psi_ref, lateral_ref, second_ref, first_ref, ratio_ref, inv_ref, total_ref,
               scaled_ref, map_ref):
        is_odd = lax.rem(lax.axis_index("bulk"), 2) == 1

        def body(i, state):
            below, above = lateral_ref[i, 0], lateral_ref[i, 1]
            right = []
            for c in range(5):
                one = first_ref[pl.ds(c * planes + i, 1), :]
                two = second_ref[pl.ds(c * planes + i, 1), :]
                here = psi_ref[i, c]
                down = jnp.concatenate([jnp.where(is_odd, one, two), here[:width - 1]], axis=0)
                up = jnp.concatenate([here[1:], jnp.where(is_odd, two, one)], axis=0)
                right.append(source_ref[i, c] - below * down - above * up)
            out = []
            for h, rows in enumerate(halves(width)):
                r = [v[8 * h:8 * h + 8] for v in right]
                d = block(inv_ref, i, rows)
                e = block(ratio_ref, i, rows)
                g = [dot5(d[c], r) for c in range(5)]
                out.append((g, [g[c] - dot5(e[c], state[h]) for c in range(5)]))
            for h, rows in enumerate(halves(width)):
                for c in range(5):
                    scaled_ref[i, c, rows, :] = out[h][0][c]
            return [f for _, f in out]

        zero = [[jnp.zeros((8, LANES), F32)] * 5 for _ in halves(width)]
        state = lax.fori_loop(0, planes, body, zero, unroll=2)
        keep_map(map_ref, total_ref, state, width)

    return pl.pallas_call(
        kernel,
        out_shape=(VMEM(source.shape, F32), jax.ShapeDtypeStruct((6,) + source.shape[1:], F32)),
        in_specs=vmem_specs(8),
        out_specs=tuple(vmem_specs(2)),
        compiler_params=pltpu.CompilerParams(vmem_limit_bytes=4 << 20),
        name="forward_local",
    )(*[in_vmem(v) for v in (source, psi, lateral, second, first, ratio, inv, total)])


def some_ratios(coupled, inv, count):
    planes, width = coupled.shape[0], coupled.shape[3]

    def kernel(coupled_ref, inv_ref, ratio_ref):
        def body(t, carry):
            at = planes - 1 - t
            for rows in halves(width):
                ratio = ratio_of(coupled_ref, inv_ref, at, rows)
                for c in range(5):
                    for x in range(5):
                        ratio_ref[at, c, x, rows, :] = ratio[c][x]
            return carry

        lax.fori_loop(0, count, body, 0, unroll=2)

    return pl.pallas_call(
        kernel,
        out_shape=VMEM(coupled.shape, F32),
        in_specs=vmem_specs(2),
        out_specs=pl.BlockSpec(memory_space=VMEM),
        compiler_params=pltpu.CompilerParams(vmem_limit_bytes=4 << 20),
        cost_estimate=pl.CostEstimate(flops=100_000_000, bytes_accessed=8_000, transcendentals=0),
        name="some_ratios",
    )(in_vmem(coupled), in_vmem(inv))


def matrices(coupled, inv, backward, name, started=None, count=0):
    planes, width = coupled.shape[0], coupled.shape[3]

    def kernel(coupled_ref, inv_ref, *refs):
        ratio_ref, total_ref = refs[-2:]
        set_identity(total_ref, planes)

        def body(t, carry, known):
            at = planes - 1 - t if backward else t
            for rows in halves(width):
                if known:
                    ratio = block(ratio_ref, at, rows)
                    total = next_total(ratio, total_ref, rows)
                    for c in range(5):
                        for x in range(5):
                            total_ref[c, x, rows, :] = total[c][x]
                else:
                    ratio = ratio_of(coupled_ref, inv_ref, at, rows)
                    keep_matrices(ratio, next_total(ratio, total_ref, rows), ratio_ref, total_ref, at, rows)
            return carry

        if count:
            lax.fori_loop(0, count, lambda t, carry: body(t, carry, True), 0, unroll=2)
        lax.fori_loop(count, planes, lambda t, carry: body(t, carry, False), 0, unroll=2)

    operands = [coupled, inv] + ([] if started is None else [started])
    return pl.pallas_call(
        kernel,
        out_shape=(VMEM(coupled.shape, F32), jax.ShapeDtypeStruct(coupled.shape[1:], F32)),
        in_specs=vmem_specs(len(operands)),
        out_specs=tuple(vmem_specs(2)),
        input_output_aliases={} if started is None else {2: 0},
        compiler_params=pltpu.CompilerParams(vmem_limit_bytes=4 << 20),
        cost_estimate=pl.CostEstimate(flops=5_000_000_000, bytes_accessed=20_000_000, transcendentals=0),
        name=name,
    )(*[in_vmem(v) for v in operands])


def forward_then_back(scaled, arriving, ratio, back_ratio, back_total):
    planes, width = scaled.shape[0], scaled.shape[2]

    def kernel(scaled_ref, near_ref, reach_ref, other_ref, ratio_ref, back_ref, total_ref,
               field_ref, map_ref):
        def ahead(i, state):
            out = []
            for h, rows in enumerate(halves(width)):
                e = block(ratio_ref, i, rows)
                out.append([scaled_ref[i, c, rows, :] - dot5(e[c], state[h]) for c in range(5)])
            for h, rows in enumerate(halves(width)):
                for c in range(5):
                    field_ref[i, c, rows, :] = out[h][c]
            return out

        start = last_join(near_ref, reach_ref, other_ref, False, width)
        lax.fori_loop(0, planes, ahead, start, unroll=4)

        def back(t, state):
            i = planes - 1 - t
            out = []
            for h, rows in enumerate(halves(width)):
                e = block(back_ref, i, rows)
                out.append([field_ref[i, c, rows, :] - dot5(e[c], state[h]) for c in range(5)])
            return out

        zero = [[jnp.zeros((8, LANES), F32)] * 5 for _ in halves(width)]
        state = lax.fori_loop(0, planes, back, zero, unroll=4)
        keep_map(map_ref, total_ref, state, width)

    return pl.pallas_call(
        kernel,
        out_shape=(VMEM(scaled.shape, F32), jax.ShapeDtypeStruct((6,) + scaled.shape[1:], F32)),
        in_specs=vmem_specs(7),
        out_specs=tuple(vmem_specs(2)),
        compiler_params=pltpu.CompilerParams(vmem_limit_bytes=4 << 20),
        name="forward_then_back",
    )(*[in_vmem(v) for v in (scaled, *arriving, ratio, back_ratio, back_total)])


def face_slots(owner, node, owners):
    face_rows = owner.shape[0]
    cap = 2 * face_rows * LANES // owners
    bucket_rows = 2 * face_rows

    def kernel(owner_ref, node_ref, slot_ref, nodes_ref):
        sub = lax.broadcasted_iota(jnp.int32, (LANES, LANES), 0)
        lane = lax.broadcasted_iota(jnp.int32, (LANES, LANES), 1)
        strict = (sub < lane).astype(F32).astype(BF16)
        ones = jnp.ones((LANES, LANES), BF16)
        fs = lax.broadcasted_iota(jnp.int32, (face_rows, face_rows), 0)
        fl = lax.broadcasted_iota(jnp.int32, (face_rows, face_rows), 1)
        lower = (fl < fs).astype(F32).astype(BF16)
        own = owner_ref[...]
        masks = [(own == o).astype(F32) for o in range(owners)]
        stacked = jnp.concatenate(masks, axis=0).astype(BF16)
        before = jnp.dot(stacked, strict, preferred_element_type=F32)
        totals = jnp.dot(stacked, ones, preferred_element_type=F32).astype(BF16)
        rank = jnp.zeros((face_rows, LANES), F32)
        for o in range(owners):
            here = slice(o * face_rows, (o + 1) * face_rows)
            offset = jnp.dot(lower, totals[here], preferred_element_type=F32)
            rank = rank + masks[o] * (before[here] + offset + float(o * cap))
        slot = rank.astype(jnp.int32)
        slot_ref[...] = slot
        nodes = node_ref[...]
        high = (nodes // LANES).astype(F32)
        low = (nodes % LANES).astype(F32)
        parts = place_in_slots(slot, [high, low], bucket_rows)
        nodes_ref[...] = float(LANES) * parts[0] + parts[1]

    return pl.pallas_call(
        kernel,
        out_shape=(VMEM((face_rows, LANES), jnp.int32), VMEM((bucket_rows, LANES), F32)),
        in_specs=vmem_specs(2),
        out_specs=tuple(vmem_specs(2)),
        compiler_params=pltpu.CompilerParams(vmem_limit_bytes=4 << 20),
        cost_estimate=pl.CostEstimate(flops=4_000_000, bytes_accessed=10_000_000, transcendentals=0),
        name="face_slots",
    )(in_vmem(owner), in_vmem(node))


def spread(row, rows):
    tile = jnp.broadcast_to(row, (16, LANES)).astype(BF16)
    return jnp.concatenate([tile] * (rows // 16), axis=0)


def split(value):
    high = value.astype(BF16)
    return high, (value - high.astype(F32)).astype(BF16)


def place_in_slots(slot, parts, bucket_rows):
    face_rows = slot.shape[0]
    high = (slot // LANES).astype(F32)
    low = (slot % LANES).astype(F32)
    parts = [p.astype(F32) for p in parts]
    high_iota = lax.broadcasted_iota(jnp.int32, (bucket_rows, LANES), 0).astype(F32).astype(BF16)
    low_iota = lax.broadcasted_iota(jnp.int32, (LANES, LANES), 0).astype(F32).astype(BF16)
    ones, none = jnp.ones((LANES, LANES), BF16), jnp.zeros((LANES, LANES), BF16)
    zero = jnp.zeros((bucket_rows, LANES), BF16)
    lefts, rights = [], []
    for f in range(face_rows):
        row = slice(f, f + 1)
        hot = high_iota == spread(high[row], bucket_rows)
        lefts.append(jnp.concatenate(
            [jnp.where(hot, spread(p[row], bucket_rows), zero) for p in parts], axis=0))
        rights.append(jnp.where(low_iota == spread(low[row], LANES), ones, none))
    out = lax.dot_general(jnp.concatenate(lefts, axis=1), jnp.concatenate(rights, axis=1),
                          (((1,), (1,)), ((), ())), preferred_element_type=F32)
    return [out[k * bucket_rows:(k + 1) * bucket_rows] for k in range(len(parts))]


def backward_and_faces(field, arriving, back_ratio, count, cell, weight, slot, nodes, devices, owners):
    planes, width = field.shape[0], field.shape[2]
    face_rows = cell.shape[0]
    bucket_rows = nodes.shape[0]
    rows_each = bucket_rows // owners
    group = 2
    piece = 4
    batch = 8

    def kernel(count_ref, field_ref, near_ref, reach_ref, other_ref, back_ref, cell_ref, weight_ref,
               slot_ref, nodes_ref, adjoint_hbm, send_ref, adjoint_ref, parts_ref, value_ref, sems):
        def write(k):
            return pltpu.make_async_copy(adjoint_ref.at[pl.ds(k * batch, batch)],
                                         adjoint_hbm.at[pl.ds(k * batch, batch)], sems.at[k])

        def back(t, state):
            i = planes - 1 - t
            out = []
            for h, rows in enumerate(halves(width)):
                e = block(back_ref, i, rows)
                out.append([field_ref[i, c, rows, :] - dot5(e[c], state[h]) for c in range(5)])
            for h, rows in enumerate(halves(width)):
                for c in range(5):
                    adjoint_ref[i, c, rows, :] = out[h][c]
            for c in range(5):
                high, low = split(jnp.concatenate([o[c] for o in out], axis=0))
                at = pl.ds(pl.multiple_of((i * 5 + c) * width, width), width)
                parts_ref[at, :LANES] = high
                parts_ref[at, LANES:] = low
            return out

        state = last_join(near_ref, reach_ref, other_ref, True, width)
        for k in reversed(range(planes // batch)):
            first = planes - (k + 1) * batch
            state = lax.fori_loop(first, first + batch, back, state, unroll=4)
            write(k).start()

        lane_iota = lax.broadcasted_iota(jnp.int32, (LANES, LANES), 0).astype(F32).astype(BF16)
        sub8 = lax.broadcasted_iota(jnp.int32, (8, LANES), 0)

        def gather(g, carry):
            cells = [cell_ref[pl.ds(g * group + u, 1), :] for u in range(group)]
            hots, offs = [], []
            for at in cells:
                lanes = spread((at % LANES).astype(F32), LANES)
                hots.append(jnp.where(lane_iota == lanes, jnp.ones((LANES, LANES), BF16),
                                      jnp.zeros((LANES, LANES), BF16)))
                offs.append(jnp.broadcast_to(at // LANES, (8, LANES)) - sub8)
            hot = jnp.concatenate(hots, axis=1)
            hot = jnp.concatenate([hot, hot], axis=0)
            found = [[jnp.zeros((8, LANES), F32)] * 5 for _ in range(group)]
            for p in range(0, planes, piece):
                got = jnp.dot(parts_ref[p * 5 * width:(p + piece) * 5 * width, :], hot,
                              preferred_element_type=F32)
                for i in range(piece):
                    for h in range(width // 8):
                        for u in range(group):
                            mask = offs[u] == (p + i) * width + 8 * h
                            for c in range(5):
                                row = (i * 5 + c) * width + 8 * h
                                found[u][c] = jnp.where(mask, got[row:row + 8, u * LANES:(u + 1) * LANES],
                                                        found[u][c])
            weights = weight_ref[:, pl.ds(pl.multiple_of(g * (group * LANES), group * LANES), group * LANES)]
            for u in range(group):
                w = [jnp.broadcast_to(weights[c:c + 1, u * LANES:(u + 1) * LANES], (8, LANES)) for c in range(5)]
                value_ref[pl.ds(g * group + u, 1), :] = jnp.sum(dot5(w, found[u]), axis=0, keepdims=True)
            return carry

        lax.fori_loop(0, face_rows // group, gather, 0, unroll=4)
        live = lax.broadcasted_iota(jnp.int32, (face_rows, LANES), 0) * LANES + lax.broadcasted_iota(
            jnp.int32, (face_rows, LANES), 1) < count_ref[0]
        high, low = split(jnp.where(live, value_ref[...], 0.0))
        placed = place_in_slots(slot_ref[...], [high, low], bucket_rows)
        values = placed[0] + placed[1]
        for o in range(owners):
            here = slice(o * rows_each, (o + 1) * rows_each)
            both = jnp.concatenate([values[here], nodes_ref[here, :]], axis=0)
            for d in range(o, devices, owners):
                send_ref[d] = both
        for k in range(planes // batch):
            write(k).wait()

    return pl.pallas_call(
        kernel,
        out_shape=(
            jax.ShapeDtypeStruct(field.shape, F32),
            jax.ShapeDtypeStruct((devices, 2 * rows_each, LANES), F32),
        ),
        in_specs=[pl.BlockSpec(memory_space=pltpu.SMEM)] + vmem_specs(9),
        out_specs=(pl.BlockSpec(memory_space=pltpu.HBM), pl.BlockSpec(memory_space=VMEM)),
        scratch_shapes=[
            VMEM(field.shape, F32),
            VMEM((planes * 5 * width, 2 * LANES), BF16),
            VMEM((face_rows, LANES), F32),
            pltpu.SemaphoreType.DMA((planes // batch,)),
        ],
        compiler_params=pltpu.CompilerParams(vmem_limit_bytes=12 << 20),
        name="backward_and_faces",
    )(count, in_vmem(field), *[in_vmem(v) for v in arriving], in_vmem(back_ratio), in_vmem(cell),
      in_vmem(weight), in_vmem(slot), in_vmem(nodes))


def node_sums(got):
    devices, rows2, _ = got.shape
    rows_each = rows2 // 2
    side = NODES_DEV // LANES
    batch = min(devices, 128 // rows_each)

    def kernel(got_ref, out_ref):
        iota = lax.broadcasted_iota(jnp.int32, (LANES, LANES), 0).astype(F32).astype(BF16)
        side_iota = lax.broadcasted_iota(jnp.int32, (side, LANES), 0).astype(F32).astype(BF16)
        ones, zero = jnp.ones((LANES, LANES), BF16), jnp.zeros((LANES, LANES), BF16)
        side_zero = jnp.zeros((side, LANES), BF16)

        def body(t, total):
            lefts, rights = [], []
            for u in range(batch):
                d = t * batch + u
                for r in range(rows_each):
                    value = got_ref[d, r:r + 1, :]
                    node = got_ref[d, rows_each + r:rows_each + r + 1, :].astype(jnp.int32)
                    high = value.astype(BF16).astype(F32)
                    hot = side_iota == spread((node // LANES).astype(F32), side)
                    lefts.append(jnp.concatenate([
                        jnp.where(hot, spread(high, side), side_zero),
                        jnp.where(hot, spread(value - high, side), side_zero)], axis=0))
                    rights.append(jnp.where(iota == spread((node % LANES).astype(F32), LANES), ones, zero))
            return total + lax.dot_general(
                jnp.concatenate(lefts, axis=1), jnp.concatenate(rights, axis=1),
                (((1,), (1,)), ((), ())), preferred_element_type=F32)

        total = jnp.zeros((2 * side, LANES), F32)
        if batch == devices:
            total = body(0, total)
        else:
            total = lax.fori_loop(0, devices // batch, body, total)
        out_ref[...] = total[:side] + total[side:]

    return pl.pallas_call(
        kernel,
        out_shape=jax.ShapeDtypeStruct((side, LANES), F32),
        in_specs=vmem_specs(1),
        out_specs=pl.BlockSpec(memory_space=VMEM),
        compiler_params=pltpu.CompilerParams(vmem_limit_bytes=24 << 20),
        name="node_sums",
    )(in_vmem(got))


def comes_after(stage, backward):
    bit = lax.rem(lax.div(lax.axis_index("sweep"), 1 << stage), 2)
    return bit == (0 if backward else 1)


def matvec(matrix, vector):
    return [dot5(row, vector) for row in matrix]


def matmat(matrix, other):
    return [[dot5(row, [other[e][x] for e in range(5)]) for x in range(5)] for row in matrix]


def load_matrix(ref, rows):
    return [[ref[c, d, rows, :] for d in range(5)] for c in range(5)]


def load_vector(ref, rows):
    return [ref[c, rows, :] for c in range(5)]


def pick(flag, one, two):
    if isinstance(one, list):
        return [pick(flag, a, b) for a, b in zip(one, two)]
    return jnp.where(flag, one, two)


def last_join(near_ref, reach_ref, other_ref, backward, width):
    after = comes_after(lax.axis_size("sweep").bit_length() - 2, backward)
    start = []
    for rows in halves(width):
        near = load_vector(near_ref, rows)
        gain = matvec(load_matrix(reach_ref, rows), load_vector(other_ref, rows))
        start.append([n + jnp.where(after, g, 0.0) for n, g in zip(near, gain)])
    return start


def join(stage, backward, near, reach, own, other, whole):
    first = near is None
    _, _, width, _ = own.shape
    vector = own.shape[1:]
    outs = [vector, (5,) + vector, own.shape if whole else vector]
    operands = [own, other] + ([] if first else [near, reach])

    def kernel(*refs):
        ins, out = refs[:len(operands)], refs[len(operands):]
        after = comes_after(stage, backward)
        for rows in halves(width):
            mine, theirs = load_vector(ins[0].at[5], rows), load_vector(ins[1].at[5], rows)
            my_total, their_total = load_matrix(ins[0], rows), load_matrix(ins[1], rows)
            if first:
                entering = theirs
                through = their_total
                before = [jnp.zeros((8, LANES), F32)] * 5
                unit = [[jnp.full((8, LANES), 1.0 if c == d else 0.0, F32) for d in range(5)] for c in range(5)]
            else:
                before, unit = load_vector(ins[2], rows), load_matrix(ins[3], rows)
                entering = [a + b for a, b in zip(before, matvec(unit, theirs))]
                through = matmat(unit, their_total)
            entering, through = pick(after, entering, before), pick(after, through, unit)
            downstream = pick(after, my_total, their_total)
            sent = matvec(downstream, pick(after, theirs, mine))
            sent = [a + b for a, b in zip(pick(after, mine, theirs), sent)]
            sent_ref = out[2].at[5] if whole else out[2]
            for c in range(5):
                out[0][c, rows, :] = entering[c]
                sent_ref[c, rows, :] = sent[c]
                for d in range(5):
                    out[1][c, d, rows, :] = through[c][d]
            if whole:
                product = matmat(downstream, pick(after, their_total, my_total))
                for c in range(5):
                    for d in range(5):
                        out[2][c, d, rows, :] = product[c][d]

    return pl.pallas_call(
        kernel,
        out_shape=tuple(jax.ShapeDtypeStruct(shape, F32) for shape in outs),
        in_specs=vmem_specs(len(operands)),
        out_specs=tuple(vmem_specs(3)),
        compiler_params=pltpu.CompilerParams(vmem_limit_bytes=4 << 20),
        name="join",
    )(*[in_vmem(v) for v in operands])


def relay(own, backward):
    size = lax.axis_size("sweep")
    stages = size.bit_length() - 1
    near = reach = None
    for stage in range(stages):
        pairs = [(i, i ^ (1 << stage)) for i in range(size)]
        other = lax.ppermute(own, "sweep", pairs)
        if stage == stages - 1:
            return (near, reach, other), own
        near, reach, own = join(stage, backward, near, reach, own, other, stage + 2 < stages)


def per_device(source, psi_old, lateral, lower_jac, upper_jac, diag_inv, face_weight, face_cell,
               face_owner, face_node, face_count):
    bulk = lax.axis_size("bulk")
    devices = bulk * lax.axis_size("sweep")
    low_pairs = [(i, i ^ 1) for i in range(bulk) if i ^ 1 < bulk]
    high_pairs = [(i, j) for i in range(bulk) for j in [i + 1 if i % 2 else i - 1] if 0 <= j < bulk]
    low_edge, high_edge = edge_rows(psi_old)
    low_edge, high_edge, lower_jac, upper_jac = lax.optimization_barrier(
        (low_edge, high_edge, lower_jac, upper_jac))
    second = lax.ppermute(high_edge, "bulk", high_pairs)
    first = lax.ppermute(low_edge, "bulk", low_pairs)

    ratio, total = matrices(lower_jac, diag_inv, False, "forward_matrices")
    count = 14 * upper_jac.shape[0] // 32
    started = some_ratios(upper_jac, diag_inv, count)
    ratio, started = lax.optimization_barrier((ratio, started))
    scaled, own = forward_local(source, psi_old, lateral, second, first, ratio, diag_inv, total)
    arriving, joined = relay(own, False)
    started, joined = lax.optimization_barrier((started, joined))
    back_ratio, back_total = matrices(upper_jac, diag_inv, True, "backward_matrices", started, count)
    field, own = forward_then_back(scaled, arriving, ratio, back_ratio, back_total)
    arriving, _ = relay(own, True)

    slots = face_cell.shape[0]
    rows = (slots // LANES, LANES)
    slot, nodes = face_slots(face_owner.reshape(rows), face_node.reshape(rows), bulk)
    adjoint, send = backward_and_faces(field, arriving, back_ratio, face_count, face_cell.reshape(rows),
                                       face_weight, slot, nodes, devices, bulk)
    got = lax.all_to_all(send, ("sweep", "bulk"), 0, 0, tiled=True)
    return adjoint, node_sums(got).reshape(NODES_DEV)


def solution(mesh):
    placed = (
        P("sweep", None, "bulk", None),
        P("sweep", None, "bulk", None),
        P("sweep", None, "bulk", None),
        P("sweep", None, None, "bulk", None),
        P("sweep", None, None, "bulk", None),
        P("sweep", None, None, "bulk", None),
        P(None, ("sweep", "bulk")),
        P(("sweep", "bulk")),
        P(("sweep", "bulk"), None),
        P(("sweep", "bulk")),
        P(("sweep", "bulk")),
    )
    return jax.shard_map(
        per_device,
        mesh=mesh,
        in_specs=placed,
        out_specs=(P("sweep", None, "bulk", None), P("bulk")),
        check_vma=False,
    )
```

```python
import jax
import jax.numpy as jnp
from jax import lax
from jax.experimental import pallas as pl
from jax.experimental.pallas import tpu as pltpu
from jax.sharding import PartitionSpec as P

NODES_DEV = 16384
LANES = 128
F32 = jnp.float32
BF16 = jnp.bfloat16
VMEM = pltpu.VMEM


def dot5(a, b):
    p = [x * y for x, y in zip(a, b)]
    return ((p[0] + p[1]) + (p[2] + p[3])) + p[4]


def block(ref, at, rows):
    return [[ref[at, c, d, rows, :] for d in range(5)] for c in range(5)]


def halves(width):
    return [pl.ds(8 * h, 8) for h in range(width // 8)]


def in_vmem(value):
    return pltpu.with_memory_space_constraint(value, VMEM)


def in_hbm(value):
    return pltpu.with_memory_space_constraint(value, pltpu.HBM)


def vmem_specs(n):
    return [pl.BlockSpec(memory_space=VMEM)] * n


def ratio_of(coupled, inv, at, rows):
    j = block(coupled, at, rows)
    d = block(inv, at, rows)
    return [[dot5(d[c], [j[e][x] for e in range(5)]) for x in range(5)] for c in range(5)]


def next_total(ratio, total_ref, rows):
    old = [[total_ref[e, x, rows, :] for x in range(5)] for e in range(5)]
    return [[dot5(ratio[c], [old[e][x] for e in range(5)]) for x in range(5)] for c in range(5)]


def keep_matrices(ratio, total, ratio_ref, total_ref, at, rows):
    for c in range(5):
        for x in range(5):
            ratio_ref[at, c, x, rows, :] = ratio[c][x]
            total_ref[c, x, rows, :] = total[c][x]


def keep_map(map_ref, total_ref, leaving, width):
    map_ref[:5] = total_ref[...]
    for h, rows in enumerate(halves(width)):
        for c in range(5):
            map_ref[5, c, rows, :] = leaving[h][c]


def set_identity(total_ref, planes):
    sign = 1.0 if planes % 2 == 0 else -1.0
    for c in range(5):
        for d in range(5):
            total_ref[c, d] = jnp.full(total_ref.shape[2:], sign if c == d else 0.0, F32)


def edge_rows(psi):
    planes, fields, width, _ = psi.shape
    shape = (fields * planes, LANES)

    def kernel(psi_hbm, low_ref, high_ref, head_ref, tail_ref, sems):
        copies = []
        for c in range(fields):
            rows = pl.ds(c * planes, planes)
            copies.append(pltpu.make_async_copy(psi_hbm.at[:, c, 0, :], head_ref.at[rows], sems.at[0, c]))
            copies.append(pltpu.make_async_copy(psi_hbm.at[:, c, width - 1, :], tail_ref.at[rows], sems.at[1, c]))
        for copy in copies:
            copy.start()
        is_odd = lax.rem(lax.axis_index("bulk"), 2) == 1
        for copy in copies:
            copy.wait()
        head, tail = head_ref[...], tail_ref[...]
        low_ref[...] = jnp.where(is_odd, head, tail)
        high_ref[...] = jnp.where(is_odd, tail, head)

    return pl.pallas_call(
        kernel,
        out_shape=(jax.ShapeDtypeStruct(shape, F32), jax.ShapeDtypeStruct(shape, F32)),
        in_specs=[pl.BlockSpec(memory_space=pltpu.HBM)],
        out_specs=tuple(vmem_specs(2)),
        scratch_shapes=[VMEM(shape, F32), VMEM(shape, F32), pltpu.SemaphoreType.DMA((2, fields))],
        compiler_params=pltpu.CompilerParams(vmem_limit_bytes=4 << 20),
        cost_estimate=pl.CostEstimate(flops=10_000_000_000, bytes_accessed=20_000_000, transcendentals=0),
        name="edge_rows",
    )(in_hbm(psi))


def forward_local(source, psi, lateral, second, first, ratio, inv, total):
    planes, width = source.shape[0], source.shape[2]

    def kernel(source_ref, psi_ref, lateral_ref, second_ref, first_ref, ratio_ref, inv_ref, total_ref,
               scaled_ref, map_ref):
        is_odd = lax.rem(lax.axis_index("bulk"), 2) == 1

        def body(i, state):
            below, above = lateral_ref[i, 0], lateral_ref[i, 1]
            right = []
            for c in range(5):
                one = first_ref[pl.ds(c * planes + i, 1), :]
                two = second_ref[pl.ds(c * planes + i, 1), :]
                here = psi_ref[i, c]
                down = jnp.concatenate([jnp.where(is_odd, one, two), here[:width - 1]], axis=0)
                up = jnp.concatenate([here[1:], jnp.where(is_odd, two, one)], axis=0)
                right.append(source_ref[i, c] - below * down - above * up)
            out = []
            for h, rows in enumerate(halves(width)):
                r = [v[8 * h:8 * h + 8] for v in right]
                d = block(inv_ref, i, rows)
                e = block(ratio_ref, i, rows)
                g = [dot5(d[c], r) for c in range(5)]
                out.append((g, [g[c] - dot5(e[c], state[h]) for c in range(5)]))
            for h, rows in enumerate(halves(width)):
                for c in range(5):
                    scaled_ref[i, c, rows, :] = out[h][0][c]
            return [f for _, f in out]

        zero = [[jnp.zeros((8, LANES), F32)] * 5 for _ in halves(width)]
        state = lax.fori_loop(0, planes, body, zero, unroll=2)
        keep_map(map_ref, total_ref, state, width)

    return pl.pallas_call(
        kernel,
        out_shape=(VMEM(source.shape, F32), jax.ShapeDtypeStruct((6,) + source.shape[1:], F32)),
        in_specs=vmem_specs(8),
        out_specs=tuple(vmem_specs(2)),
        compiler_params=pltpu.CompilerParams(vmem_limit_bytes=4 << 20),
        name="forward_local",
    )(*[in_vmem(v) for v in (source, psi, lateral, second, first, ratio, inv, total)])


def matrices(coupled, inv, backward, name):
    planes, width = coupled.shape[0], coupled.shape[3]

    def kernel(coupled_ref, inv_ref, ratio_ref, total_ref):
        set_identity(total_ref, planes)

        def body(t, carry):
            at = planes - 1 - t if backward else t
            for rows in halves(width):
                ratio = ratio_of(coupled_ref, inv_ref, at, rows)
                keep_matrices(ratio, next_total(ratio, total_ref, rows), ratio_ref, total_ref, at, rows)
            return carry

        lax.fori_loop(0, planes, body, 0, unroll=2)

    return pl.pallas_call(
        kernel,
        out_shape=(VMEM(coupled.shape, F32), jax.ShapeDtypeStruct(coupled.shape[1:], F32)),
        in_specs=vmem_specs(2),
        out_specs=tuple(vmem_specs(2)),
        compiler_params=pltpu.CompilerParams(vmem_limit_bytes=4 << 20),
        cost_estimate=pl.CostEstimate(flops=5_000_000_000, bytes_accessed=20_000_000, transcendentals=0),
        name=name,
    )(in_vmem(coupled), in_vmem(inv))


def forward_then_back(scaled, arriving, ratio, back_ratio, back_total):
    planes, width = scaled.shape[0], scaled.shape[2]

    def kernel(scaled_ref, near_ref, reach_ref, other_ref, ratio_ref, back_ref, total_ref,
               field_ref, map_ref):
        def ahead(i, state):
            out = []
            for h, rows in enumerate(halves(width)):
                e = block(ratio_ref, i, rows)
                out.append([scaled_ref[i, c, rows, :] - dot5(e[c], state[h]) for c in range(5)])
            for h, rows in enumerate(halves(width)):
                for c in range(5):
                    field_ref[i, c, rows, :] = out[h][c]
            return out

        start = last_join(near_ref, reach_ref, other_ref, False, width)
        lax.fori_loop(0, planes, ahead, start, unroll=4)

        def back(t, state):
            i = planes - 1 - t
            out = []
            for h, rows in enumerate(halves(width)):
                e = block(back_ref, i, rows)
                out.append([field_ref[i, c, rows, :] - dot5(e[c], state[h]) for c in range(5)])
            return out

        zero = [[jnp.zeros((8, LANES), F32)] * 5 for _ in halves(width)]
        state = lax.fori_loop(0, planes, back, zero, unroll=4)
        keep_map(map_ref, total_ref, state, width)

    return pl.pallas_call(
        kernel,
        out_shape=(VMEM(scaled.shape, F32), jax.ShapeDtypeStruct((6,) + scaled.shape[1:], F32)),
        in_specs=vmem_specs(7),
        out_specs=tuple(vmem_specs(2)),
        compiler_params=pltpu.CompilerParams(vmem_limit_bytes=4 << 20),
        name="forward_then_back",
    )(*[in_vmem(v) for v in (scaled, *arriving, ratio, back_ratio, back_total)])


def face_slots(owner, node, owners):
    face_rows = owner.shape[0]
    cap = 2 * face_rows * LANES // owners
    bucket_rows = 2 * face_rows

    def kernel(owner_ref, node_ref, slot_ref, nodes_ref):
        sub = lax.broadcasted_iota(jnp.int32, (LANES, LANES), 0)
        lane = lax.broadcasted_iota(jnp.int32, (LANES, LANES), 1)
        strict = (sub < lane).astype(F32).astype(BF16)
        ones = jnp.ones((LANES, LANES), BF16)
        fs = lax.broadcasted_iota(jnp.int32, (face_rows, face_rows), 0)
        fl = lax.broadcasted_iota(jnp.int32, (face_rows, face_rows), 1)
        lower = (fl < fs).astype(F32).astype(BF16)
        own = owner_ref[...]
        masks = [(own == o).astype(F32) for o in range(owners)]
        stacked = jnp.concatenate(masks, axis=0).astype(BF16)
        before = jnp.dot(stacked, strict, preferred_element_type=F32)
        totals = jnp.dot(stacked, ones, preferred_element_type=F32).astype(BF16)
        rank = jnp.zeros((face_rows, LANES), F32)
        for o in range(owners):
            here = slice(o * face_rows, (o + 1) * face_rows)
            offset = jnp.dot(lower, totals[here], preferred_element_type=F32)
            rank = rank + masks[o] * (before[here] + offset + float(o * cap))
        slot = rank.astype(jnp.int32)
        slot_ref[...] = slot
        nodes = node_ref[...]
        high = (nodes // LANES).astype(F32)
        low = (nodes % LANES).astype(F32)
        parts = place_in_slots(slot, [high, low], bucket_rows)
        nodes_ref[...] = float(LANES) * parts[0] + parts[1]

    return pl.pallas_call(
        kernel,
        out_shape=(VMEM((face_rows, LANES), jnp.int32), VMEM((bucket_rows, LANES), F32)),
        in_specs=vmem_specs(2),
        out_specs=tuple(vmem_specs(2)),
        compiler_params=pltpu.CompilerParams(vmem_limit_bytes=4 << 20),
        cost_estimate=pl.CostEstimate(flops=4_000_000, bytes_accessed=10_000_000, transcendentals=0),
        name="face_slots",
    )(in_vmem(owner), in_vmem(node))


def spread(row, rows):
    tile = jnp.broadcast_to(row, (16, LANES)).astype(BF16)
    return jnp.concatenate([tile] * (rows // 16), axis=0)


def split(value):
    high = value.astype(BF16)
    return high, (value - high.astype(F32)).astype(BF16)


def place_in_slots(slot, parts, bucket_rows):
    face_rows = slot.shape[0]
    high = (slot // LANES).astype(F32)
    low = (slot % LANES).astype(F32)
    parts = [p.astype(F32) for p in parts]
    high_iota = lax.broadcasted_iota(jnp.int32, (bucket_rows, LANES), 0).astype(F32).astype(BF16)
    low_iota = lax.broadcasted_iota(jnp.int32, (LANES, LANES), 0).astype(F32).astype(BF16)
    ones, none = jnp.ones((LANES, LANES), BF16), jnp.zeros((LANES, LANES), BF16)
    zero = jnp.zeros((bucket_rows, LANES), BF16)
    lefts, rights = [], []
    for f in range(face_rows):
        row = slice(f, f + 1)
        hot = high_iota == spread(high[row], bucket_rows)
        lefts.append(jnp.concatenate(
            [jnp.where(hot, spread(p[row], bucket_rows), zero) for p in parts], axis=0))
        rights.append(jnp.where(low_iota == spread(low[row], LANES), ones, none))
    out = lax.dot_general(jnp.concatenate(lefts, axis=1), jnp.concatenate(rights, axis=1),
                          (((1,), (1,)), ((), ())), preferred_element_type=F32)
    return [out[k * bucket_rows:(k + 1) * bucket_rows] for k in range(len(parts))]


def backward_and_faces(field, arriving, back_ratio, count, cell, weight, slot, nodes, devices, owners):
    planes, width = field.shape[0], field.shape[2]
    face_rows = cell.shape[0]
    bucket_rows = nodes.shape[0]
    rows_each = bucket_rows // owners
    half = rows_each // 2
    group = 2
    piece = 4
    batch = 8

    def kernel(count_ref, field_ref, near_ref, reach_ref, other_ref, back_ref, cell_ref, weight_ref,
               slot_ref, nodes_ref, adjoint_hbm, send_ref, adjoint_ref, parts_ref, value_ref, sems):
        def write(k):
            return pltpu.make_async_copy(adjoint_ref.at[pl.ds(k * batch, batch)],
                                         adjoint_hbm.at[pl.ds(k * batch, batch)], sems.at[k])

        def back(t, state):
            i = planes - 1 - t
            out = []
            for h, rows in enumerate(halves(width)):
                e = block(back_ref, i, rows)
                out.append([field_ref[i, c, rows, :] - dot5(e[c], state[h]) for c in range(5)])
            for h, rows in enumerate(halves(width)):
                for c in range(5):
                    adjoint_ref[i, c, rows, :] = out[h][c]
            for c in range(5):
                high, low = split(jnp.concatenate([o[c] for o in out], axis=0))
                at = pl.ds(pl.multiple_of((i * 5 + c) * width, width), width)
                parts_ref[at, :LANES] = high
                parts_ref[at, LANES:] = low
            return out

        state = last_join(near_ref, reach_ref, other_ref, True, width)
        for k in reversed(range(planes // batch)):
            first = planes - (k + 1) * batch
            state = lax.fori_loop(first, first + batch, back, state, unroll=4)
            write(k).start()

        lane_iota = lax.broadcasted_iota(jnp.int32, (LANES, LANES), 0).astype(F32).astype(BF16)
        sub8 = lax.broadcasted_iota(jnp.int32, (8, LANES), 0)

        def gather(g, carry):
            cells = [cell_ref[pl.ds(g * group + u, 1), :] for u in range(group)]
            hots, offs = [], []
            for at in cells:
                lanes = spread((at % LANES).astype(F32), LANES)
                hots.append(jnp.where(lane_iota == lanes, jnp.ones((LANES, LANES), BF16),
                                      jnp.zeros((LANES, LANES), BF16)))
                offs.append(jnp.broadcast_to(at // LANES, (8, LANES)) - sub8)
            hot = jnp.concatenate(hots, axis=1)
            hot = jnp.concatenate([hot, hot], axis=0)
            found = [[jnp.zeros((8, LANES), F32)] * 5 for _ in range(group)]
            for p in range(0, planes, piece):
                got = jnp.dot(parts_ref[p * 5 * width:(p + piece) * 5 * width, :], hot,
                              preferred_element_type=F32)
                for i in range(piece):
                    for h in range(width // 8):
                        for u in range(group):
                            mask = offs[u] == (p + i) * width + 8 * h
                            for c in range(5):
                                row = (i * 5 + c) * width + 8 * h
                                found[u][c] = jnp.where(mask, got[row:row + 8, u * LANES:(u + 1) * LANES],
                                                        found[u][c])
            weights = weight_ref[:, pl.ds(pl.multiple_of(g * (group * LANES), group * LANES), group * LANES)]
            for u in range(group):
                w = [jnp.broadcast_to(weights[c:c + 1, u * LANES:(u + 1) * LANES], (8, LANES)) for c in range(5)]
                value_ref[pl.ds(g * group + u, 1), :] = jnp.sum(dot5(w, found[u]), axis=0, keepdims=True)
            return carry

        lax.fori_loop(0, face_rows // group, gather, 0, unroll=4)
        live = lax.broadcasted_iota(jnp.int32, (face_rows, LANES), 0) * LANES + lax.broadcasted_iota(
            jnp.int32, (face_rows, LANES), 1) < count_ref[0]
        high, low = split(jnp.where(live, value_ref[...], 0.0))
        placed = place_in_slots(slot_ref[...], [high, low], bucket_rows)
        values = placed[0] + placed[1]
        for o in range(owners):
            for core in range(2):
                start = o * rows_each + core * half
                here = slice(start, start + half)
                both = jnp.concatenate([values[here], nodes_ref[here, :]], axis=0)
                for d in range(core * owners + o, devices, 2 * owners):
                    send_ref[d] = both
        for k in range(planes // batch):
            write(k).wait()

    return pl.pallas_call(
        kernel,
        out_shape=(
            jax.ShapeDtypeStruct(field.shape, F32),
            jax.ShapeDtypeStruct((devices, 2 * half, LANES), F32),
        ),
        in_specs=[pl.BlockSpec(memory_space=pltpu.SMEM)] + vmem_specs(9),
        out_specs=(pl.BlockSpec(memory_space=pltpu.HBM), pl.BlockSpec(memory_space=VMEM)),
        scratch_shapes=[
            VMEM(field.shape, F32),
            VMEM((planes * 5 * width, 2 * LANES), BF16),
            VMEM((face_rows, LANES), F32),
            pltpu.SemaphoreType.DMA((planes // batch,)),
        ],
        compiler_params=pltpu.CompilerParams(vmem_limit_bytes=12 << 20),
        name="backward_and_faces",
    )(count, in_vmem(field), *[in_vmem(v) for v in arriving], in_vmem(back_ratio), in_vmem(cell),
      in_vmem(weight), in_vmem(slot), in_vmem(nodes))


def node_sums(got):
    devices, rows2, _ = got.shape
    rows_each = rows2 // 2
    side = NODES_DEV // LANES
    batch = min(devices, 128 // rows_each)

    def kernel(got_ref, out_ref):
        iota = lax.broadcasted_iota(jnp.int32, (LANES, LANES), 0).astype(F32).astype(BF16)
        side_iota = lax.broadcasted_iota(jnp.int32, (side, LANES), 0).astype(F32).astype(BF16)
        ones, zero = jnp.ones((LANES, LANES), BF16), jnp.zeros((LANES, LANES), BF16)
        side_zero = jnp.zeros((side, LANES), BF16)

        def body(t, total):
            lefts, rights = [], []
            for u in range(batch):
                d = t * batch + u
                for r in range(rows_each):
                    value = got_ref[d, r:r + 1, :]
                    node = got_ref[d, rows_each + r:rows_each + r + 1, :].astype(jnp.int32)
                    high = value.astype(BF16).astype(F32)
                    hot = side_iota == spread((node // LANES).astype(F32), side)
                    lefts.append(jnp.concatenate([
                        jnp.where(hot, spread(high, side), side_zero),
                        jnp.where(hot, spread(value - high, side), side_zero)], axis=0))
                    rights.append(jnp.where(iota == spread((node % LANES).astype(F32), LANES), ones, zero))
            return total + lax.dot_general(
                jnp.concatenate(lefts, axis=1), jnp.concatenate(rights, axis=1),
                (((1,), (1,)), ((), ())), preferred_element_type=F32)

        total = jnp.zeros((2 * side, LANES), F32)
        if batch == devices:
            total = body(0, total)
        else:
            total = lax.fori_loop(0, devices // batch, body, total)
        out_ref[...] = total[:side] + total[side:]

    return pl.pallas_call(
        kernel,
        out_shape=jax.ShapeDtypeStruct((side, LANES), F32),
        in_specs=vmem_specs(1),
        out_specs=pl.BlockSpec(memory_space=VMEM),
        compiler_params=pltpu.CompilerParams(vmem_limit_bytes=24 << 20),
        name="node_sums",
    )(in_vmem(got))


def comes_after(stage, backward):
    bit = lax.rem(lax.div(lax.axis_index("sweep"), 1 << stage), 2)
    return bit == (0 if backward else 1)


def matvec(matrix, vector):
    return [dot5(row, vector) for row in matrix]


def matmat(matrix, other):
    return [[dot5(row, [other[e][x] for e in range(5)]) for x in range(5)] for row in matrix]


def load_matrix(ref, rows):
    return [[ref[c, d, rows, :] for d in range(5)] for c in range(5)]


def load_vector(ref, rows):
    return [ref[c, rows, :] for c in range(5)]


def pick(flag, one, two):
    if isinstance(one, list):
        return [pick(flag, a, b) for a, b in zip(one, two)]
    return jnp.where(flag, one, two)


def last_join(near_ref, reach_ref, other_ref, backward, width):
    after = comes_after(lax.axis_size("sweep").bit_length() - 2, backward)
    start = []
    for rows in halves(width):
        near = load_vector(near_ref, rows)
        gain = matvec(load_matrix(reach_ref, rows), load_vector(other_ref, rows))
        start.append([n + jnp.where(after, g, 0.0) for n, g in zip(near, gain)])
    return start


def join(stage, backward, near, reach, own, other, whole):
    first = near is None
    _, _, width, _ = own.shape
    vector = own.shape[1:]
    outs = [vector, (5,) + vector, own.shape if whole else vector]
    operands = [own, other] + ([] if first else [near, reach])

    def kernel(*refs):
        ins, out = refs[:len(operands)], refs[len(operands):]
        after = comes_after(stage, backward)
        for rows in halves(width):
            mine, theirs = load_vector(ins[0].at[5], rows), load_vector(ins[1].at[5], rows)
            my_total, their_total = load_matrix(ins[0], rows), load_matrix(ins[1], rows)
            if first:
                entering = theirs
                through = their_total
                before = [jnp.zeros((8, LANES), F32)] * 5
                unit = [[jnp.full((8, LANES), 1.0 if c == d else 0.0, F32) for d in range(5)] for c in range(5)]
            else:
                before, unit = load_vector(ins[2], rows), load_matrix(ins[3], rows)
                entering = [a + b for a, b in zip(before, matvec(unit, theirs))]
                through = matmat(unit, their_total)
            entering, through = pick(after, entering, before), pick(after, through, unit)
            downstream = pick(after, my_total, their_total)
            sent = matvec(downstream, pick(after, theirs, mine))
            sent = [a + b for a, b in zip(pick(after, mine, theirs), sent)]
            sent_ref = out[2].at[5] if whole else out[2]
            for c in range(5):
                out[0][c, rows, :] = entering[c]
                sent_ref[c, rows, :] = sent[c]
                for d in range(5):
                    out[1][c, d, rows, :] = through[c][d]
            if whole:
                product = matmat(downstream, pick(after, their_total, my_total))
                for c in range(5):
                    for d in range(5):
                        out[2][c, d, rows, :] = product[c][d]

    return pl.pallas_call(
        kernel,
        out_shape=tuple(jax.ShapeDtypeStruct(shape, F32) for shape in outs),
        in_specs=vmem_specs(len(operands)),
        out_specs=tuple(vmem_specs(3)),
        compiler_params=pltpu.CompilerParams(vmem_limit_bytes=4 << 20),
        name="join",
    )(*[in_vmem(v) for v in operands])


def relay(own, backward):
    size = lax.axis_size("sweep")
    stages = size.bit_length() - 1
    near = reach = None
    for stage in range(stages):
        pairs = [(i, i ^ (1 << stage)) for i in range(size)]
        other = lax.ppermute(own, "sweep", pairs)
        if stage == stages - 1:
            return (near, reach, other), own
        near, reach, own = join(stage, backward, near, reach, own, other, stage + 2 < stages)


def per_device(source, psi_old, lateral, lower_jac, upper_jac, diag_inv, face_weight, face_cell,
               face_owner, face_node, face_count):
    bulk = lax.axis_size("bulk")
    devices = bulk * lax.axis_size("sweep")
    low_pairs = [(i, i ^ 1) for i in range(bulk) if i ^ 1 < bulk]
    high_pairs = [(i, j) for i in range(bulk) for j in [i + 1 if i % 2 else i - 1] if 0 <= j < bulk]
    low_edge, high_edge = edge_rows(psi_old)
    low_edge, high_edge, lower_jac = lax.optimization_barrier((low_edge, high_edge, lower_jac))
    second = lax.ppermute(high_edge, "bulk", high_pairs)
    first = lax.ppermute(low_edge, "bulk", low_pairs)

    ratio, total = matrices(lower_jac, diag_inv, False, "forward_matrices")
    scaled, own = forward_local(source, psi_old, lateral, second, first, ratio, diag_inv, total)
    arriving, joined = relay(own, False)
    upper_jac, joined = lax.optimization_barrier((upper_jac, joined))
    back_ratio, back_total = matrices(upper_jac, diag_inv, True, "backward_matrices")
    field, own = forward_then_back(scaled, arriving, ratio, back_ratio, back_total)
    arriving, _ = relay(own, True)

    slots = face_cell.shape[0]
    rows = (slots // LANES, LANES)
    slot, nodes = face_slots(face_owner.reshape(rows), face_node.reshape(rows), bulk)
    adjoint, send = backward_and_faces(field, arriving, back_ratio, face_count, face_cell.reshape(rows),
                                       face_weight, slot, nodes, devices, bulk)
    got = lax.all_to_all(send, ("sweep", "bulk"), 0, 0, tiled=True)
    mine = node_sums(got)
    pairs = [(i, i ^ 1) for i in range(lax.axis_size("sweep"))]
    return adjoint, (mine + lax.ppermute(mine, "sweep", pairs)).reshape(NODES_DEV)


def solution(mesh):
    placed = (
        P("sweep", None, "bulk", None),
        P("sweep", None, "bulk", None),
        P("sweep", None, "bulk", None),
        P("sweep", None, None, "bulk", None),
        P("sweep", None, None, "bulk", None),
        P("sweep", None, None, "bulk", None),
        P(None, ("sweep", "bulk")),
        P(("sweep", "bulk")),
        P(("sweep", "bulk"), None),
        P(("sweep", "bulk")),
        P(("sweep", "bulk")),
    )
    return jax.shard_map(
        per_device,
        mesh=mesh,
        in_specs=placed,
        out_specs=(P("sweep", None, "bulk", None), P("bulk")),
        check_vma=False,
    )
```

```python
import jax
import jax.numpy as jnp
from jax import lax
from jax.experimental import pallas as pl
from jax.experimental.pallas import tpu as pltpu
from jax.sharding import PartitionSpec as P

NODES_DEV = 16384
LANES = 128
F32 = jnp.float32
BF16 = jnp.bfloat16
VMEM = pltpu.VMEM


def dot5(a, b):
    p = [x * y for x, y in zip(a, b)]
    return ((p[0] + p[1]) + (p[2] + p[3])) + p[4]


def block(ref, at, rows):
    return [[ref[at, c, d, rows, :] for d in range(5)] for c in range(5)]


def halves(width):
    return [pl.ds(8 * h, 8) for h in range(width // 8)]


def in_vmem(value):
    return pltpu.with_memory_space_constraint(value, VMEM)


def in_hbm(value):
    return pltpu.with_memory_space_constraint(value, pltpu.HBM)


def vmem_specs(n):
    return [pl.BlockSpec(memory_space=VMEM)] * n


def ratio_of(coupled, inv, at, rows):
    j = block(coupled, at, rows)
    d = block(inv, at, rows)
    return [[dot5(d[c], [j[e][x] for e in range(5)]) for x in range(5)] for c in range(5)]


def next_total(ratio, total_ref, rows):
    old = [[total_ref[e, x, rows, :] for x in range(5)] for e in range(5)]
    return [[dot5(ratio[c], [old[e][x] for e in range(5)]) for x in range(5)] for c in range(5)]


def keep_matrices(ratio, total, ratio_ref, total_ref, at, rows):
    for c in range(5):
        for x in range(5):
            ratio_ref[at, c, x, rows, :] = ratio[c][x]
            total_ref[c, x, rows, :] = total[c][x]


def keep_map(map_ref, total_ref, leaving, width):
    map_ref[:5] = total_ref[...]
    for h, rows in enumerate(halves(width)):
        for c in range(5):
            map_ref[5, c, rows, :] = leaving[h][c]


def set_identity(total_ref, planes):
    sign = 1.0 if planes % 2 == 0 else -1.0
    for c in range(5):
        for d in range(5):
            total_ref[c, d] = jnp.full(total_ref.shape[2:], sign if c == d else 0.0, F32)


def edge_rows(psi):
    planes, fields, width, _ = psi.shape
    shape = (fields * planes, LANES)

    def kernel(psi_hbm, low_ref, high_ref, head_ref, tail_ref, sems):
        copies = []
        for c in range(fields):
            rows = pl.ds(c * planes, planes)
            copies.append(pltpu.make_async_copy(psi_hbm.at[:, c, 0, :], head_ref.at[rows], sems.at[0, c]))
            copies.append(pltpu.make_async_copy(psi_hbm.at[:, c, width - 1, :], tail_ref.at[rows], sems.at[1, c]))
        for copy in copies:
            copy.start()
        is_odd = lax.rem(lax.axis_index("bulk"), 2) == 1
        for copy in copies:
            copy.wait()
        head, tail = head_ref[...], tail_ref[...]
        low_ref[...] = jnp.where(is_odd, head, tail)
        high_ref[...] = jnp.where(is_odd, tail, head)

    return pl.pallas_call(
        kernel,
        out_shape=(jax.ShapeDtypeStruct(shape, F32), jax.ShapeDtypeStruct(shape, F32)),
        in_specs=[pl.BlockSpec(memory_space=pltpu.HBM)],
        out_specs=tuple(vmem_specs(2)),
        scratch_shapes=[VMEM(shape, F32), VMEM(shape, F32), pltpu.SemaphoreType.DMA((2, fields))],
        compiler_params=pltpu.CompilerParams(vmem_limit_bytes=4 << 20),
        cost_estimate=pl.CostEstimate(flops=10_000_000_000, bytes_accessed=20_000_000, transcendentals=0),
        name="edge_rows",
    )(in_hbm(psi))


def inner_right_side(source, psi, lateral):
    planes, width = source.shape[0], source.shape[2]

    def kernel(source_ref, psi_ref, lateral_ref, right_ref, edge_ref):
        row = lax.broadcasted_iota(jnp.int32, (width, LANES), 0)
        none = jnp.zeros((1, LANES), F32)

        def body(i, carry):
            below, above = lateral_ref[i, 0], lateral_ref[i, 1]
            edge_ref[i, 0] = jnp.where(row == 0, below, 0.0)[:8]
            edge_ref[i, 1] = jnp.where(row == width - 1, above, 0.0)[width - 8:]
            right = []
            for c in range(5):
                here = psi_ref[i, c]
                down = jnp.concatenate([none, here[:width - 1]], axis=0)
                up = jnp.concatenate([here[1:], none], axis=0)
                right.append(source_ref[i, c] - below * down - above * up)
            for c in range(5):
                right_ref[i, c] = right[c]
            return carry

        lax.fori_loop(0, planes, body, 0, unroll=2)

    return pl.pallas_call(
        kernel,
        out_shape=(VMEM(source.shape, F32), VMEM((planes, 2, 8, LANES), F32)),
        in_specs=vmem_specs(3),
        out_specs=tuple(vmem_specs(2)),
        compiler_params=pltpu.CompilerParams(vmem_limit_bytes=4 << 20),
        name="inner_right_side",
    )(*[in_vmem(v) for v in (source, psi, lateral)])


def forward_local(right, edge, second, first, ratio, inv, total):
    planes, width = right.shape[0], right.shape[2]
    parts = halves(width)

    def kernel(right_ref, edge_ref, second_ref, first_ref, ratio_ref, inv_ref, total_ref,
               scaled_ref, map_ref, low_ref, high_ref):
        is_odd = lax.rem(lax.axis_index("bulk"), 2) == 1
        one, two = first_ref[...], second_ref[...]
        low_ref[...] = jnp.where(is_odd, one, two)
        high_ref[...] = jnp.where(is_odd, two, one)

        def body(i, state):
            out = []
            for h, rows in enumerate(parts):
                r = [right_ref[i, c, rows, :] for c in range(5)]
                for last, halo_ref in ((0, low_ref), (len(parts) - 1, high_ref)):
                    if h == last:
                        k = 0 if halo_ref is low_ref else 1
                        r = [r[c] - edge_ref[i, k] * halo_ref[pl.ds(c * planes + i, 1), :] for c in range(5)]
                d = block(inv_ref, i, rows)
                e = block(ratio_ref, i, rows)
                g = [dot5(d[c], r) for c in range(5)]
                out.append((g, [g[c] - dot5(e[c], state[h]) for c in range(5)]))
            for h, rows in enumerate(parts):
                for c in range(5):
                    scaled_ref[i, c, rows, :] = out[h][0][c]
            return [f for _, f in out]

        zero = [[jnp.zeros((8, LANES), F32)] * 5 for _ in parts]
        state = lax.fori_loop(0, planes, body, zero, unroll=2)
        keep_map(map_ref, total_ref, state, width)

    return pl.pallas_call(
        kernel,
        out_shape=(VMEM(right.shape, F32), jax.ShapeDtypeStruct((6,) + right.shape[1:], F32)),
        in_specs=vmem_specs(7),
        out_specs=tuple(vmem_specs(2)),
        scratch_shapes=[VMEM(first.shape, F32), VMEM(first.shape, F32)],
        compiler_params=pltpu.CompilerParams(vmem_limit_bytes=4 << 20),
        name="forward_local",
    )(*[in_vmem(v) for v in (right, edge, second, first, ratio, inv, total)])


def matrices(coupled, inv, backward, name):
    planes, width = coupled.shape[0], coupled.shape[3]

    def kernel(coupled_ref, inv_ref, ratio_ref, total_ref):
        set_identity(total_ref, planes)

        def body(t, carry):
            at = planes - 1 - t if backward else t
            for rows in halves(width):
                ratio = ratio_of(coupled_ref, inv_ref, at, rows)
                keep_matrices(ratio, next_total(ratio, total_ref, rows), ratio_ref, total_ref, at, rows)
            return carry

        lax.fori_loop(0, planes, body, 0, unroll=2)

    return pl.pallas_call(
        kernel,
        out_shape=(VMEM(coupled.shape, F32), jax.ShapeDtypeStruct(coupled.shape[1:], F32)),
        in_specs=vmem_specs(2),
        out_specs=tuple(vmem_specs(2)),
        compiler_params=pltpu.CompilerParams(vmem_limit_bytes=4 << 20),
        cost_estimate=pl.CostEstimate(flops=5_000_000_000, bytes_accessed=20_000_000, transcendentals=0),
        name=name,
    )(in_vmem(coupled), in_vmem(inv))


def forward_then_back(scaled, arriving, ratio, back_ratio, back_total):
    planes, width = scaled.shape[0], scaled.shape[2]

    def kernel(scaled_ref, near_ref, reach_ref, other_ref, ratio_ref, back_ref, total_ref,
               field_ref, map_ref):
        def ahead(i, state):
            out = []
            for h, rows in enumerate(halves(width)):
                e = block(ratio_ref, i, rows)
                out.append([scaled_ref[i, c, rows, :] - dot5(e[c], state[h]) for c in range(5)])
            for h, rows in enumerate(halves(width)):
                for c in range(5):
                    field_ref[i, c, rows, :] = out[h][c]
            return out

        start = last_join(near_ref, reach_ref, other_ref, False, width)
        lax.fori_loop(0, planes, ahead, start, unroll=4)

        def back(t, state):
            i = planes - 1 - t
            out = []
            for h, rows in enumerate(halves(width)):
                e = block(back_ref, i, rows)
                out.append([field_ref[i, c, rows, :] - dot5(e[c], state[h]) for c in range(5)])
            return out

        zero = [[jnp.zeros((8, LANES), F32)] * 5 for _ in halves(width)]
        state = lax.fori_loop(0, planes, back, zero, unroll=4)
        keep_map(map_ref, total_ref, state, width)

    return pl.pallas_call(
        kernel,
        out_shape=(VMEM(scaled.shape, F32), jax.ShapeDtypeStruct((6,) + scaled.shape[1:], F32)),
        in_specs=vmem_specs(7),
        out_specs=tuple(vmem_specs(2)),
        compiler_params=pltpu.CompilerParams(vmem_limit_bytes=4 << 20),
        name="forward_then_back",
    )(*[in_vmem(v) for v in (scaled, *arriving, ratio, back_ratio, back_total)])


def face_slots(owner, node, owners):
    face_rows = owner.shape[0]
    cap = 2 * face_rows * LANES // owners
    bucket_rows = 2 * face_rows

    def kernel(owner_ref, node_ref, slot_ref, nodes_ref):
        sub = lax.broadcasted_iota(jnp.int32, (LANES, LANES), 0)
        lane = lax.broadcasted_iota(jnp.int32, (LANES, LANES), 1)
        strict = (sub < lane).astype(F32).astype(BF16)
        ones = jnp.ones((LANES, LANES), BF16)
        fs = lax.broadcasted_iota(jnp.int32, (face_rows, face_rows), 0)
        fl = lax.broadcasted_iota(jnp.int32, (face_rows, face_rows), 1)
        lower = (fl < fs).astype(F32).astype(BF16)
        own = owner_ref[...]
        masks = [(own == o).astype(F32) for o in range(owners)]
        stacked = jnp.concatenate(masks, axis=0).astype(BF16)
        before = jnp.dot(stacked, strict, preferred_element_type=F32)
        totals = jnp.dot(stacked, ones, preferred_element_type=F32).astype(BF16)
        rank = jnp.zeros((face_rows, LANES), F32)
        for o in range(owners):
            here = slice(o * face_rows, (o + 1) * face_rows)
            offset = jnp.dot(lower, totals[here], preferred_element_type=F32)
            rank = rank + masks[o] * (before[here] + offset + float(o * cap))
        slot = rank.astype(jnp.int32)
        slot_ref[...] = slot
        nodes = node_ref[...]
        high = (nodes // LANES).astype(F32)
        low = (nodes % LANES).astype(F32)
        parts = place_in_slots(slot, [high, low], bucket_rows)
        nodes_ref[...] = float(LANES) * parts[0] + parts[1]

    return pl.pallas_call(
        kernel,
        out_shape=(VMEM((face_rows, LANES), jnp.int32), VMEM((bucket_rows, LANES), F32)),
        in_specs=vmem_specs(2),
        out_specs=tuple(vmem_specs(2)),
        compiler_params=pltpu.CompilerParams(vmem_limit_bytes=4 << 20),
        cost_estimate=pl.CostEstimate(flops=4_000_000, bytes_accessed=10_000_000, transcendentals=0),
        name="face_slots",
    )(in_vmem(owner), in_vmem(node))


def spread(row, rows):
    tile = jnp.broadcast_to(row, (16, LANES)).astype(BF16)
    return jnp.concatenate([tile] * (rows // 16), axis=0)


def split(value):
    high = value.astype(BF16)
    return high, (value - high.astype(F32)).astype(BF16)


def place_in_slots(slot, parts, bucket_rows):
    face_rows = slot.shape[0]
    high = (slot // LANES).astype(F32)
    low = (slot % LANES).astype(F32)
    parts = [p.astype(F32) for p in parts]
    high_iota = lax.broadcasted_iota(jnp.int32, (bucket_rows, LANES), 0).astype(F32).astype(BF16)
    low_iota = lax.broadcasted_iota(jnp.int32, (LANES, LANES), 0).astype(F32).astype(BF16)
    ones, none = jnp.ones((LANES, LANES), BF16), jnp.zeros((LANES, LANES), BF16)
    zero = jnp.zeros((bucket_rows, LANES), BF16)
    lefts, rights = [], []
    for f in range(face_rows):
        row = slice(f, f + 1)
        hot = high_iota == spread(high[row], bucket_rows)
        lefts.append(jnp.concatenate(
            [jnp.where(hot, spread(p[row], bucket_rows), zero) for p in parts], axis=0))
        rights.append(jnp.where(low_iota == spread(low[row], LANES), ones, none))
    out = lax.dot_general(jnp.concatenate(lefts, axis=1), jnp.concatenate(rights, axis=1),
                          (((1,), (1,)), ((), ())), preferred_element_type=F32)
    return [out[k * bucket_rows:(k + 1) * bucket_rows] for k in range(len(parts))]


def backward_and_faces(field, arriving, back_ratio, count, cell, weight, slot, nodes, devices, owners):
    planes, width = field.shape[0], field.shape[2]
    face_rows = cell.shape[0]
    bucket_rows = nodes.shape[0]
    rows_each = bucket_rows // owners
    half = rows_each // 2
    group = 2
    piece = 4
    batch = 8

    def kernel(count_ref, field_ref, near_ref, reach_ref, other_ref, back_ref, cell_ref, weight_ref,
               slot_ref, nodes_ref, adjoint_hbm, send_ref, adjoint_ref, parts_ref, value_ref, sems):
        def write(k):
            return pltpu.make_async_copy(adjoint_ref.at[pl.ds(k * batch, batch)],
                                         adjoint_hbm.at[pl.ds(k * batch, batch)], sems.at[k])

        def back(t, state):
            i = planes - 1 - t
            out = []
            for h, rows in enumerate(halves(width)):
                e = block(back_ref, i, rows)
                out.append([field_ref[i, c, rows, :] - dot5(e[c], state[h]) for c in range(5)])
            for h, rows in enumerate(halves(width)):
                for c in range(5):
                    adjoint_ref[i, c, rows, :] = out[h][c]
            for c in range(5):
                high, low = split(jnp.concatenate([o[c] for o in out], axis=0))
                at = pl.ds(pl.multiple_of((i * 5 + c) * width, width), width)
                parts_ref[at, :LANES] = high
                parts_ref[at, LANES:] = low
            return out

        state = last_join(near_ref, reach_ref, other_ref, True, width)
        for k in reversed(range(planes // batch)):
            first = planes - (k + 1) * batch
            state = lax.fori_loop(first, first + batch, back, state, unroll=4)
            write(k).start()

        lane_iota = lax.broadcasted_iota(jnp.int32, (LANES, LANES), 0).astype(F32).astype(BF16)
        sub8 = lax.broadcasted_iota(jnp.int32, (8, LANES), 0)

        def gather(g, carry):
            cells = [cell_ref[pl.ds(g * group + u, 1), :] for u in range(group)]
            hots, offs = [], []
            for at in cells:
                lanes = spread((at % LANES).astype(F32), LANES)
                hots.append(jnp.where(lane_iota == lanes, jnp.ones((LANES, LANES), BF16),
                                      jnp.zeros((LANES, LANES), BF16)))
                offs.append(jnp.broadcast_to(at // LANES, (8, LANES)) - sub8)
            hot = jnp.concatenate(hots, axis=1)
            hot = jnp.concatenate([hot, hot], axis=0)
            found = [[jnp.zeros((8, LANES), F32)] * 5 for _ in range(group)]
            for p in range(0, planes, piece):
                got = jnp.dot(parts_ref[p * 5 * width:(p + piece) * 5 * width, :], hot,
                              preferred_element_type=F32)
                for i in range(piece):
                    for h in range(width // 8):
                        for u in range(group):
                            mask = offs[u] == (p + i) * width + 8 * h
                            for c in range(5):
                                row = (i * 5 + c) * width + 8 * h
                                found[u][c] = jnp.where(mask, got[row:row + 8, u * LANES:(u + 1) * LANES],
                                                        found[u][c])
            weights = weight_ref[:, pl.ds(pl.multiple_of(g * (group * LANES), group * LANES), group * LANES)]
            for u in range(group):
                w = [jnp.broadcast_to(weights[c:c + 1, u * LANES:(u + 1) * LANES], (8, LANES)) for c in range(5)]
                value_ref[pl.ds(g * group + u, 1), :] = jnp.sum(dot5(w, found[u]), axis=0, keepdims=True)
            return carry

        lax.fori_loop(0, face_rows // group, gather, 0, unroll=4)
        live = lax.broadcasted_iota(jnp.int32, (face_rows, LANES), 0) * LANES + lax.broadcasted_iota(
            jnp.int32, (face_rows, LANES), 1) < count_ref[0]
        high, low = split(jnp.where(live, value_ref[...], 0.0))
        placed = place_in_slots(slot_ref[...], [high, low], bucket_rows)
        values = placed[0] + placed[1]
        for o in range(owners):
            for core in range(2):
                start = o * rows_each + core * half
                here = slice(start, start + half)
                both = jnp.concatenate([values[here], nodes_ref[here, :]], axis=0)
                for d in range(core * owners + o, devices, 2 * owners):
                    send_ref[d] = both
        for k in range(planes // batch):
            write(k).wait()

    return pl.pallas_call(
        kernel,
        out_shape=(
            jax.ShapeDtypeStruct(field.shape, F32),
            jax.ShapeDtypeStruct((devices, 2 * half, LANES), F32),
        ),
        in_specs=[pl.BlockSpec(memory_space=pltpu.SMEM)] + vmem_specs(9),
        out_specs=(pl.BlockSpec(memory_space=pltpu.HBM), pl.BlockSpec(memory_space=VMEM)),
        scratch_shapes=[
            VMEM(field.shape, F32),
            VMEM((planes * 5 * width, 2 * LANES), BF16),
            VMEM((face_rows, LANES), F32),
            pltpu.SemaphoreType.DMA((planes // batch,)),
        ],
        compiler_params=pltpu.CompilerParams(vmem_limit_bytes=12 << 20),
        name="backward_and_faces",
    )(count, in_vmem(field), *[in_vmem(v) for v in arriving], in_vmem(back_ratio), in_vmem(cell),
      in_vmem(weight), in_vmem(slot), in_vmem(nodes))


def node_sums(got):
    devices, rows2, _ = got.shape
    rows_each = rows2 // 2
    side = NODES_DEV // LANES
    batch = min(devices, 128 // rows_each)

    def kernel(got_ref, out_ref):
        iota = lax.broadcasted_iota(jnp.int32, (LANES, LANES), 0).astype(F32).astype(BF16)
        side_iota = lax.broadcasted_iota(jnp.int32, (side, LANES), 0).astype(F32).astype(BF16)
        ones, zero = jnp.ones((LANES, LANES), BF16), jnp.zeros((LANES, LANES), BF16)
        side_zero = jnp.zeros((side, LANES), BF16)

        def body(t, total):
            lefts, rights = [], []
            for u in range(batch):
                d = t * batch + u
                for r in range(rows_each):
                    value = got_ref[d, r:r + 1, :]
                    node = got_ref[d, rows_each + r:rows_each + r + 1, :].astype(jnp.int32)
                    high = value.astype(BF16).astype(F32)
                    hot = side_iota == spread((node // LANES).astype(F32), side)
                    lefts.append(jnp.concatenate([
                        jnp.where(hot, spread(high, side), side_zero),
                        jnp.where(hot, spread(value - high, side), side_zero)], axis=0))
                    rights.append(jnp.where(iota == spread((node % LANES).astype(F32), LANES), ones, zero))
            return total + lax.dot_general(
                jnp.concatenate(lefts, axis=1), jnp.concatenate(rights, axis=1),
                (((1,), (1,)), ((), ())), preferred_element_type=F32)

        total = jnp.zeros((2 * side, LANES), F32)
        if batch == devices:
            total = body(0, total)
        else:
            total = lax.fori_loop(0, devices // batch, body, total)
        out_ref[...] = total[:side] + total[side:]

    return pl.pallas_call(
        kernel,
        out_shape=jax.ShapeDtypeStruct((side, LANES), F32),
        in_specs=vmem_specs(1),
        out_specs=pl.BlockSpec(memory_space=VMEM),
        compiler_params=pltpu.CompilerParams(vmem_limit_bytes=24 << 20),
        name="node_sums",
    )(in_vmem(got))


def comes_after(stage, backward):
    bit = lax.rem(lax.div(lax.axis_index("sweep"), 1 << stage), 2)
    return bit == (0 if backward else 1)


def matvec(matrix, vector):
    return [dot5(row, vector) for row in matrix]


def matmat(matrix, other):
    return [[dot5(row, [other[e][x] for e in range(5)]) for x in range(5)] for row in matrix]


def load_matrix(ref, rows):
    return [[ref[c, d, rows, :] for d in range(5)] for c in range(5)]


def load_vector(ref, rows):
    return [ref[c, rows, :] for c in range(5)]


def pick(flag, one, two):
    if isinstance(one, list):
        return [pick(flag, a, b) for a, b in zip(one, two)]
    return jnp.where(flag, one, two)


def last_join(near_ref, reach_ref, other_ref, backward, width):
    after = comes_after(lax.axis_size("sweep").bit_length() - 2, backward)
    start = []
    for rows in halves(width):
        near = load_vector(near_ref, rows)
        gain = matvec(load_matrix(reach_ref, rows), load_vector(other_ref, rows))
        start.append([n + jnp.where(after, g, 0.0) for n, g in zip(near, gain)])
    return start


def join(stage, backward, near, reach, own, other, whole):
    first = near is None
    _, _, width, _ = own.shape
    vector = own.shape[1:]
    outs = [vector, (5,) + vector, own.shape if whole else vector]
    operands = [own, other] + ([] if first else [near, reach])

    def kernel(*refs):
        ins, out = refs[:len(operands)], refs[len(operands):]
        after = comes_after(stage, backward)
        for rows in halves(width):
            mine, theirs = load_vector(ins[0].at[5], rows), load_vector(ins[1].at[5], rows)
            my_total, their_total = load_matrix(ins[0], rows), load_matrix(ins[1], rows)
            if first:
                entering = theirs
                through = their_total
                before = [jnp.zeros((8, LANES), F32)] * 5
                unit = [[jnp.full((8, LANES), 1.0 if c == d else 0.0, F32) for d in range(5)] for c in range(5)]
            else:
                before, unit = load_vector(ins[2], rows), load_matrix(ins[3], rows)
                entering = [a + b for a, b in zip(before, matvec(unit, theirs))]
                through = matmat(unit, their_total)
            entering, through = pick(after, entering, before), pick(after, through, unit)
            downstream = pick(after, my_total, their_total)
            sent = matvec(downstream, pick(after, theirs, mine))
            sent = [a + b for a, b in zip(pick(after, mine, theirs), sent)]
            sent_ref = out[2].at[5] if whole else out[2]
            for c in range(5):
                out[0][c, rows, :] = entering[c]
                sent_ref[c, rows, :] = sent[c]
                for d in range(5):
                    out[1][c, d, rows, :] = through[c][d]
            if whole:
                product = matmat(downstream, pick(after, their_total, my_total))
                for c in range(5):
                    for d in range(5):
                        out[2][c, d, rows, :] = product[c][d]

    return pl.pallas_call(
        kernel,
        out_shape=tuple(jax.ShapeDtypeStruct(shape, F32) for shape in outs),
        in_specs=vmem_specs(len(operands)),
        out_specs=tuple(vmem_specs(3)),
        compiler_params=pltpu.CompilerParams(vmem_limit_bytes=4 << 20),
        name="join",
    )(*[in_vmem(v) for v in operands])


def relay(own, backward):
    size = lax.axis_size("sweep")
    stages = size.bit_length() - 1
    near = reach = None
    for stage in range(stages):
        pairs = [(i, i ^ (1 << stage)) for i in range(size)]
        other = lax.ppermute(own, "sweep", pairs)
        if stage == stages - 1:
            return (near, reach, other), own
        near, reach, own = join(stage, backward, near, reach, own, other, stage + 2 < stages)


def per_device(source, psi_old, lateral, lower_jac, upper_jac, diag_inv, face_weight, face_cell,
               face_owner, face_node, face_count):
    bulk = lax.axis_size("bulk")
    devices = bulk * lax.axis_size("sweep")
    low_pairs = [(i, i ^ 1) for i in range(bulk) if i ^ 1 < bulk]
    high_pairs = [(i, j) for i in range(bulk) for j in [i + 1 if i % 2 else i - 1] if 0 <= j < bulk]
    low_edge, high_edge = edge_rows(psi_old)
    low_edge, high_edge, lower_jac = lax.optimization_barrier((low_edge, high_edge, lower_jac))
    second = lax.ppermute(high_edge, "bulk", high_pairs)
    first = lax.ppermute(low_edge, "bulk", low_pairs)

    ratio, total = matrices(lower_jac, diag_inv, False, "forward_matrices")
    right, edge = inner_right_side(source, psi_old, lateral)
    right, edge, ratio = lax.optimization_barrier((right, edge, ratio))
    scaled, own = forward_local(right, edge, second, first, ratio, diag_inv, total)
    arriving, joined = relay(own, False)
    upper_jac, joined = lax.optimization_barrier((upper_jac, joined))
    back_ratio, back_total = matrices(upper_jac, diag_inv, True, "backward_matrices")
    field, own = forward_then_back(scaled, arriving, ratio, back_ratio, back_total)
    arriving, _ = relay(own, True)

    slots = face_cell.shape[0]
    rows = (slots // LANES, LANES)
    slot, nodes = face_slots(face_owner.reshape(rows), face_node.reshape(rows), bulk)
    adjoint, send = backward_and_faces(field, arriving, back_ratio, face_count, face_cell.reshape(rows),
                                       face_weight, slot, nodes, devices, bulk)
    got = lax.all_to_all(send, ("sweep", "bulk"), 0, 0, tiled=True)
    mine = node_sums(got)
    pairs = [(i, i ^ 1) for i in range(lax.axis_size("sweep"))]
    return adjoint, (mine + lax.ppermute(mine, "sweep", pairs)).reshape(NODES_DEV)


def solution(mesh):
    placed = (
        P("sweep", None, "bulk", None),
        P("sweep", None, "bulk", None),
        P("sweep", None, "bulk", None),
        P("sweep", None, None, "bulk", None),
        P("sweep", None, None, "bulk", None),
        P("sweep", None, None, "bulk", None),
        P(None, ("sweep", "bulk")),
        P(("sweep", "bulk")),
        P(("sweep", "bulk"), None),
        P(("sweep", "bulk")),
        P(("sweep", "bulk")),
    )
    return jax.shard_map(
        per_device,
        mesh=mesh,
        in_specs=placed,
        out_specs=(P("sweep", None, "bulk", None), P("bulk")),
        check_vma=False,
    )
```

```python
import jax
import jax.numpy as jnp
from jax import lax
from jax.experimental import pallas as pl
from jax.experimental.pallas import tpu as pltpu
from jax.sharding import PartitionSpec as P

NODES_DEV = 16384
LANES = 128
F32 = jnp.float32
BF16 = jnp.bfloat16
VMEM = pltpu.VMEM


def dot5(a, b):
    p = [x * y for x, y in zip(a, b)]
    return ((p[0] + p[1]) + (p[2] + p[3])) + p[4]


def block(ref, at, rows):
    return [[ref[at, c, d, rows, :] for d in range(5)] for c in range(5)]


def halves(width):
    return [pl.ds(8 * h, 8) for h in range(width // 8)]


def in_vmem(value):
    return pltpu.with_memory_space_constraint(value, VMEM)


def in_hbm(value):
    return pltpu.with_memory_space_constraint(value, pltpu.HBM)


def vmem_specs(n):
    return [pl.BlockSpec(memory_space=VMEM)] * n


def ratio_of(coupled, inv, at, rows):
    j = block(coupled, at, rows)
    d = block(inv, at, rows)
    return [[dot5(d[c], [j[e][x] for e in range(5)]) for x in range(5)] for c in range(5)]


def next_total(ratio, total_ref, rows):
    old = [[total_ref[e, x, rows, :] for x in range(5)] for e in range(5)]
    return [[dot5(ratio[c], [old[e][x] for e in range(5)]) for x in range(5)] for c in range(5)]


def keep_matrices(ratio, total, ratio_ref, total_ref, at, rows):
    for c in range(5):
        for x in range(5):
            ratio_ref[at, c, x, rows, :] = ratio[c][x]
            total_ref[c, x, rows, :] = total[c][x]


def keep_map(map_ref, total_ref, leaving, width):
    map_ref[:5] = total_ref[...]
    for h, rows in enumerate(halves(width)):
        for c in range(5):
            map_ref[5, c, rows, :] = leaving[h][c]


def set_identity(total_ref, planes):
    sign = 1.0 if planes % 2 == 0 else -1.0
    for c in range(5):
        for d in range(5):
            total_ref[c, d] = jnp.full(total_ref.shape[2:], sign if c == d else 0.0, F32)


def edge_rows(psi):
    planes, fields, width, _ = psi.shape
    shape = (fields * planes, LANES)

    def kernel(psi_hbm, low_ref, high_ref, head_ref, tail_ref, sems):
        copies = []
        for c in range(fields):
            rows = pl.ds(c * planes, planes)
            copies.append(pltpu.make_async_copy(psi_hbm.at[:, c, 0, :], head_ref.at[rows], sems.at[0, c]))
            copies.append(pltpu.make_async_copy(psi_hbm.at[:, c, width - 1, :], tail_ref.at[rows], sems.at[1, c]))
        for copy in copies:
            copy.start()
        is_odd = lax.rem(lax.axis_index("bulk"), 2) == 1
        for copy in copies:
            copy.wait()
        head, tail = head_ref[...], tail_ref[...]
        low_ref[...] = jnp.where(is_odd, head, tail)
        high_ref[...] = jnp.where(is_odd, tail, head)

    return pl.pallas_call(
        kernel,
        out_shape=(jax.ShapeDtypeStruct(shape, F32), jax.ShapeDtypeStruct(shape, F32)),
        in_specs=[pl.BlockSpec(memory_space=pltpu.HBM)],
        out_specs=tuple(vmem_specs(2)),
        scratch_shapes=[VMEM(shape, F32), VMEM(shape, F32), pltpu.SemaphoreType.DMA((2, fields))],
        compiler_params=pltpu.CompilerParams(vmem_limit_bytes=4 << 20),
        cost_estimate=pl.CostEstimate(flops=10_000_000_000, bytes_accessed=20_000_000, transcendentals=0),
        name="edge_rows",
    )(in_hbm(psi))


def forward_local(source, psi, lateral, second, first, ratio, inv, total):
    planes, width = source.shape[0], source.shape[2]

    def kernel(source_ref, psi_ref, lateral_ref, second_ref, first_ref, ratio_ref, inv_ref, total_ref,
               scaled_ref, map_ref):
        is_odd = lax.rem(lax.axis_index("bulk"), 2) == 1

        def body(i, state):
            below, above = lateral_ref[i, 0], lateral_ref[i, 1]
            right = []
            for c in range(5):
                one = first_ref[pl.ds(c * planes + i, 1), :]
                two = second_ref[pl.ds(c * planes + i, 1), :]
                here = psi_ref[i, c]
                down = jnp.concatenate([jnp.where(is_odd, one, two), here[:width - 1]], axis=0)
                up = jnp.concatenate([here[1:], jnp.where(is_odd, two, one)], axis=0)
                right.append(source_ref[i, c] - below * down - above * up)
            out = []
            for h, rows in enumerate(halves(width)):
                r = [v[8 * h:8 * h + 8] for v in right]
                d = block(inv_ref, i, rows)
                e = block(ratio_ref, i, rows)
                g = [dot5(d[c], r) for c in range(5)]
                out.append((g, [g[c] - dot5(e[c], state[h]) for c in range(5)]))
            for h, rows in enumerate(halves(width)):
                for c in range(5):
                    scaled_ref[i, c, rows, :] = out[h][0][c]
            return [f for _, f in out]

        zero = [[jnp.zeros((8, LANES), F32)] * 5 for _ in halves(width)]
        state = lax.fori_loop(0, planes, body, zero, unroll=4)
        keep_map(map_ref, total_ref, state, width)

    return pl.pallas_call(
        kernel,
        out_shape=(VMEM(source.shape, F32), jax.ShapeDtypeStruct((6,) + source.shape[1:], F32)),
        in_specs=vmem_specs(8),
        out_specs=tuple(vmem_specs(2)),
        compiler_params=pltpu.CompilerParams(vmem_limit_bytes=4 << 20),
        name="forward_local",
    )(*[in_vmem(v) for v in (source, psi, lateral, second, first, ratio, inv, total)])


def matrices(coupled, inv, backward, name):
    planes, width = coupled.shape[0], coupled.shape[3]

    def kernel(coupled_ref, inv_ref, ratio_ref, total_ref):
        set_identity(total_ref, planes)

        def body(t, carry):
            at = planes - 1 - t if backward else t
            for rows in halves(width):
                ratio = ratio_of(coupled_ref, inv_ref, at, rows)
                keep_matrices(ratio, next_total(ratio, total_ref, rows), ratio_ref, total_ref, at, rows)
            return carry

        lax.fori_loop(0, planes, body, 0, unroll=4)

    return pl.pallas_call(
        kernel,
        out_shape=(VMEM(coupled.shape, F32), jax.ShapeDtypeStruct(coupled.shape[1:], F32)),
        in_specs=vmem_specs(2),
        out_specs=tuple(vmem_specs(2)),
        compiler_params=pltpu.CompilerParams(vmem_limit_bytes=4 << 20),
        cost_estimate=pl.CostEstimate(flops=5_000_000_000, bytes_accessed=20_000_000, transcendentals=0),
        name=name,
    )(in_vmem(coupled), in_vmem(inv))


def forward_then_back(scaled, arriving, ratio, back_ratio, back_total):
    planes, width = scaled.shape[0], scaled.shape[2]

    def kernel(scaled_ref, near_ref, reach_ref, other_ref, ratio_ref, back_ref, total_ref,
               field_ref, map_ref):
        def ahead(i, state):
            out = []
            for h, rows in enumerate(halves(width)):
                e = block(ratio_ref, i, rows)
                out.append([scaled_ref[i, c, rows, :] - dot5(e[c], state[h]) for c in range(5)])
            for h, rows in enumerate(halves(width)):
                for c in range(5):
                    field_ref[i, c, rows, :] = out[h][c]
            return out

        start = last_join(near_ref, reach_ref, other_ref, False, width)
        lax.fori_loop(0, planes, ahead, start, unroll=4)

        def back(t, state):
            i = planes - 1 - t
            out = []
            for h, rows in enumerate(halves(width)):
                e = block(back_ref, i, rows)
                out.append([field_ref[i, c, rows, :] - dot5(e[c], state[h]) for c in range(5)])
            return out

        zero = [[jnp.zeros((8, LANES), F32)] * 5 for _ in halves(width)]
        state = lax.fori_loop(0, planes, back, zero, unroll=4)
        keep_map(map_ref, total_ref, state, width)

    return pl.pallas_call(
        kernel,
        out_shape=(VMEM(scaled.shape, F32), jax.ShapeDtypeStruct((6,) + scaled.shape[1:], F32)),
        in_specs=vmem_specs(7),
        out_specs=tuple(vmem_specs(2)),
        compiler_params=pltpu.CompilerParams(vmem_limit_bytes=4 << 20),
        name="forward_then_back",
    )(*[in_vmem(v) for v in (scaled, *arriving, ratio, back_ratio, back_total)])


def face_slots(owner, node, owners):
    face_rows = owner.shape[0]
    cap = 2 * face_rows * LANES // owners
    bucket_rows = 2 * face_rows

    def kernel(owner_ref, node_ref, slot_ref, nodes_ref):
        sub = lax.broadcasted_iota(jnp.int32, (LANES, LANES), 0)
        lane = lax.broadcasted_iota(jnp.int32, (LANES, LANES), 1)
        strict = (sub < lane).astype(F32).astype(BF16)
        ones = jnp.ones((LANES, LANES), BF16)
        fs = lax.broadcasted_iota(jnp.int32, (face_rows, face_rows), 0)
        fl = lax.broadcasted_iota(jnp.int32, (face_rows, face_rows), 1)
        lower = (fl < fs).astype(F32).astype(BF16)
        own = owner_ref[...]
        masks = [(own == o).astype(F32) for o in range(owners)]
        stacked = jnp.concatenate(masks, axis=0).astype(BF16)
        before = jnp.dot(stacked, strict, preferred_element_type=F32)
        totals = jnp.dot(stacked, ones, preferred_element_type=F32).astype(BF16)
        rank = jnp.zeros((face_rows, LANES), F32)
        for o in range(owners):
            here = slice(o * face_rows, (o + 1) * face_rows)
            offset = jnp.dot(lower, totals[here], preferred_element_type=F32)
            rank = rank + masks[o] * (before[here] + offset + float(o * cap))
        slot = rank.astype(jnp.int32)
        slot_ref[...] = slot
        nodes = node_ref[...]
        high = (nodes // LANES).astype(F32)
        low = (nodes % LANES).astype(F32)
        parts = place_in_slots(slot, [high, low], bucket_rows)
        nodes_ref[...] = float(LANES) * parts[0] + parts[1]

    return pl.pallas_call(
        kernel,
        out_shape=(VMEM((face_rows, LANES), jnp.int32), VMEM((bucket_rows, LANES), F32)),
        in_specs=vmem_specs(2),
        out_specs=tuple(vmem_specs(2)),
        compiler_params=pltpu.CompilerParams(vmem_limit_bytes=4 << 20),
        cost_estimate=pl.CostEstimate(flops=4_000_000, bytes_accessed=10_000_000, transcendentals=0),
        name="face_slots",
    )(in_vmem(owner), in_vmem(node))


def spread(row, rows):
    tile = jnp.broadcast_to(row, (16, LANES)).astype(BF16)
    return jnp.concatenate([tile] * (rows // 16), axis=0)


def split(value):
    high = value.astype(BF16)
    return high, (value - high.astype(F32)).astype(BF16)


def place_in_slots(slot, parts, bucket_rows):
    face_rows = slot.shape[0]
    high = (slot // LANES).astype(F32)
    low = (slot % LANES).astype(F32)
    parts = [p.astype(F32) for p in parts]
    high_iota = lax.broadcasted_iota(jnp.int32, (bucket_rows, LANES), 0).astype(F32).astype(BF16)
    low_iota = lax.broadcasted_iota(jnp.int32, (LANES, LANES), 0).astype(F32).astype(BF16)
    ones, none = jnp.ones((LANES, LANES), BF16), jnp.zeros((LANES, LANES), BF16)
    zero = jnp.zeros((bucket_rows, LANES), BF16)
    lefts, rights = [], []
    for f in range(face_rows):
        row = slice(f, f + 1)
        hot = high_iota == spread(high[row], bucket_rows)
        lefts.append(jnp.concatenate(
            [jnp.where(hot, spread(p[row], bucket_rows), zero) for p in parts], axis=0))
        rights.append(jnp.where(low_iota == spread(low[row], LANES), ones, none))
    out = lax.dot_general(jnp.concatenate(lefts, axis=1), jnp.concatenate(rights, axis=1),
                          (((1,), (1,)), ((), ())), preferred_element_type=F32)
    return [out[k * bucket_rows:(k + 1) * bucket_rows] for k in range(len(parts))]


def backward_and_faces(field, arriving, back_ratio, count, cell, weight, slot, nodes, devices, owners):
    planes, width = field.shape[0], field.shape[2]
    face_rows = cell.shape[0]
    bucket_rows = nodes.shape[0]
    rows_each = bucket_rows // owners
    half = rows_each // 2
    group = 2
    piece = 4
    batch = 8

    def kernel(count_ref, field_ref, near_ref, reach_ref, other_ref, back_ref, cell_ref, weight_ref,
               slot_ref, nodes_ref, adjoint_hbm, send_ref, adjoint_ref, parts_ref, value_ref, sems):
        def write(k):
            return pltpu.make_async_copy(adjoint_ref.at[pl.ds(k * batch, batch)],
                                         adjoint_hbm.at[pl.ds(k * batch, batch)], sems.at[k])

        def back(t, state):
            i = planes - 1 - t
            out = []
            for h, rows in enumerate(halves(width)):
                e = block(back_ref, i, rows)
                out.append([field_ref[i, c, rows, :] - dot5(e[c], state[h]) for c in range(5)])
            for h, rows in enumerate(halves(width)):
                for c in range(5):
                    adjoint_ref[i, c, rows, :] = out[h][c]
            for c in range(5):
                high, low = split(jnp.concatenate([o[c] for o in out], axis=0))
                at = pl.ds(pl.multiple_of((i * 5 + c) * width, width), width)
                parts_ref[at, :LANES] = high
                parts_ref[at, LANES:] = low
            return out

        state = last_join(near_ref, reach_ref, other_ref, True, width)
        for k in reversed(range(planes // batch)):
            first = planes - (k + 1) * batch
            state = lax.fori_loop(first, first + batch, back, state, unroll=4)
            write(k).start()

        lane_iota = lax.broadcasted_iota(jnp.int32, (LANES, LANES), 0).astype(F32).astype(BF16)
        sub8 = lax.broadcasted_iota(jnp.int32, (8, LANES), 0)

        def gather(g, carry):
            cells = [cell_ref[pl.ds(g * group + u, 1), :] for u in range(group)]
            hots, offs = [], []
            for at in cells:
                lanes = spread((at % LANES).astype(F32), LANES)
                hots.append(jnp.where(lane_iota == lanes, jnp.ones((LANES, LANES), BF16),
                                      jnp.zeros((LANES, LANES), BF16)))
                offs.append(jnp.broadcast_to(at // LANES, (8, LANES)) - sub8)
            hot = jnp.concatenate(hots, axis=1)
            hot = jnp.concatenate([hot, hot], axis=0)
            found = [[jnp.zeros((8, LANES), F32)] * 5 for _ in range(group)]
            for p in range(0, planes, piece):
                got = jnp.dot(parts_ref[p * 5 * width:(p + piece) * 5 * width, :], hot,
                              preferred_element_type=F32)
                for i in range(piece):
                    for h in range(width // 8):
                        for u in range(group):
                            mask = offs[u] == (p + i) * width + 8 * h
                            for c in range(5):
                                row = (i * 5 + c) * width + 8 * h
                                found[u][c] = jnp.where(mask, got[row:row + 8, u * LANES:(u + 1) * LANES],
                                                        found[u][c])
            weights = weight_ref[:, pl.ds(pl.multiple_of(g * (group * LANES), group * LANES), group * LANES)]
            for u in range(group):
                w = [jnp.broadcast_to(weights[c:c + 1, u * LANES:(u + 1) * LANES], (8, LANES)) for c in range(5)]
                value_ref[pl.ds(g * group + u, 1), :] = jnp.sum(dot5(w, found[u]), axis=0, keepdims=True)
            return carry

        lax.fori_loop(0, face_rows // group, gather, 0, unroll=4)
        live = lax.broadcasted_iota(jnp.int32, (face_rows, LANES), 0) * LANES + lax.broadcasted_iota(
            jnp.int32, (face_rows, LANES), 1) < count_ref[0]
        high, low = split(jnp.where(live, value_ref[...], 0.0))
        placed = place_in_slots(slot_ref[...], [high, low], bucket_rows)
        values = placed[0] + placed[1]
        for o in range(owners):
            for core in range(2):
                start = o * rows_each + core * half
                here = slice(start, start + half)
                both = jnp.concatenate([values[here], nodes_ref[here, :]], axis=0)
                for d in range(core * owners + o, devices, 2 * owners):
                    send_ref[d] = both
        for k in range(planes // batch):
            write(k).wait()

    return pl.pallas_call(
        kernel,
        out_shape=(
            jax.ShapeDtypeStruct(field.shape, F32),
            jax.ShapeDtypeStruct((devices, 2 * half, LANES), F32),
        ),
        in_specs=[pl.BlockSpec(memory_space=pltpu.SMEM)] + vmem_specs(9),
        out_specs=(pl.BlockSpec(memory_space=pltpu.HBM), pl.BlockSpec(memory_space=VMEM)),
        scratch_shapes=[
            VMEM(field.shape, F32),
            VMEM((planes * 5 * width, 2 * LANES), BF16),
            VMEM((face_rows, LANES), F32),
            pltpu.SemaphoreType.DMA((planes // batch,)),
        ],
        compiler_params=pltpu.CompilerParams(vmem_limit_bytes=12 << 20),
        name="backward_and_faces",
    )(count, in_vmem(field), *[in_vmem(v) for v in arriving], in_vmem(back_ratio), in_vmem(cell),
      in_vmem(weight), in_vmem(slot), in_vmem(nodes))


def node_sums(got):
    devices, rows2, _ = got.shape
    rows_each = rows2 // 2
    side = NODES_DEV // LANES
    batch = min(devices, 128 // rows_each)

    def kernel(got_ref, out_ref):
        iota = lax.broadcasted_iota(jnp.int32, (LANES, LANES), 0).astype(F32).astype(BF16)
        side_iota = lax.broadcasted_iota(jnp.int32, (side, LANES), 0).astype(F32).astype(BF16)
        ones, zero = jnp.ones((LANES, LANES), BF16), jnp.zeros((LANES, LANES), BF16)
        side_zero = jnp.zeros((side, LANES), BF16)

        def body(t, total):
            lefts, rights = [], []
            for u in range(batch):
                d = t * batch + u
                for r in range(rows_each):
                    value = got_ref[d, r:r + 1, :]
                    node = got_ref[d, rows_each + r:rows_each + r + 1, :].astype(jnp.int32)
                    high = value.astype(BF16).astype(F32)
                    hot = side_iota == spread((node // LANES).astype(F32), side)
                    lefts.append(jnp.concatenate([
                        jnp.where(hot, spread(high, side), side_zero),
                        jnp.where(hot, spread(value - high, side), side_zero)], axis=0))
                    rights.append(jnp.where(iota == spread((node % LANES).astype(F32), LANES), ones, zero))
            return total + lax.dot_general(
                jnp.concatenate(lefts, axis=1), jnp.concatenate(rights, axis=1),
                (((1,), (1,)), ((), ())), preferred_element_type=F32)

        total = jnp.zeros((2 * side, LANES), F32)
        if batch == devices:
            total = body(0, total)
        else:
            total = lax.fori_loop(0, devices // batch, body, total)
        out_ref[...] = total[:side] + total[side:]

    return pl.pallas_call(
        kernel,
        out_shape=jax.ShapeDtypeStruct((side, LANES), F32),
        in_specs=vmem_specs(1),
        out_specs=pl.BlockSpec(memory_space=VMEM),
        compiler_params=pltpu.CompilerParams(vmem_limit_bytes=24 << 20),
        name="node_sums",
    )(in_vmem(got))


def comes_after(stage, backward):
    bit = lax.rem(lax.div(lax.axis_index("sweep"), 1 << stage), 2)
    return bit == (0 if backward else 1)


def matvec(matrix, vector):
    return [dot5(row, vector) for row in matrix]


def matmat(matrix, other):
    return [[dot5(row, [other[e][x] for e in range(5)]) for x in range(5)] for row in matrix]


def load_matrix(ref, rows):
    return [[ref[c, d, rows, :] for d in range(5)] for c in range(5)]


def load_vector(ref, rows):
    return [ref[c, rows, :] for c in range(5)]


def pick(flag, one, two):
    if isinstance(one, list):
        return [pick(flag, a, b) for a, b in zip(one, two)]
    return jnp.where(flag, one, two)


def last_join(near_ref, reach_ref, other_ref, backward, width):
    after = comes_after(lax.axis_size("sweep").bit_length() - 2, backward)
    start = []
    for rows in halves(width):
        near = load_vector(near_ref, rows)
        gain = matvec(load_matrix(reach_ref, rows), load_vector(other_ref, rows))
        start.append([n + jnp.where(after, g, 0.0) for n, g in zip(near, gain)])
    return start


def join(stage, backward, near, reach, own, other, whole):
    first = near is None
    _, _, width, _ = own.shape
    vector = own.shape[1:]
    outs = [vector, (5,) + vector, own.shape if whole else vector]
    operands = [own, other] + ([] if first else [near, reach])

    def kernel(*refs):
        ins, out = refs[:len(operands)], refs[len(operands):]
        after = comes_after(stage, backward)
        for rows in halves(width):
            mine, theirs = load_vector(ins[0].at[5], rows), load_vector(ins[1].at[5], rows)
            my_total, their_total = load_matrix(ins[0], rows), load_matrix(ins[1], rows)
            if first:
                entering = theirs
                through = their_total
                before = [jnp.zeros((8, LANES), F32)] * 5
                unit = [[jnp.full((8, LANES), 1.0 if c == d else 0.0, F32) for d in range(5)] for c in range(5)]
            else:
                before, unit = load_vector(ins[2], rows), load_matrix(ins[3], rows)
                entering = [a + b for a, b in zip(before, matvec(unit, theirs))]
                through = matmat(unit, their_total)
            entering, through = pick(after, entering, before), pick(after, through, unit)
            downstream = pick(after, my_total, their_total)
            sent = matvec(downstream, pick(after, theirs, mine))
            sent = [a + b for a, b in zip(pick(after, mine, theirs), sent)]
            sent_ref = out[2].at[5] if whole else out[2]
            for c in range(5):
                out[0][c, rows, :] = entering[c]
                sent_ref[c, rows, :] = sent[c]
                for d in range(5):
                    out[1][c, d, rows, :] = through[c][d]
            if whole:
                product = matmat(downstream, pick(after, their_total, my_total))
                for c in range(5):
                    for d in range(5):
                        out[2][c, d, rows, :] = product[c][d]

    return pl.pallas_call(
        kernel,
        out_shape=tuple(jax.ShapeDtypeStruct(shape, F32) for shape in outs),
        in_specs=vmem_specs(len(operands)),
        out_specs=tuple(vmem_specs(3)),
        compiler_params=pltpu.CompilerParams(vmem_limit_bytes=4 << 20),
        name="join",
    )(*[in_vmem(v) for v in operands])


def relay(own, backward):
    size = lax.axis_size("sweep")
    stages = size.bit_length() - 1
    near = reach = None
    for stage in range(stages):
        pairs = [(i, i ^ (1 << stage)) for i in range(size)]
        other = lax.ppermute(own, "sweep", pairs)
        if stage == stages - 1:
            return (near, reach, other), own
        near, reach, own = join(stage, backward, near, reach, own, other, stage + 2 < stages)


def per_device(source, psi_old, lateral, lower_jac, upper_jac, diag_inv, face_weight, face_cell,
               face_owner, face_node, face_count):
    bulk = lax.axis_size("bulk")
    devices = bulk * lax.axis_size("sweep")
    low_pairs = [(i, i ^ 1) for i in range(bulk) if i ^ 1 < bulk]
    high_pairs = [(i, j) for i in range(bulk) for j in [i + 1 if i % 2 else i - 1] if 0 <= j < bulk]
    low_edge, high_edge = edge_rows(psi_old)
    low_edge, high_edge, lower_jac = lax.optimization_barrier((low_edge, high_edge, lower_jac))
    second = lax.ppermute(high_edge, "bulk", high_pairs)
    first = lax.ppermute(low_edge, "bulk", low_pairs)

    ratio, total = matrices(lower_jac, diag_inv, False, "forward_matrices")
    scaled, own = forward_local(source, psi_old, lateral, second, first, ratio, diag_inv, total)
    arriving, joined = relay(own, False)
    upper_jac, joined = lax.optimization_barrier((upper_jac, joined))
    back_ratio, back_total = matrices(upper_jac, diag_inv, True, "backward_matrices")
    field, own = forward_then_back(scaled, arriving, ratio, back_ratio, back_total)
    arriving, _ = relay(own, True)

    slots = face_cell.shape[0]
    rows = (slots // LANES, LANES)
    slot, nodes = face_slots(face_owner.reshape(rows), face_node.reshape(rows), bulk)
    adjoint, send = backward_and_faces(field, arriving, back_ratio, face_count, face_cell.reshape(rows),
                                       face_weight, slot, nodes, devices, bulk)
    got = lax.all_to_all(send, ("sweep", "bulk"), 0, 0, tiled=True)
    mine = node_sums(got)
    pairs = [(i, i ^ 1) for i in range(lax.axis_size("sweep"))]
    return adjoint, (mine + lax.ppermute(mine, "sweep", pairs)).reshape(NODES_DEV)


def solution(mesh):
    placed = (
        P("sweep", None, "bulk", None),
        P("sweep", None, "bulk", None),
        P("sweep", None, "bulk", None),
        P("sweep", None, None, "bulk", None),
        P("sweep", None, None, "bulk", None),
        P("sweep", None, None, "bulk", None),
        P(None, ("sweep", "bulk")),
        P(("sweep", "bulk")),
        P(("sweep", "bulk"), None),
        P(("sweep", "bulk")),
        P(("sweep", "bulk")),
    )
    return jax.shard_map(
        per_device,
        mesh=mesh,
        in_specs=placed,
        out_specs=(P("sweep", None, "bulk", None), P("bulk")),
        check_vma=False,
    )
```
